32 devices in a mesh: doc: 4 (over y, core), seq: 8 (over z, x).
Axes of the slice: x: 2, y: 2, z: 4, core: 2. Of those that a mesh axis runs over, the one named last changes fastest.
Arguments:
- dec_in: bfloat16 [8, 1024, 1472], P('doc', 'seq'), may hold values from -6 to 6
- enc_in: bfloat16 [8, 4096, 1472], P('doc', 'seq'), may hold values from -6 to 6
- tgt_len: int32 [8], P('doc'), may hold values from 256 to 1024, as said below
- enc_len: int32 [8], P('doc'), may hold values from 200 to 4096, as said below
- self_qkv: bfloat16 [3, 1472, 384], P(None, 'seq', 'doc'), may hold values from -0.078125 to 0.078125
- self_out: bfloat16 [384, 1472], P('doc', 'seq'), may hold values from -1.75 to 1.75
- cross_q: bfloat16 [1472, 384], P('seq', 'doc'), may hold values from -0.078125 to 0.078125
- cross_kv: bfloat16 [2, 1472, 384], P(None, 'seq', 'doc'), may hold values from -0.078125 to 0.078125
- cross_out: bfloat16 [384, 1472], P('doc', 'seq'), may hold values from -1.75 to 1.75
- ff_in: bfloat16 [2, 1472, 3584], P(None, 'seq', 'doc'), may hold values from -0.15625 to 0.15625
- ff_out: bfloat16 [3584, 1472], P('doc', 'seq'), may hold values from -0.125 to 0.125
- gains: bfloat16 [3, 1472], P(None, 'seq'), may hold values from 0.099609375 to 1.8984375
- cotangent: bfloat16 [8, 1024, 1472], P('doc', 'seq'), may hold values from -6 to 6
Outputs:
- layer_out: float32 [8, 1024, 1472], P('doc', 'seq')
- dec_grad: float32 [8, 1024, 1472], P('doc', 'seq')
- enc_grad: float32 [8, 4096, 1472], P('doc', 'seq')
- grad_self_qkv: float32 [3, 1472, 384], P(None, 'seq', 'doc')
- grad_self_out: float32 [384, 1472], P('doc', 'seq')
- grad_cross_q: float32 [1472, 384], P('seq', 'doc')
- grad_cross_kv: float32 [2, 1472, 384], P(None, 'seq', 'doc')
- grad_cross_out: float32 [384, 1472], P('doc', 'seq')
- grad_ff_in: float32 [2, 1472, 3584], P(None, 'seq', 'doc')
- grad_ff_out: float32 [3584, 1472], P('doc', 'seq')
- grad_gains: float32 [3, 1472], P(None, 'seq')
The draws below stay inside these ranges and needn't reach their ends.
Inputs may be any that keep to these rules, and one draw needn't show every extreme that they name: `tgt_len`: one document of every draw has all 1024 positions in use. `enc_len`: one document of every draw has all 4096 slots live and another has 200.
All inputs are finite; a program needn't handle non-finite values.
Results may differ from the reference program's by a relative error of at most 0.034.
The reference program's roundings to bfloat16 on the way count: a program that leaves them out, or rounds other values in their place, can miss the bound.
Values may be sent and summed in bfloat16 or wider, within the bound.
No kernel may reach another device: no remote copies, remote signals or barrier semaphores. Data moves between devices by JAX's collectives and lax.ppermute only.
A program may use at most 384 MiB of HBM per device.

```python
import jax
import jax.numpy as jnp
from jax import lax

D = 1472
HEADS = 6
HEAD_DIM = 64
FF = 3584
ENC_LEN = 4096
ENC_MIN = 200
TGT_LEN = 1024
HQ = 384
DOCS = 8


def draw_tgt_len(key, part):
    own_key = jax.random.fold_in(key, 23)
    first_key, second_key = jax.random.split(own_key)
    counts = jax.random.randint(first_key, (DOCS,), TGT_LEN // 4, TGT_LEN + 1)
    shuffled = jax.random.permutation(second_key, DOCS)
    return counts.at[shuffled[0]].set(TGT_LEN).astype(jnp.int32)


def draw_enc_len(key, part):
    own_key = jax.random.fold_in(key, 11)
    first_key, second_key = jax.random.split(own_key)
    counts = jax.random.randint(first_key, (DOCS,), ENC_MIN, ENC_LEN + 1)
    shuffled = jax.random.permutation(second_key, DOCS)
    return counts.at[shuffled[0]].set(ENC_LEN).at[shuffled[1]].set(ENC_MIN).astype(jnp.int32)


def spiked(entries, key, source, target, parts, factor):
    def block_of(dim):
        return (jnp.arange(entries.shape[dim]) // (entries.shape[dim] // parts)).reshape((-1,) + (1,) * (entries.ndim - 1 - dim))

    one_side = jax.random.permutation(key, parts)[block_of(target)]
    far = (block_of(target) + parts // 2) % parts
    return jnp.where((block_of(source) == one_side) | (block_of(source) == far), factor * entries, entries)


def steps_of(stream_key, dims, pieces, low, top_value):
    def one(axis_at, parts):
        draws = jax.random.uniform(jax.random.fold_in(jax.random.fold_in(stream_key, 6), axis_at), (parts,), jnp.float32, low / len(pieces), top_value / len(pieces))
        return jnp.repeat(jnp.exp(draws), dims[axis_at] // parts).reshape((-1,) + (1,) * (len(dims) - axis_at - 1))

    gain = one(*pieces[0])
    for cut in pieces[1:]:
        gain = gain * one(*cut)
    return gain


def noise(key, dims, scale, limit, cuts=(), kind=jnp.bfloat16):
    values = scale * jax.random.normal(key, dims, jnp.float32)
    if cuts:
        values = values * steps_of(key, dims, cuts, -0.22, 0.18)
    return jnp.clip(values, -limit, limit).astype(kind)


def gaussian_with(key, dims, spread, most, cuts, heavy, kind=jnp.bfloat16):
    values = spread * jax.random.normal(key, dims, jnp.float32)
    if cuts:
        values = values * steps_of(key, dims, cuts, -0.22, 0.18)
    return jnp.clip(spiked(values, jax.random.fold_in(key, 3), *heavy), -most, most).astype(kind)


def setup_inputs(seed: int = 0) -> dict:
    keys = jax.random.split(jax.random.key(seed), 14)
    dec_in = noise(keys[0], (DOCS, TGT_LEN, D), 1.0, 6.0, ((0, 4), (1, 8)))
    enc_in = noise(keys[1], (DOCS, ENC_LEN, D), 1.0, 6.0, ((0, 4), (1, 8)))
    tgt_len = draw_tgt_len(jax.random.fold_in(keys[13], 71), 0)
    enc_len = draw_enc_len(jax.random.fold_in(keys[13], 71), 0)
    self_qkv = noise(keys[4], (3, D, HQ), (4 * D) ** -0.5, 0.078125, ((1, 8), (2, 4)))
    self_out = noise(keys[5], (HQ, D), (HQ // 32) ** -0.5, 1.75, ((0, 4), (1, 8)))
    cross_q = noise(keys[6], (D, HQ), (4 * D) ** -0.5, 0.078125, ((0, 8), (1, 4)))
    cross_kv = noise(keys[7], (2, D, HQ), (4 * D) ** -0.5, 0.078125, ((1, 8), (2, 4)))
    cross_out = noise(keys[8], (HQ, D), (HQ // 32) ** -0.5, 1.75, ((0, 4), (1, 8)))
    ff_in = noise(keys[9], (2, D, FF), D ** -0.5, 0.15625, ((1, 8), (2, 4)))
    ff_out = noise(keys[10], (FF, D), (FF // 2) ** -0.5, 0.125, ((0, 4), (1, 8)))
    gains = jnp.clip(1.0 + 0.18 * jax.random.normal(keys[11], (3, D), jnp.float32), 0.099609375, 1.8984375).astype(jnp.bfloat16)
    cotangent = gaussian_with(keys[12], (DOCS, TGT_LEN, D), 1.0, 6.0, ((0, 4), (1, 8)), (1, 2, 8, 2.0))
    return {"dec_in": dec_in, "enc_in": enc_in, "tgt_len": tgt_len, "enc_len": enc_len, "self_qkv": self_qkv, "self_out": self_out, "cross_q": cross_q, "cross_kv": cross_kv, "cross_out": cross_out, "ff_in": ff_in, "ff_out": ff_out, "gains": gains, "cotangent": cotangent}


@jax.custom_vjp
def low(v):
    return lax.optimization_barrier(v.astype(jnp.bfloat16)).astype(jnp.float32)

@jax.custom_vjp
def low_back(v):
    return v

def low_keep(v):
    return (low(v), None)

def low_pass(kept, grad):
    return (grad,)

def back_keep(v):
    return (v, None)

def back_low(kept, grad):
    return (low(grad),)
low.defvjp(low_keep, low_pass)
low_back.defvjp(back_keep, back_low)
EPSILON = 1e-06
NEGATIVE = -1e+30
HIGHEST = lax.Precision.HIGHEST

def rms_norm(values, gain_row):
    inverse = lax.rsqrt(lax.optimization_barrier(jnp.mean(values * values, axis=-1, keepdims=True)) + EPSILON)
    return values * inverse * gain_row

def matmul(left_op, right_op):
    return jnp.dot(left_op, right_op, precision=HIGHEST, preferred_element_type=jnp.float32)

def attend(queries, keys_in, values_in, allowed):
    count = queries.shape[0]
    heads_q = queries.reshape(count, HEADS, HEAD_DIM)
    heads_k = keys_in.reshape(keys_in.shape[0], HEADS, HEAD_DIM)
    heads_v = values_in.reshape(values_in.shape[0], HEADS, HEAD_DIM)
    scores = low_back(jnp.einsum('qhd,khd->qhk', heads_q, heads_k, precision=HIGHEST))
    scores = jnp.where(allowed[:, None, :], scores, NEGATIVE)
    peak_row = lax.optimization_barrier(jnp.max(scores, axis=-1, keepdims=True))
    raised = jnp.exp(scores - peak_row)
    totals = low_back(lax.optimization_barrier(jnp.sum(raised, axis=-1, keepdims=True)))
    numerator = low_back(jnp.einsum('qhk,khd->qhd', low(raised), heads_v, precision=HIGHEST))
    return low((numerator / totals).reshape(count, HEADS * HEAD_DIM))

def layer(stream, encoded, tgt_count, enc_count, weights):
    self_qkv, self_out, cross_q, cross_kv, cross_out, ff_in, ff_out, gains = weights
    normed = low(rms_norm(stream, gains[0]))
    queries = low_back(low(matmul(normed, self_qkv[0])))
    keys_in = low_back(low(matmul(normed, self_qkv[1])))
    values_in = low_back(low(matmul(normed, self_qkv[2])))
    positions = jnp.arange(TGT_LEN, dtype=jnp.int32)
    self_valid = (positions[None, :] <= positions[:, None]) & (positions[None, :] < tgt_count)
    attended = attend(queries, keys_in, values_in, self_valid)
    stream = stream + low_back(matmul(attended, self_out))
    normed = low(rms_norm(stream, gains[1]))
    queries = low_back(low(matmul(normed, cross_q)))
    keys_in = low_back(low(matmul(encoded, cross_kv[0])))
    values_in = low_back(low(matmul(encoded, cross_kv[1])))
    slot_index = jnp.arange(ENC_LEN, dtype=jnp.int32)
    cross_valid = jnp.broadcast_to((slot_index < enc_count)[None, :], (TGT_LEN, ENC_LEN))
    attended = attend(queries, keys_in, values_in, cross_valid)
    stream = stream + low_back(matmul(attended, cross_out))
    normed = low(rms_norm(stream, gains[2]))
    gate_pre = low_back(matmul(normed, ff_in[0]))
    up_pre = low_back(matmul(normed, ff_in[1]))
    hidden = low(jax.nn.gelu(gate_pre, approximate=True) * up_pre)
    return stream + matmul(hidden, ff_out)

def reference(dec_in, enc_in, tgt_len, enc_len, self_qkv, self_out, cross_q, cross_kv, cross_out, ff_in, ff_out, gains, cotangent):
    weights = (self_qkv.astype(jnp.float32), self_out.astype(jnp.float32), cross_q.astype(jnp.float32), cross_kv.astype(jnp.float32), cross_out.astype(jnp.float32), ff_in.astype(jnp.float32), ff_out.astype(jnp.float32), gains.astype(jnp.float32))

    def forward(stream_all, encoded_all, weight_set):

        def one_doc(bundle):
            return layer(bundle[0], bundle[1], bundle[2], bundle[3], weight_set)
        return lax.map(jax.checkpoint(one_doc), (stream_all, encoded_all, tgt_len, enc_len))
    result, pullback = jax.vjp(forward, dec_in.astype(jnp.float32), enc_in.astype(jnp.float32), weights)
    d_stream, d_encoded, d_weights = pullback(cotangent.astype(jnp.float32))
    return (result, d_stream, d_encoded, d_weights[0], d_weights[1], d_weights[2], d_weights[3], d_weights[4], d_weights[5], d_weights[6], d_weights[7])
```

```python
import functools

import jax
import jax.numpy as jnp
from jax import lax
from jax.experimental import pallas as pl
from jax.experimental.pallas import tpu as pltpu
from jax.sharding import PartitionSpec as P

HEADS = 6
HEAD_DIM = 64


EPSILON = 1e-06
NEGATIVE = -1e30


def norm_parts(values, gain_row):
    inverse = lax.rsqrt(jnp.mean(values * values, axis=-1, keepdims=True) + EPSILON)
    return (values * inverse * gain_row, inverse)


def norm_back(values, inverse, gain_row, upstream):
    weighted = upstream * gain_row
    inner_sum = jnp.mean(weighted * values, axis=-1, keepdims=True)
    lowered = weighted * inverse - values * (inverse * inverse * inverse) * inner_sum
    return (lowered, jnp.sum(upstream * values * inverse, axis=0))


def matmul_rows(left_op, right_op):
    return jnp.dot(left_op, right_op, preferred_element_type=jnp.float32)


def matmul_back(left_op, right_op):
    return lax.dot_general(
        left_op, right_op, (((1,), (1,)), ((), ())), preferred_element_type=jnp.float32
    )


def matmul_outer(left_op, right_op):
    return lax.dot_general(
        left_op, right_op, (((0,), (0,)), ((), ())), preferred_element_type=jnp.float32
    )


def head_scores(queries, keys_in, allowed):
    scores = jnp.einsum("bqhd,bkhd->bqhk", queries, keys_in, preferred_element_type=jnp.float32)
    return jnp.where(allowed[:, :, None, :], scores, NEGATIVE)


def weigh_values(raised, values_in):
    return jnp.einsum(
        "bqhk,bkhd->bqhd",
        raised.astype(jnp.bfloat16),
        values_in,
        preferred_element_type=jnp.float32,
    )


def mixed_grads(dmixed, numerator, totals):
    d_numer = (dmixed / totals[..., None]).astype(jnp.bfloat16)
    d_total = (-jnp.sum(dmixed * numerator, axis=-1) / (totals * totals)).astype(jnp.bfloat16)
    return (d_numer, d_total)


def score_grads(raised, d_numer, d_total, values_in):
    through = jnp.einsum("bqhd,bkhd->bqhk", d_numer, values_in, preferred_element_type=jnp.float32)
    return (raised * (through + d_total.astype(jnp.float32)[..., None])).astype(jnp.bfloat16)


def pair_grads(d_scores, raised, queries, keys_in, d_numer):
    d_query = jnp.einsum("bqhk,bkhd->bqhd", d_scores, keys_in, preferred_element_type=jnp.float32)
    d_keys = jnp.einsum("bqhk,bqhd->bkhd", d_scores, queries, preferred_element_type=jnp.float32)
    d_values = jnp.einsum(
        "bqhk,bqhd->bkhd", raised.astype(jnp.bfloat16), d_numer, preferred_element_type=jnp.float32
    )
    return (d_query, d_keys, d_values)


def block_size(docs_here):
    if docs_here % 4 == 0:
        return 4
    if docs_here % 2 == 0:
        return 2
    return 1


def feed_forward(rows_in, cot_in, w_in, w_out):
    gate_pre = matmul_rows(rows_in, w_in[0])
    up_pre = matmul_rows(rows_in, w_in[1])
    hidden = (jax.nn.gelu(gate_pre, approximate=True) * up_pre).astype(jnp.bfloat16)
    branch = matmul_rows(hidden, w_out)
    grad_out = matmul_outer(hidden, cot_in)
    d_hidden = matmul_back(cot_in, w_out)
    unused, gelu_pull = jax.vjp(
        lambda gate_val, up_val: jax.nn.gelu(gate_val, approximate=True) * up_val, gate_pre, up_pre
    )
    d_gate, d_up = gelu_pull(d_hidden)
    d_gate_up = jnp.stack([d_gate, d_up]).astype(jnp.bfloat16)
    grad_in = jnp.einsum("td,ctf->cdf", rows_in, d_gate_up, preferred_element_type=jnp.float32)
    d_rows = jnp.einsum("ctf,cdf->td", d_gate_up, w_in, preferred_element_type=jnp.float32)
    return (branch, grad_in, grad_out, d_rows)


def per_device(
    dec_in,
    enc_in,
    tgt_len,
    enc_len,
    self_qkv,
    self_out,
    cross_q,
    cross_kv,
    cross_out,
    ff_in,
    ff_out,
    gains,
    cotangent,
):
    by_rows = (
        lax.all_gather(self_qkv, "seq", axis=1, tiled=True),
        lax.all_gather(self_out, "seq", axis=1, tiled=True),
        lax.all_gather(cross_q, "seq", axis=0, tiled=True),
        lax.all_gather(cross_kv, "seq", axis=1, tiled=True),
        lax.all_gather(cross_out, "seq", axis=1, tiled=True),
        lax.all_gather(ff_in, "seq", axis=1, tiled=True),
        lax.all_gather(ff_out, "seq", axis=1, tiled=True),
        lax.all_gather(gains, "seq", axis=1, tiled=True),
    )
    w_qkv, w_so, w_cq, w_ckv, w_co, w_in, w_out = (
        lax.all_gather(by_rows[0], "doc", axis=2, tiled=True),
        lax.all_gather(by_rows[1], "doc", axis=0, tiled=True),
        lax.all_gather(by_rows[2], "doc", axis=1, tiled=True),
        lax.all_gather(by_rows[3], "doc", axis=2, tiled=True),
        lax.all_gather(by_rows[4], "doc", axis=0, tiled=True),
        lax.all_gather(by_rows[5], "doc", axis=2, tiled=True),
        lax.all_gather(by_rows[6], "doc", axis=0, tiled=True),
    )
    gain_all = by_rows[7].astype(jnp.float32)
    docs_here, rows_doc, model_width = dec_in.shape
    slot_count = enc_in.shape[1]
    seq_ranks = lax.axis_size("seq")
    my_rank = lax.axis_index("seq")
    length = rows_doc * seq_ranks
    inner_width = HEADS * HEAD_DIM
    rows_all = docs_here * rows_doc
    stream = dec_in.reshape(rows_all, model_width).astype(jnp.float32)
    normed1, inverse1 = norm_parts(stream, gain_all[0])
    normed1 = normed1.astype(jnp.bfloat16)
    proj_qkv = jnp.einsum("td,cdk->ctk", normed1, w_qkv, preferred_element_type=jnp.float32).astype(
        jnp.bfloat16
    )
    self_query = proj_qkv[0].reshape(docs_here, rows_doc, HEADS, HEAD_DIM)
    keys_all, values_all = (
        lax.all_gather(
            proj_qkv[1].reshape(docs_here, rows_doc, inner_width), "seq", axis=1, tiled=True
        ),
        lax.all_gather(
            proj_qkv[2].reshape(docs_here, rows_doc, inner_width), "seq", axis=1, tiled=True
        ),
    )
    keys_all = keys_all.reshape(docs_here, length, HEADS, HEAD_DIM)
    values_all = values_all.reshape(docs_here, length, HEADS, HEAD_DIM)
    query_pos = my_rank * rows_doc + jnp.arange(rows_doc, dtype=jnp.int32)
    key_pos = jnp.arange(length, dtype=jnp.int32)
    self_allowed = (key_pos[None, None, :] <= query_pos[None, :, None]) & (
        key_pos[None, None, :] < tgt_len[:, None, None]
    )
    self_scores = head_scores(self_query, keys_all, self_allowed)
    self_top = jnp.max(self_scores, axis=-1)
    self_raised = jnp.exp(self_scores - self_top[..., None])
    self_total = jnp.sum(self_raised, axis=-1)
    self_numer = weigh_values(self_raised, values_all)
    self_mixed = (
        (self_numer / self_total[..., None]).astype(jnp.bfloat16).reshape(rows_all, inner_width)
    )
    stream1 = stream + matmul_rows(self_mixed, w_so)
    normed2, inverse2 = norm_parts(stream1, gain_all[1])
    normed2 = normed2.astype(jnp.bfloat16)
    cross_query = (
        matmul_rows(normed2, w_cq).astype(jnp.bfloat16).reshape(docs_here, rows_doc, inner_width)
    )
    enc_proj = jnp.einsum(
        "bsd,cdk->cbsk", enc_in, w_ckv, preferred_element_type=jnp.float32
    ).astype(jnp.bfloat16)
    queries_all = lax.all_gather(cross_query, "seq", axis=1, tiled=True)
    per_block = block_size(docs_here)
    block_count = docs_here // per_block

    def split_docs(array):
        return array.reshape((block_count, per_block) + array.shape[1:])

    block_queries = split_docs(queries_all.reshape(docs_here, length, HEADS, HEAD_DIM))
    block_keys = split_docs(enc_proj[0].reshape(docs_here, slot_count, HEADS, HEAD_DIM))
    block_values = split_docs(enc_proj[1].reshape(docs_here, slot_count, HEADS, HEAD_DIM))
    slot_pos = my_rank * slot_count + jnp.arange(slot_count, dtype=jnp.int32)
    slot_live = split_docs(slot_pos[None, :] < enc_len[:, None])

    def cross_scores(queries, keys_in, slot_alive):
        allowed = jnp.broadcast_to(
            slot_alive[:, None, :], (slot_alive.shape[0], queries.shape[1], slot_alive.shape[1])
        )
        return head_scores(queries, keys_in, allowed)

    def local_peak(bundle):
        return jnp.max(cross_scores(bundle[0], bundle[1], bundle[2]), axis=-1)

    local_top = lax.map(local_peak, (block_queries, block_keys, slot_live))
    cross_top = lax.pmax(local_top.reshape(docs_here, length, HEADS), "seq")
    block_top = split_docs(cross_top)

    def cross_partial(bundle):
        queries, keys_in, values_in, slot_alive, peak_row = bundle
        raised = jnp.exp(cross_scores(queries, keys_in, slot_alive) - peak_row[..., None])
        return (weigh_values(raised, values_in), jnp.sum(raised, axis=-1))

    part_numer, part_total = lax.map(
        cross_partial, (block_queries, block_keys, block_values, slot_live, block_top)
    )
    cross_numer, cross_total = (
        lax.psum_scatter(
            part_numer.reshape(docs_here, length, inner_width),
            "seq",
            scatter_dimension=1,
            tiled=True,
        ),
        lax.psum_scatter(
            part_total.reshape(docs_here, length, HEADS), "seq", scatter_dimension=1, tiled=True
        ),
    )
    cross_numer = cross_numer.reshape(docs_here, rows_doc, HEADS, HEAD_DIM)
    cross_mixed = (
        (cross_numer / cross_total[..., None]).astype(jnp.bfloat16).reshape(rows_all, inner_width)
    )
    stream2 = stream1 + matmul_rows(cross_mixed, w_co)
    normed3, inverse3 = norm_parts(stream2, gain_all[2])
    normed3 = normed3.astype(jnp.bfloat16)
    cot_rows = cotangent.reshape(rows_all, model_width)
    ff_branch, grad_in, grad_out, d_normed3 = feed_forward(normed3, cot_rows, w_in, w_out)
    layer_out = (stream2 + ff_branch).reshape(docs_here, rows_doc, model_width)
    back_three, gain_grad3 = norm_back(stream2, inverse3, gain_all[2], d_normed3)
    d_stream2 = cot_rows.astype(jnp.float32) + back_three
    d_branch2 = d_stream2.astype(jnp.bfloat16)
    grad_co = matmul_outer(cross_mixed, d_branch2)
    d_mixed2 = matmul_back(d_branch2, w_co).reshape(docs_here, rows_doc, HEADS, HEAD_DIM)
    d_numer2, d_total2 = mixed_grads(d_mixed2, cross_numer, cross_total)
    numer_back, total_back = (
        lax.all_gather(
            d_numer2.reshape(docs_here, rows_doc, inner_width), "seq", axis=1, tiled=True
        ),
        lax.all_gather(d_total2, "seq", axis=1, tiled=True),
    )

    def cross_back_block(bundle):
        queries, keys_in, values_in, slot_alive, peak_row, d_numer, d_total = bundle
        raised = jnp.exp(cross_scores(queries, keys_in, slot_alive) - peak_row[..., None])
        d_scores = score_grads(raised, d_numer, d_total, values_in)
        return pair_grads(d_scores, raised, queries, keys_in, d_numer)

    part_dq, part_dk, part_dv = lax.map(
        cross_back_block,
        (
            block_queries,
            block_keys,
            block_values,
            slot_live,
            block_top,
            split_docs(numer_back.reshape(docs_here, length, HEADS, HEAD_DIM)),
            split_docs(total_back),
        ),
    )
    d_cross_q = lax.psum_scatter(
        part_dq.reshape(docs_here, length, inner_width), "seq", scatter_dimension=1, tiled=True
    )
    d_cross_q = d_cross_q.astype(jnp.bfloat16).reshape(rows_all, inner_width)
    d_enc_proj = jnp.stack(
        [
            part_dk.reshape(docs_here, slot_count, inner_width),
            part_dv.reshape(docs_here, slot_count, inner_width),
        ]
    ).astype(jnp.bfloat16)
    grad_cq = matmul_outer(normed2, d_cross_q)
    grad_ckv = jnp.einsum("bsd,cbsk->cdk", enc_in, d_enc_proj, preferred_element_type=jnp.float32)
    enc_grad = jnp.einsum("cbsk,cdk->bsd", d_enc_proj, w_ckv, preferred_element_type=jnp.float32)
    back_two, gain_grad2 = norm_back(stream1, inverse2, gain_all[1], matmul_back(d_cross_q, w_cq))
    d_stream1 = d_stream2 + back_two
    d_branch1 = d_stream1.astype(jnp.bfloat16)
    grad_so = matmul_outer(self_mixed, d_branch1)
    d_mixed1 = matmul_back(d_branch1, w_so).reshape(docs_here, rows_doc, HEADS, HEAD_DIM)
    d_numer1, d_total1 = mixed_grads(d_mixed1, self_numer, self_total)
    again_raised = jnp.exp(head_scores(self_query, keys_all, self_allowed) - self_top[..., None])
    d_scores1 = score_grads(again_raised, d_numer1, d_total1, values_all)
    d_query1, part_dk1, part_dv1 = pair_grads(
        d_scores1, again_raised, self_query, keys_all, d_numer1
    )
    d_keys1, d_values1 = (
        lax.psum_scatter(
            part_dk1.reshape(docs_here, length, inner_width), "seq", scatter_dimension=1, tiled=True
        ),
        lax.psum_scatter(
            part_dv1.reshape(docs_here, length, inner_width), "seq", scatter_dimension=1, tiled=True
        ),
    )
    d_qkv = jnp.stack(
        [
            d_query1.reshape(rows_all, inner_width),
            d_keys1.reshape(rows_all, inner_width),
            d_values1.reshape(rows_all, inner_width),
        ]
    ).astype(jnp.bfloat16)
    grad_qkv = jnp.einsum("td,ctk->cdk", normed1, d_qkv, preferred_element_type=jnp.float32)
    d_normed1 = jnp.einsum("ctk,cdk->td", d_qkv, w_qkv, preferred_element_type=jnp.float32)
    back_one, gain_grad1 = norm_back(stream, inverse1, gain_all[0], d_normed1)
    dec_grad = (d_stream1 + back_one).reshape(docs_here, rows_doc, model_width)
    gain_sum = lax.psum(jnp.stack([gain_grad1, gain_grad2, gain_grad3]), ("doc", "seq"))
    share_len = model_width // seq_ranks
    grad_gains = lax.dynamic_slice_in_dim(gain_sum, my_rank * share_len, share_len, 1)
    halfway = (
        lax.psum_scatter(grad_qkv, "doc", scatter_dimension=2, tiled=True),
        lax.psum_scatter(grad_so, "doc", scatter_dimension=0, tiled=True),
        lax.psum_scatter(grad_cq, "doc", scatter_dimension=1, tiled=True),
        lax.psum_scatter(grad_ckv, "doc", scatter_dimension=2, tiled=True),
        lax.psum_scatter(grad_co, "doc", scatter_dimension=0, tiled=True),
        lax.psum_scatter(grad_in, "doc", scatter_dimension=2, tiled=True),
        lax.psum_scatter(grad_out, "doc", scatter_dimension=0, tiled=True),
    )
    reduced = (
        lax.psum_scatter(halfway[0], "seq", scatter_dimension=1, tiled=True),
        lax.psum_scatter(halfway[1], "seq", scatter_dimension=1, tiled=True),
        lax.psum_scatter(halfway[2], "seq", scatter_dimension=0, tiled=True),
        lax.psum_scatter(halfway[3], "seq", scatter_dimension=1, tiled=True),
        lax.psum_scatter(halfway[4], "seq", scatter_dimension=1, tiled=True),
        lax.psum_scatter(halfway[5], "seq", scatter_dimension=1, tiled=True),
        lax.psum_scatter(halfway[6], "seq", scatter_dimension=1, tiled=True),
    )
    return (
        layer_out,
        dec_grad,
        enc_grad,
        reduced[0],
        reduced[1],
        reduced[2],
        reduced[3],
        reduced[4],
        reduced[5],
        reduced[6],
        grad_gains,
    )


FOLD = 2


def _masked_rows(is_second, shape, axis):
    index = lax.broadcasted_iota(jnp.int32, shape, axis)
    return (index >= HEAD_DIM) == is_second


def _transposed(array, dtype):
    return jnp.transpose(array.astype(jnp.float32)).astype(dtype)


def _score_mask(chunk, size, block, count, width, causal):
    slot = chunk * size + lax.broadcasted_iota(jnp.int32, (size, width), 0)
    live = slot < count
    if causal:
        query = block * width + lax.broadcasted_iota(jnp.int32, (size, width), 1)
        live = live & (slot <= query)
    return live


def _steps(info_ref, rows, wide):
    blocks = rows // wide
    half = blocks // 2
    return blocks, half, blocks + half


def _chunk_count(count, block, wide, size, causal):
    chunks = (count + size - 1) // size
    if causal:
        chunks = jnp.minimum(chunks, ((block + 1) * wide + size - 1) // size)
    return chunks


def attend_kernel(wide, size, causal, packed, info_ref, *refs):
    if packed:
        qkv_ref, att_ref, mix_ref, stat_ref, vt_ref, score_ref = refs
        lanes = 2 * HEAD_DIM
        q_ref, k_ref, v_ref = (qkv_ref.at[:, pl.ds(i * lanes, lanes)] for i in range(3))
    else:
        q_ref, kv_ref, att_ref, mix_ref, stat_ref, vt_ref, score_ref = refs
        lanes = 2 * HEAD_DIM
        k_ref, v_ref = (kv_ref.at[:, pl.ds(i * lanes, lanes)] for i in range(2))
    rows = q_ref.shape[0]
    slots = k_ref.shape[0]
    count = info_ref[0]
    part = info_ref[1]
    blocks, half, total_steps = _steps(info_ref, rows, wide)

    def flip(c, carry):
        at = pl.multiple_of(c * size, size)
        vt_ref[:, pl.ds(at, size)] = _transposed(v_ref[pl.ds(at, size), :], jnp.bfloat16)
        return carry

    lax.fori_loop(0, slots // size, flip, 0)

    def step(i, carry):
        second = i >= blocks
        block = jnp.where(second, half * part + i - blocks, i)
        at = pl.multiple_of(block * wide, wide)
        mine = _masked_rows(second, (lanes, wide), 0)
        queries = jnp.where(mine, jnp.transpose(q_ref[pl.ds(at, wide), :].astype(jnp.float32)), 0.0)
        queries = queries.astype(jnp.bfloat16)
        chunks = _chunk_count(count, block, wide, size, causal)

        def scores(c, top):
            spot = pl.multiple_of(c * size, size)
            s = jnp.dot(k_ref[pl.ds(spot, size), :], queries, preferred_element_type=jnp.float32)
            s = jnp.where(_score_mask(c, size, block, count, wide, causal), s, NEGATIVE)
            score_ref[pl.ds(spot, size), :] = s
            return jnp.maximum(top, jnp.max(s.reshape(size // 8, 8, wide), axis=0))

        top = lax.fori_loop(0, chunks, scores, jnp.full((8, wide), NEGATIVE, jnp.float32))
        top = jnp.max(top, axis=0, keepdims=True)

        def weigh(c, carry):
            total, numer = carry
            spot = pl.multiple_of(c * size, size)
            e = jnp.exp(score_ref[pl.ds(spot, size), :] - top)
            total = total + jnp.sum(e.reshape(size // 8, 8, wide), axis=0)
            numer = numer + jnp.dot(
                vt_ref[:, pl.ds(spot, size)], e.astype(jnp.bfloat16), preferred_element_type=jnp.float32
            )
            return total, numer

        total, numer = lax.fori_loop(
            0,
            chunks,
            weigh,
            (jnp.zeros((8, wide), jnp.float32), jnp.zeros((lanes, wide), jnp.float32)),
        )
        total = jnp.sum(total, axis=0, keepdims=True)
        mixed = jnp.where(mine, numer / total, 0.0)
        back = jnp.transpose(mixed)

        @pl.when(jnp.logical_not(second))
        def _():
            att_ref[pl.ds(at, wide), :] = back.astype(jnp.bfloat16)
            mix_ref[:, pl.ds(at, wide)] = mixed
            stat_ref[0:1, pl.ds(at, wide)] = top
            stat_ref[1:2, pl.ds(at, wide)] = total

        @pl.when(second)
        def _():
            kept = att_ref[pl.ds(at, wide), :].astype(jnp.float32)
            att_ref[pl.ds(at, wide), :] = (kept + back).astype(jnp.bfloat16)
            mix_ref[:, pl.ds(at, wide)] = mix_ref[:, pl.ds(at, wide)] + mixed
            stat_ref[2:3, pl.ds(at, wide)] = top
            stat_ref[3:4, pl.ds(at, wide)] = total

        return carry

    lax.fori_loop(0, total_steps, step, 0)


def attend_back_kernel(wide, size, causal, packed, info_ref, *refs):
    lanes = 2 * HEAD_DIM
    if packed:
        qkv_ref, dmix_ref, mix_ref, stat_ref, out_ref, kt_ref, dk_ref, dv_ref, dq_ref = refs
        q_ref, k_ref, v_ref = (qkv_ref.at[:, pl.ds(i * lanes, lanes)] for i in range(3))
    else:
        q_ref, kv_ref, dmix_ref, mix_ref, stat_ref, dqo_ref, out_ref, kt_ref, dk_ref, dv_ref, dq_ref = refs
        k_ref, v_ref = (kv_ref.at[:, pl.ds(i * lanes, lanes)] for i in range(2))
    rows = q_ref.shape[0]
    slots = k_ref.shape[0]
    count = info_ref[0]
    part = info_ref[1]
    blocks, half, total_steps = _steps(info_ref, rows, wide)

    def flip(c, carry):
        at = pl.multiple_of(c * size, size)
        kt_ref[:, pl.ds(at, size)] = _transposed(k_ref[pl.ds(at, size), :], jnp.bfloat16)
        dk_ref[pl.ds(at, size), :] = jnp.zeros((size, lanes), jnp.float32)
        dv_ref[pl.ds(at, size), :] = jnp.zeros((size, lanes), jnp.float32)
        return carry

    lax.fori_loop(0, slots // size, flip, 0)

    def step(i, carry):
        second = i >= blocks
        block = jnp.where(second, half * part + i - blocks, i)
        at = pl.multiple_of(block * wide, wide)
        mine = _masked_rows(second, (lanes, wide), 0)
        mine_lanes = _masked_rows(second, (wide, lanes), 1)
        q_plain = q_ref[pl.ds(at, wide), :].astype(jnp.float32)
        q_rows = jnp.where(mine_lanes, q_plain, 0.0).astype(jnp.bfloat16)
        q_cols = jnp.where(mine, jnp.transpose(q_plain), 0.0).astype(jnp.bfloat16)
        dmix = jnp.where(mine, jnp.transpose(dmix_ref[pl.ds(at, wide), :].astype(jnp.float32)), 0.0)
        stats = stat_ref[:, pl.ds(at, wide)]
        top = jnp.where(second, stats[2:3, :], stats[0:1, :])
        total = jnp.where(second, stats[3:4, :], stats[1:2, :])
        dn_wide = dmix / total
        dn_cols = dn_wide.astype(jnp.bfloat16)
        dn_rows = jnp.transpose(dn_wide).astype(jnp.bfloat16)
        mixed = mix_ref[:, pl.ds(at, wide)]
        dtotal = -jnp.sum(dmix * mixed, axis=0, keepdims=True) / total
        dtotal = dtotal.astype(jnp.bfloat16).astype(jnp.float32)
        chunks = _chunk_count(count, block, wide, size, causal)

        def one(c, dq):
            spot = pl.multiple_of(c * size, size)
            s = jnp.dot(k_ref[pl.ds(spot, size), :], q_cols, preferred_element_type=jnp.float32)
            s = jnp.where(_score_mask(c, size, block, count, wide, causal), s, NEGATIVE)
            e = jnp.exp(s - top)
            through = jnp.dot(v_ref[pl.ds(spot, size), :], dn_cols, preferred_element_type=jnp.float32)
            ds = (e * (through + dtotal)).astype(jnp.bfloat16)
            dv_ref[pl.ds(spot, size), :] = dv_ref[pl.ds(spot, size), :] + jnp.dot(
                e.astype(jnp.bfloat16), dn_rows, preferred_element_type=jnp.float32
            )
            dk_ref[pl.ds(spot, size), :] = dk_ref[pl.ds(spot, size), :] + jnp.dot(
                ds, q_rows, preferred_element_type=jnp.float32
            )
            return dq + jnp.dot(kt_ref[:, pl.ds(spot, size)], ds, preferred_element_type=jnp.float32)

        dq = lax.fori_loop(0, chunks, one, jnp.zeros((lanes, wide), jnp.float32))
        back = jnp.transpose(jnp.where(mine, dq, 0.0))

        @pl.when(jnp.logical_not(second))
        def _():
            dq_ref[pl.ds(at, wide), :] = back

        @pl.when(second)
        def _():
            dq_ref[pl.ds(at, wide), :] = dq_ref[pl.ds(at, wide), :] + back

        return carry

    lax.fori_loop(0, total_steps, step, 0)
    shift = lanes if packed else 0
    if packed:
        out_ref[:, 0:lanes] = dq_ref[...].astype(jnp.bfloat16)
    else:
        dqo_ref[...] = dq_ref[...].astype(jnp.bfloat16)

    def emit(c, carry):
        at = pl.multiple_of(c * size, size)
        out_ref[pl.ds(at, size), shift : shift + lanes] = dk_ref[pl.ds(at, size), :].astype(jnp.bfloat16)
        out_ref[pl.ds(at, size), shift + lanes : shift + 2 * lanes] = dv_ref[pl.ds(at, size), :].astype(
            jnp.bfloat16
        )
        return carry

    lax.fori_loop(0, slots // size, emit, 0)


def attention(info, parts, causal):
    lanes = 2 * HEAD_DIM
    rows = parts[0].shape[0]
    slots = parts[-1].shape[0]
    wide = min(256, rows // 2)
    size = min(256 if causal else 512, slots)
    work = rows * slots * lanes * (2 if causal else 4)
    return pl.pallas_call(
        functools.partial(attend_kernel, wide, size, causal, len(parts) == 1),
        name="attend_self" if causal else "attend_cross",
        out_shape=(
            jax.ShapeDtypeStruct((rows, lanes), jnp.bfloat16),
            jax.ShapeDtypeStruct((lanes, rows), jnp.float32),
            jax.ShapeDtypeStruct((8, rows), jnp.float32),
        ),
        in_specs=[pl.BlockSpec(memory_space=pltpu.SMEM)]
        + [pl.BlockSpec(memory_space=pltpu.VMEM)] * len(parts),
        out_specs=(pl.BlockSpec(memory_space=pltpu.VMEM),) * 3,
        scratch_shapes=[
            pltpu.VMEM((lanes, slots), jnp.bfloat16),
            pltpu.VMEM((slots, wide), jnp.float32),
        ],
        compiler_params=pltpu.CompilerParams(vmem_limit_bytes=32 * 1024 * 1024),
        cost_estimate=pl.CostEstimate(flops=work, bytes_accessed=slots * lanes * 8, transcendentals=rows * slots),
    )(info, *parts)


def attention_back(info, parts, dmix, mixed, stats, causal):
    lanes = 2 * HEAD_DIM
    rows = parts[0].shape[0]
    slots = parts[-1].shape[0]
    wide = min(256, rows // 2)
    size = min(256 if causal else 512, slots)
    work = rows * slots * lanes * (5 if causal else 10)
    packed = len(parts) == 1
    outs = (jax.ShapeDtypeStruct((slots, (3 if packed else 2) * lanes), jnp.bfloat16),)
    if not packed:
        outs = (jax.ShapeDtypeStruct((rows, lanes), jnp.bfloat16),) + outs
    return pl.pallas_call(
        functools.partial(attend_back_kernel, wide, size, causal, packed),
        name="attend_self_back" if causal else "attend_cross_back",
        out_shape=outs,
        in_specs=[pl.BlockSpec(memory_space=pltpu.SMEM)]
        + [pl.BlockSpec(memory_space=pltpu.VMEM)] * (len(parts) + 3),
        out_specs=(pl.BlockSpec(memory_space=pltpu.VMEM),) * len(outs),
        scratch_shapes=[
            pltpu.VMEM((lanes, slots), jnp.bfloat16),
            pltpu.VMEM((slots, lanes), jnp.float32),
            pltpu.VMEM((slots, lanes), jnp.float32),
            pltpu.VMEM((rows, lanes), jnp.float32),
        ],
        compiler_params=pltpu.CompilerParams(vmem_limit_bytes=40 * 1024 * 1024),
        cost_estimate=pl.CostEstimate(flops=work, bytes_accessed=slots * lanes * 8, transcendentals=rows * slots),
    )(info, *parts, dmix, mixed, stats)


def spread_heads(array):
    d = HEAD_DIM
    pick = lambda h: array[..., h * d : (h + 1) * d]
    return jnp.stack(
        [jnp.concatenate([pick(a), pick(b)], axis=-1) for a, b in ((0, 1), (2, 1), (3, 4), (5, 4))]
    )


def merge_heads(array):
    d = HEAD_DIM
    wide = array.astype(jnp.float32)
    first = [wide[j, ..., :d] for j in range(4)]
    shared = [wide[j, ..., d:] + wide[j + 1, ..., d:] for j in (0, 2)]
    return jnp.concatenate(
        [first[0], shared[0], first[1], first[2], shared[1], first[3]], axis=-1
    ).astype(jnp.bfloat16)


def by_document(array, x_rank, swap):
    own = lax.dynamic_index_in_dim(array, x_rank, 0, False)
    other = lax.ppermute(lax.dynamic_index_in_dim(array, 1 - x_rank, 0, False), "seq", swap)
    first = x_rank == 0
    return jnp.concatenate([jnp.where(first, own, other), jnp.where(first, other, own)], axis=0)


def by_position(array, x_rank, swap):
    pair = array.reshape((2, array.shape[0] // 2) + array.shape[1:])
    own = lax.dynamic_index_in_dim(pair, x_rank, 0, False)
    other = lax.ppermute(lax.dynamic_index_in_dim(pair, 1 - x_rank, 0, False), "seq", swap)
    first = x_rank == 0
    return jnp.stack([jnp.where(first, own, other), jnp.where(first, other, own)])


def exchange_z(array, z_rank, shifts):
    count = array.shape[0]
    arrived = [
        lax.ppermute(lax.dynamic_index_in_dim(array, (z_rank + k) % count, 0, False), "seq", shifts[k])
        for k in range(1, count)
    ]
    out = array
    for k in range(1, count):
        out = lax.dynamic_update_index_in_dim(out, arrived[k - 1], (z_rank - k) % count, 0)
    return out


def gather_doc(array, pairs_core, pairs_y):
    across = lax.ppermute(array, "doc", pairs_y)
    beside = lax.ppermute(array, "doc", pairs_core)
    far = lax.ppermute(across, "doc", pairs_core)
    return jnp.concatenate([array, beside, across, far], axis=0)


def scatter_doc(array, pairs_core, pairs_y):
    n = array.shape[0] // 4
    low = array.astype(jnp.bfloat16)
    share = lax.ppermute(
        jnp.concatenate([low[n : 2 * n], low[3 * n :]], axis=0), "doc", pairs_core
    ).astype(jnp.float32)
    mine = array[:n] + share[:n]
    across = (array[2 * n : 3 * n] + share[n:]).astype(jnp.bfloat16)
    return mine + lax.ppermute(across, "doc", pairs_y).astype(jnp.float32)


def by_heads(
    dec_in,
    enc_in,
    tgt_len,
    enc_len,
    self_qkv,
    self_out,
    cross_q,
    cross_kv,
    cross_out,
    ff_in,
    ff_out,
    gains,
    cotangent,
):
    f32, bf16 = jnp.float32, jnp.bfloat16
    docs_here, rows_doc, width = dec_in.shape
    slots_doc = enc_in.shape[1]
    doc_ranks, seq_ranks = lax.axis_size("doc"), lax.axis_size("seq")
    seq_rank = lax.axis_index("seq")
    z_rank, x_rank = seq_rank // 2, seq_rank % 2
    swap = [(i, i ^ 1) for i in range(seq_ranks)]
    shifts = [[(i, (i + 2 * k) % seq_ranks) for i in range(seq_ranks)] for k in range(seq_ranks // 2)]
    pairs_core = [(i, i ^ 1) for i in range(doc_ranks)]
    pairs_y = [(i, i ^ 2) for i in range(doc_ranks)]
    inner = HEADS * HEAD_DIM
    share = inner // doc_ranks
    depth = width // seq_ranks
    rows = docs_here * rows_doc

    small = jnp.concatenate(
        [self_qkv[0], self_qkv[1], self_qkv[2], cross_q, cross_kv[0], cross_kv[1], self_out.T, cross_out.T],
        axis=1,
    )
    every = lax.all_gather(small, ("doc", "seq"), axis=0, tiled=True).reshape(doc_ranks, width, 8 * share)
    w_qkv = every[:, :, : 3 * share]
    w_cq = every[:, :, 3 * share : 4 * share]
    w_ckv = every[:, :, 4 * share : 6 * share]
    w_so = every[:, :, 6 * share : 7 * share]
    w_co = every[:, :, 7 * share :]
    gain_all = lax.all_gather(gains, "seq", axis=1, tiled=True).astype(f32)
    ff_mine = jnp.concatenate([ff_in[0], ff_in[1], ff_out.T], axis=1)
    ff_all = lax.all_gather(ff_mine, "seq", axis=0, tiled=True)
    hidden_here = ff_in.shape[2]
    w_gate, w_up = ff_all[:, :hidden_here], ff_all[:, hidden_here : 2 * hidden_here]
    w_down = ff_all[:, 2 * hidden_here :]

    def project(rows_in, weight, parts):
        out = jnp.einsum("td,edk->etk", rows_in, weight, preferred_element_type=f32).astype(bf16)
        return [
            jnp.concatenate([out[e, :, i * share : (i + 1) * share] for e in range(doc_ranks)], axis=-1)
            for i in range(parts)
        ]

    def lift(inner_in, weight):
        split = inner_in.reshape(inner_in.shape[0], doc_ranks, share)
        return jnp.einsum("tek,edk->td", split, weight, preferred_element_type=f32)

    def outer(rows_in, inner_in):
        split = inner_in.reshape(inner_in.shape[0], doc_ranks, share)
        return jnp.einsum("td,tek->edk", rows_in, split, preferred_element_type=f32).astype(bf16)

    info_self = jnp.stack([lax.dynamic_index_in_dim(tgt_len, x_rank, 0, False), z_rank % 2])
    info_cross = jnp.stack([lax.dynamic_index_in_dim(enc_len, x_rank, 0, False), z_rank % 2])

    stream = by_document(dec_in, x_rank, swap).astype(f32)
    cot = by_document(cotangent, x_rank, swap)
    cot_all = gather_doc(cot, pairs_core, pairs_y)
    normed1, inverse1 = norm_parts(stream, gain_all[0])
    normed1 = normed1.astype(bf16)
    qkv = jnp.concatenate([spread_heads(p) for p in project(normed1, w_qkv, 3)], axis=-1)
    qkv_heads = exchange_z(qkv, z_rank, shifts).reshape(4 * rows, 6 * HEAD_DIM)
    att1, mix1, stat1 = attention(info_self, (qkv_heads,), True)
    att1 = merge_heads(exchange_z(att1.reshape(4, rows, 2 * HEAD_DIM), z_rank, shifts))
    stream1 = stream + lift(att1, w_so)
    normed2, inverse2 = norm_parts(stream1, gain_all[1])
    normed2 = normed2.astype(bf16)
    (cq,) = project(normed2, w_cq, 1)
    cq_heads = exchange_z(spread_heads(cq), z_rank, shifts).reshape(4 * rows, 2 * HEAD_DIM)

    enc_rows = enc_in.reshape(docs_here * slots_doc, width)
    ckv = jnp.concatenate([spread_heads(p) for p in project(enc_rows, w_ckv, 2)], axis=-1)
    ckv = ckv.reshape(4, docs_here, slots_doc, 4 * HEAD_DIM).transpose(1, 2, 0, 3)
    ckv = by_document(ckv, x_rank, swap).transpose(1, 0, 2)
    ckv_heads = exchange_z(ckv, z_rank, shifts).reshape(4 * docs_here * slots_doc, 4 * HEAD_DIM)

    att2, mix2, stat2 = attention(info_cross, (cq_heads, ckv_heads), False)
    att2 = merge_heads(exchange_z(att2.reshape(4, rows, 2 * HEAD_DIM), z_rank, shifts))
    stream2 = stream1 + lift(att2, w_co)
    normed3, inverse3 = norm_parts(stream2, gain_all[2])
    normed3 = normed3.astype(bf16)

    n3_all = gather_doc(normed3, pairs_core, pairs_y)
    gate_pre = matmul_rows(n3_all, w_gate)
    up_pre = matmul_rows(n3_all, w_up)
    d_hidden = matmul_rows(cot_all, w_down)
    hidden, gelu_pull = jax.vjp(
        lambda gate_val, up_val: jax.nn.gelu(gate_val, approximate=True) * up_val, gate_pre, up_pre
    )
    d_gate, d_up = gelu_pull(d_hidden)
    hidden, d_gate, d_up = hidden.astype(bf16), d_gate.astype(bf16), d_up.astype(bf16)
    d_n3 = matmul_back(d_gate, w_gate) + matmul_back(d_up, w_up)
    d_normed3 = scatter_doc(d_n3, pairs_core, pairs_y)
    branch = scatter_doc(matmul_back(hidden, w_down), pairs_core, pairs_y)
    ff_grads = jnp.concatenate(
        [
            matmul_outer(n3_all, d_gate).astype(bf16),
            matmul_outer(n3_all, d_up).astype(bf16),
            matmul_outer(cot_all, hidden).astype(bf16),
        ],
        axis=1,
    )
    ff_sum = lax.psum_scatter(ff_grads, "seq", scatter_dimension=0, tiled=True)
    layer_out = by_position(stream2 + branch, x_rank, swap)

    back_three, gain_grad3 = norm_back(stream2, inverse3, gain_all[2], d_normed3)
    d_stream2 = cot.astype(f32) + back_three
    d_branch2 = d_stream2.astype(bf16)
    (d_mix2,) = project(d_branch2, w_co, 1)
    d_mix2 = exchange_z(spread_heads(d_mix2), z_rank, shifts).reshape(4 * rows, 2 * HEAD_DIM)
    d_cq, d_ckv = attention_back(info_cross, (cq_heads, ckv_heads), d_mix2, mix2, stat2, False)
    d_cq = merge_heads(exchange_z(d_cq.reshape(4, rows, 2 * HEAD_DIM), z_rank, shifts))
    back_two, gain_grad2 = norm_back(stream1, inverse2, gain_all[1], lift(d_cq, w_cq))
    d_stream1 = d_stream2 + back_two
    d_branch1 = d_stream1.astype(bf16)
    (d_mix1,) = project(d_branch1, w_so, 1)
    d_mix1 = exchange_z(spread_heads(d_mix1), z_rank, shifts).reshape(4 * rows, 2 * HEAD_DIM)
    (d_qkv,) = attention_back(info_self, (qkv_heads,), d_mix1, mix1, stat1, True)
    d_qkv = exchange_z(d_qkv.reshape(4, rows, 6 * HEAD_DIM), z_rank, shifts)
    lanes = 2 * HEAD_DIM
    d_q, d_k, d_v = (merge_heads(d_qkv[..., i * lanes : (i + 1) * lanes]) for i in range(3))

    d_ckv = exchange_z(d_ckv.reshape(4, docs_here * slots_doc, 4 * HEAD_DIM), z_rank, shifts)
    d_ckv = by_position(d_ckv.transpose(1, 0, 2), x_rank, swap)
    d_ckv = d_ckv.reshape(docs_here * slots_doc, 4, 4 * HEAD_DIM).transpose(1, 0, 2)
    d_ck, d_cv = (merge_heads(d_ckv[..., i * lanes : (i + 1) * lanes]) for i in range(2))
    enc_grad = lift(d_ck, w_ckv[:, :, :share]) + lift(d_cv, w_ckv[:, :, share:])
    enc_grad = enc_grad.reshape(docs_here, slots_doc, width)

    d_normed1 = (
        lift(d_q, w_qkv[:, :, :share])
        + lift(d_k, w_qkv[:, :, share : 2 * share])
        + lift(d_v, w_qkv[:, :, 2 * share :])
    )
    back_one, gain_grad1 = norm_back(stream, inverse1, gain_all[0], d_normed1)
    dec_grad = by_position(d_stream1 + back_one, x_rank, swap)

    small_grads = jnp.concatenate(
        [
            outer(normed1, d_q),
            outer(normed1, d_k),
            outer(normed1, d_v),
            outer(normed2, d_cq),
            outer(enc_rows, d_ck),
            outer(enc_rows, d_cv),
            outer(d_branch1, att1),
            outer(d_branch2, att2),
        ],
        axis=-1,
    ).reshape(doc_ranks, seq_ranks, depth, 8 * share)
    gain_terms = jnp.stack([gain_grad1, gain_grad2, gain_grad3]).reshape(3, seq_ranks, depth)
    gain_terms = gain_terms.transpose(1, 0, 2).reshape(1, seq_ranks, 1, 3 * depth).astype(bf16)
    gain_terms = jnp.pad(gain_terms, ((0, 0), (0, 0), (0, 7), (0, 8 * share - 3 * depth)))
    gain_terms = jnp.broadcast_to(gain_terms, (doc_ranks,) + gain_terms.shape[1:])
    packed = jnp.concatenate([small_grads, gain_terms], axis=2).reshape(-1, 8 * share)
    summed = lax.psum_scatter(packed, ("doc", "seq"), scatter_dimension=0, tiled=True).astype(f32)
    grad_gains = summed[depth, : 3 * depth].reshape(3, depth)
    mine = summed[:depth]
    piece = lambda i: mine[:, i * share : (i + 1) * share]
    ff_sum = ff_sum.astype(f32)
    return (
        layer_out,
        dec_grad,
        enc_grad,
        jnp.stack([piece(0), piece(1), piece(2)]),
        piece(6).T,
        piece(3),
        jnp.stack([piece(4), piece(5)]),
        piece(7).T,
        jnp.stack([ff_sum[:, :hidden_here], ff_sum[:, hidden_here : 2 * hidden_here]]),
        ff_sum[:, 2 * hidden_here :].T,
        grad_gains,
    )


def fits_by_heads(doc_ranks, seq_ranks, docs):
    return doc_ranks == 4 and seq_ranks == 8 and docs == 8


def solution(mesh):
    def either(dec_in, *others):
        docs = dec_in.shape[0] * mesh.shape["doc"]
        if fits_by_heads(mesh.shape["doc"], mesh.shape["seq"], docs):
            return by_heads(dec_in, *others)
        return per_device(dec_in, *others)

    return jax.shard_map(
        either,
        mesh=mesh,
        in_specs=(
            P("doc", "seq", None),
            P("doc", "seq", None),
            P("doc"),
            P("doc"),
            P(None, "seq", "doc"),
            P("doc", "seq"),
            P("seq", "doc"),
            P(None, "seq", "doc"),
            P("doc", "seq"),
            P(None, "seq", "doc"),
            P("doc", "seq"),
            P(None, "seq"),
            P("doc", "seq", None),
        ),
        out_specs=(
            P("doc", "seq", None),
            P("doc", "seq", None),
            P("doc", "seq", None),
            P(None, "seq", "doc"),
            P("doc", "seq"),
            P("seq", "doc"),
            P(None, "seq", "doc"),
            P("doc", "seq"),
            P(None, "seq", "doc"),
            P("doc", "seq"),
            P(None, "seq"),
        ),
        check_vma=False,
    )
```

```python
import functools

import jax
import jax.numpy as jnp
from jax import lax
from jax.experimental import pallas as pl
from jax.experimental.pallas import tpu as pltpu
from jax.sharding import PartitionSpec as P

HEADS = 6
HEAD_DIM = 64


EPSILON = 1e-06
NEGATIVE = -1e30


def norm_parts(values, gain_row):
    inverse = lax.rsqrt(jnp.mean(values * values, axis=-1, keepdims=True) + EPSILON)
    return (values * inverse * gain_row, inverse)


def norm_back(values, inverse, gain_row, upstream):
    weighted = upstream * gain_row
    inner_sum = jnp.mean(weighted * values, axis=-1, keepdims=True)
    lowered = weighted * inverse - values * (inverse * inverse * inverse) * inner_sum
    return (lowered, jnp.sum(upstream * values * inverse, axis=0))


def matmul_rows(left_op, right_op):
    return jnp.dot(left_op, right_op, preferred_element_type=jnp.float32)


def matmul_back(left_op, right_op):
    return lax.dot_general(
        left_op, right_op, (((1,), (1,)), ((), ())), preferred_element_type=jnp.float32
    )


def matmul_outer(left_op, right_op):
    return lax.dot_general(
        left_op, right_op, (((0,), (0,)), ((), ())), preferred_element_type=jnp.float32
    )


def head_scores(queries, keys_in, allowed):
    scores = jnp.einsum("bqhd,bkhd->bqhk", queries, keys_in, preferred_element_type=jnp.float32)
    return jnp.where(allowed[:, :, None, :], scores, NEGATIVE)


def weigh_values(raised, values_in):
    return jnp.einsum(
        "bqhk,bkhd->bqhd",
        raised.astype(jnp.bfloat16),
        values_in,
        preferred_element_type=jnp.float32,
    )


def mixed_grads(dmixed, numerator, totals):
    d_numer = (dmixed / totals[..., None]).astype(jnp.bfloat16)
    d_total = (-jnp.sum(dmixed * numerator, axis=-1) / (totals * totals)).astype(jnp.bfloat16)
    return (d_numer, d_total)


def score_grads(raised, d_numer, d_total, values_in):
    through = jnp.einsum("bqhd,bkhd->bqhk", d_numer, values_in, preferred_element_type=jnp.float32)
    return (raised * (through + d_total.astype(jnp.float32)[..., None])).astype(jnp.bfloat16)


def pair_grads(d_scores, raised, queries, keys_in, d_numer):
    d_query = jnp.einsum("bqhk,bkhd->bqhd", d_scores, keys_in, preferred_element_type=jnp.float32)
    d_keys = jnp.einsum("bqhk,bqhd->bkhd", d_scores, queries, preferred_element_type=jnp.float32)
    d_values = jnp.einsum(
        "bqhk,bqhd->bkhd", raised.astype(jnp.bfloat16), d_numer, preferred_element_type=jnp.float32
    )
    return (d_query, d_keys, d_values)


def block_size(docs_here):
    if docs_here % 4 == 0:
        return 4
    if docs_here % 2 == 0:
        return 2
    return 1


def feed_forward(rows_in, cot_in, w_in, w_out):
    gate_pre = matmul_rows(rows_in, w_in[0])
    up_pre = matmul_rows(rows_in, w_in[1])
    hidden = (jax.nn.gelu(gate_pre, approximate=True) * up_pre).astype(jnp.bfloat16)
    branch = matmul_rows(hidden, w_out)
    grad_out = matmul_outer(hidden, cot_in)
    d_hidden = matmul_back(cot_in, w_out)
    unused, gelu_pull = jax.vjp(
        lambda gate_val, up_val: jax.nn.gelu(gate_val, approximate=True) * up_val, gate_pre, up_pre
    )
    d_gate, d_up = gelu_pull(d_hidden)
    d_gate_up = jnp.stack([d_gate, d_up]).astype(jnp.bfloat16)
    grad_in = jnp.einsum("td,ctf->cdf", rows_in, d_gate_up, preferred_element_type=jnp.float32)
    d_rows = jnp.einsum("ctf,cdf->td", d_gate_up, w_in, preferred_element_type=jnp.float32)
    return (branch, grad_in, grad_out, d_rows)


def per_device(
    dec_in,
    enc_in,
    tgt_len,
    enc_len,
    self_qkv,
    self_out,
    cross_q,
    cross_kv,
    cross_out,
    ff_in,
    ff_out,
    gains,
    cotangent,
):
    by_rows = (
        lax.all_gather(self_qkv, "seq", axis=1, tiled=True),
        lax.all_gather(self_out, "seq", axis=1, tiled=True),
        lax.all_gather(cross_q, "seq", axis=0, tiled=True),
        lax.all_gather(cross_kv, "seq", axis=1, tiled=True),
        lax.all_gather(cross_out, "seq", axis=1, tiled=True),
        lax.all_gather(ff_in, "seq", axis=1, tiled=True),
        lax.all_gather(ff_out, "seq", axis=1, tiled=True),
        lax.all_gather(gains, "seq", axis=1, tiled=True),
    )
    w_qkv, w_so, w_cq, w_ckv, w_co, w_in, w_out = (
        lax.all_gather(by_rows[0], "doc", axis=2, tiled=True),
        lax.all_gather(by_rows[1], "doc", axis=0, tiled=True),
        lax.all_gather(by_rows[2], "doc", axis=1, tiled=True),
        lax.all_gather(by_rows[3], "doc", axis=2, tiled=True),
        lax.all_gather(by_rows[4], "doc", axis=0, tiled=True),
        lax.all_gather(by_rows[5], "doc", axis=2, tiled=True),
        lax.all_gather(by_rows[6], "doc", axis=0, tiled=True),
    )
    gain_all = by_rows[7].astype(jnp.float32)
    docs_here, rows_doc, model_width = dec_in.shape
    slot_count = enc_in.shape[1]
    seq_ranks = lax.axis_size("seq")
    my_rank = lax.axis_index("seq")
    length = rows_doc * seq_ranks
    inner_width = HEADS * HEAD_DIM
    rows_all = docs_here * rows_doc
    stream = dec_in.reshape(rows_all, model_width).astype(jnp.float32)
    normed1, inverse1 = norm_parts(stream, gain_all[0])
    normed1 = normed1.astype(jnp.bfloat16)
    proj_qkv = jnp.einsum("td,cdk->ctk", normed1, w_qkv, preferred_element_type=jnp.float32).astype(
        jnp.bfloat16
    )
    self_query = proj_qkv[0].reshape(docs_here, rows_doc, HEADS, HEAD_DIM)
    keys_all, values_all = (
        lax.all_gather(
            proj_qkv[1].reshape(docs_here, rows_doc, inner_width), "seq", axis=1, tiled=True
        ),
        lax.all_gather(
            proj_qkv[2].reshape(docs_here, rows_doc, inner_width), "seq", axis=1, tiled=True
        ),
    )
    keys_all = keys_all.reshape(docs_here, length, HEADS, HEAD_DIM)
    values_all = values_all.reshape(docs_here, length, HEADS, HEAD_DIM)
    query_pos = my_rank * rows_doc + jnp.arange(rows_doc, dtype=jnp.int32)
    key_pos = jnp.arange(length, dtype=jnp.int32)
    self_allowed = (key_pos[None, None, :] <= query_pos[None, :, None]) & (
        key_pos[None, None, :] < tgt_len[:, None, None]
    )
    self_scores = head_scores(self_query, keys_all, self_allowed)
    self_top = jnp.max(self_scores, axis=-1)
    self_raised = jnp.exp(self_scores - self_top[..., None])
    self_total = jnp.sum(self_raised, axis=-1)
    self_numer = weigh_values(self_raised, values_all)
    self_mixed = (
        (self_numer / self_total[..., None]).astype(jnp.bfloat16).reshape(rows_all, inner_width)
    )
    stream1 = stream + matmul_rows(self_mixed, w_so)
    normed2, inverse2 = norm_parts(stream1, gain_all[1])
    normed2 = normed2.astype(jnp.bfloat16)
    cross_query = (
        matmul_rows(normed2, w_cq).astype(jnp.bfloat16).reshape(docs_here, rows_doc, inner_width)
    )
    enc_proj = jnp.einsum(
        "bsd,cdk->cbsk", enc_in, w_ckv, preferred_element_type=jnp.float32
    ).astype(jnp.bfloat16)
    queries_all = lax.all_gather(cross_query, "seq", axis=1, tiled=True)
    per_block = block_size(docs_here)
    block_count = docs_here // per_block

    def split_docs(array):
        return array.reshape((block_count, per_block) + array.shape[1:])

    block_queries = split_docs(queries_all.reshape(docs_here, length, HEADS, HEAD_DIM))
    block_keys = split_docs(enc_proj[0].reshape(docs_here, slot_count, HEADS, HEAD_DIM))
    block_values = split_docs(enc_proj[1].reshape(docs_here, slot_count, HEADS, HEAD_DIM))
    slot_pos = my_rank * slot_count + jnp.arange(slot_count, dtype=jnp.int32)
    slot_live = split_docs(slot_pos[None, :] < enc_len[:, None])

    def cross_scores(queries, keys_in, slot_alive):
        allowed = jnp.broadcast_to(
            slot_alive[:, None, :], (slot_alive.shape[0], queries.shape[1], slot_alive.shape[1])
        )
        return head_scores(queries, keys_in, allowed)

    def local_peak(bundle):
        return jnp.max(cross_scores(bundle[0], bundle[1], bundle[2]), axis=-1)

    local_top = lax.map(local_peak, (block_queries, block_keys, slot_live))
    cross_top = lax.pmax(local_top.reshape(docs_here, length, HEADS), "seq")
    block_top = split_docs(cross_top)

    def cross_partial(bundle):
        queries, keys_in, values_in, slot_alive, peak_row = bundle
        raised = jnp.exp(cross_scores(queries, keys_in, slot_alive) - peak_row[..., None])
        return (weigh_values(raised, values_in), jnp.sum(raised, axis=-1))

    part_numer, part_total = lax.map(
        cross_partial, (block_queries, block_keys, block_values, slot_live, block_top)
    )
    cross_numer, cross_total = (
        lax.psum_scatter(
            part_numer.reshape(docs_here, length, inner_width),
            "seq",
            scatter_dimension=1,
            tiled=True,
        ),
        lax.psum_scatter(
            part_total.reshape(docs_here, length, HEADS), "seq", scatter_dimension=1, tiled=True
        ),
    )
    cross_numer = cross_numer.reshape(docs_here, rows_doc, HEADS, HEAD_DIM)
    cross_mixed = (
        (cross_numer / cross_total[..., None]).astype(jnp.bfloat16).reshape(rows_all, inner_width)
    )
    stream2 = stream1 + matmul_rows(cross_mixed, w_co)
    normed3, inverse3 = norm_parts(stream2, gain_all[2])
    normed3 = normed3.astype(jnp.bfloat16)
    cot_rows = cotangent.reshape(rows_all, model_width)
    ff_branch, grad_in, grad_out, d_normed3 = feed_forward(normed3, cot_rows, w_in, w_out)
    layer_out = (stream2 + ff_branch).reshape(docs_here, rows_doc, model_width)
    back_three, gain_grad3 = norm_back(stream2, inverse3, gain_all[2], d_normed3)
    d_stream2 = cot_rows.astype(jnp.float32) + back_three
    d_branch2 = d_stream2.astype(jnp.bfloat16)
    grad_co = matmul_outer(cross_mixed, d_branch2)
    d_mixed2 = matmul_back(d_branch2, w_co).reshape(docs_here, rows_doc, HEADS, HEAD_DIM)
    d_numer2, d_total2 = mixed_grads(d_mixed2, cross_numer, cross_total)
    numer_back, total_back = (
        lax.all_gather(
            d_numer2.reshape(docs_here, rows_doc, inner_width), "seq", axis=1, tiled=True
        ),
        lax.all_gather(d_total2, "seq", axis=1, tiled=True),
    )

    def cross_back_block(bundle):
        queries, keys_in, values_in, slot_alive, peak_row, d_numer, d_total = bundle
        raised = jnp.exp(cross_scores(queries, keys_in, slot_alive) - peak_row[..., None])
        d_scores = score_grads(raised, d_numer, d_total, values_in)
        return pair_grads(d_scores, raised, queries, keys_in, d_numer)

    part_dq, part_dk, part_dv = lax.map(
        cross_back_block,
        (
            block_queries,
            block_keys,
            block_values,
            slot_live,
            block_top,
            split_docs(numer_back.reshape(docs_here, length, HEADS, HEAD_DIM)),
            split_docs(total_back),
        ),
    )
    d_cross_q = lax.psum_scatter(
        part_dq.reshape(docs_here, length, inner_width), "seq", scatter_dimension=1, tiled=True
    )
    d_cross_q = d_cross_q.astype(jnp.bfloat16).reshape(rows_all, inner_width)
    d_enc_proj = jnp.stack(
        [
            part_dk.reshape(docs_here, slot_count, inner_width),
            part_dv.reshape(docs_here, slot_count, inner_width),
        ]
    ).astype(jnp.bfloat16)
    grad_cq = matmul_outer(normed2, d_cross_q)
    grad_ckv = jnp.einsum("bsd,cbsk->cdk", enc_in, d_enc_proj, preferred_element_type=jnp.float32)
    enc_grad = jnp.einsum("cbsk,cdk->bsd", d_enc_proj, w_ckv, preferred_element_type=jnp.float32)
    back_two, gain_grad2 = norm_back(stream1, inverse2, gain_all[1], matmul_back(d_cross_q, w_cq))
    d_stream1 = d_stream2 + back_two
    d_branch1 = d_stream1.astype(jnp.bfloat16)
    grad_so = matmul_outer(self_mixed, d_branch1)
    d_mixed1 = matmul_back(d_branch1, w_so).reshape(docs_here, rows_doc, HEADS, HEAD_DIM)
    d_numer1, d_total1 = mixed_grads(d_mixed1, self_numer, self_total)
    again_raised = jnp.exp(head_scores(self_query, keys_all, self_allowed) - self_top[..., None])
    d_scores1 = score_grads(again_raised, d_numer1, d_total1, values_all)
    d_query1, part_dk1, part_dv1 = pair_grads(
        d_scores1, again_raised, self_query, keys_all, d_numer1
    )
    d_keys1, d_values1 = (
        lax.psum_scatter(
            part_dk1.reshape(docs_here, length, inner_width), "seq", scatter_dimension=1, tiled=True
        ),
        lax.psum_scatter(
            part_dv1.reshape(docs_here, length, inner_width), "seq", scatter_dimension=1, tiled=True
        ),
    )
    d_qkv = jnp.stack(
        [
            d_query1.reshape(rows_all, inner_width),
            d_keys1.reshape(rows_all, inner_width),
            d_values1.reshape(rows_all, inner_width),
        ]
    ).astype(jnp.bfloat16)
    grad_qkv = jnp.einsum("td,ctk->cdk", normed1, d_qkv, preferred_element_type=jnp.float32)
    d_normed1 = jnp.einsum("ctk,cdk->td", d_qkv, w_qkv, preferred_element_type=jnp.float32)
    back_one, gain_grad1 = norm_back(stream, inverse1, gain_all[0], d_normed1)
    dec_grad = (d_stream1 + back_one).reshape(docs_here, rows_doc, model_width)
    gain_sum = lax.psum(jnp.stack([gain_grad1, gain_grad2, gain_grad3]), ("doc", "seq"))
    share_len = model_width // seq_ranks
    grad_gains = lax.dynamic_slice_in_dim(gain_sum, my_rank * share_len, share_len, 1)
    halfway = (
        lax.psum_scatter(grad_qkv, "doc", scatter_dimension=2, tiled=True),
        lax.psum_scatter(grad_so, "doc", scatter_dimension=0, tiled=True),
        lax.psum_scatter(grad_cq, "doc", scatter_dimension=1, tiled=True),
        lax.psum_scatter(grad_ckv, "doc", scatter_dimension=2, tiled=True),
        lax.psum_scatter(grad_co, "doc", scatter_dimension=0, tiled=True),
        lax.psum_scatter(grad_in, "doc", scatter_dimension=2, tiled=True),
        lax.psum_scatter(grad_out, "doc", scatter_dimension=0, tiled=True),
    )
    reduced = (
        lax.psum_scatter(halfway[0], "seq", scatter_dimension=1, tiled=True),
        lax.psum_scatter(halfway[1], "seq", scatter_dimension=1, tiled=True),
        lax.psum_scatter(halfway[2], "seq", scatter_dimension=0, tiled=True),
        lax.psum_scatter(halfway[3], "seq", scatter_dimension=1, tiled=True),
        lax.psum_scatter(halfway[4], "seq", scatter_dimension=1, tiled=True),
        lax.psum_scatter(halfway[5], "seq", scatter_dimension=1, tiled=True),
        lax.psum_scatter(halfway[6], "seq", scatter_dimension=1, tiled=True),
    )
    return (
        layer_out,
        dec_grad,
        enc_grad,
        reduced[0],
        reduced[1],
        reduced[2],
        reduced[3],
        reduced[4],
        reduced[5],
        reduced[6],
        grad_gains,
    )


FOLD = 2


def _masked_rows(is_second, shape, axis):
    index = lax.broadcasted_iota(jnp.int32, shape, axis)
    return (index >= HEAD_DIM) == is_second


def _transposed(array, dtype):
    return jnp.transpose(array.astype(jnp.float32)).astype(dtype)


def _score_mask(chunk, size, block, count, width, causal):
    slot = chunk * size + lax.broadcasted_iota(jnp.int32, (size, width), 0)
    live = slot < count
    if causal:
        query = block * width + lax.broadcasted_iota(jnp.int32, (size, width), 1)
        live = live & (slot <= query)
    return live


def _steps(info_ref, rows, wide):
    blocks = rows // wide
    half = blocks // 2
    return blocks, half, blocks + half


def _chunk_count(count, block, wide, size, causal):
    chunks = (count + size - 1) // size
    if causal:
        chunks = jnp.minimum(chunks, ((block + 1) * wide + size - 1) // size)
    return chunks


def attend_kernel(wide, size, causal, packed, info_ref, *refs):
    if packed:
        qkv_ref, att_ref, mix_ref, stat_ref, vt_ref, score_ref = refs
        lanes = 2 * HEAD_DIM
        q_ref, k_ref, v_ref = (qkv_ref.at[:, pl.ds(i * lanes, lanes)] for i in range(3))
    else:
        q_ref, kv_ref, att_ref, mix_ref, stat_ref, vt_ref, score_ref = refs
        lanes = 2 * HEAD_DIM
        k_ref, v_ref = (kv_ref.at[:, pl.ds(i * lanes, lanes)] for i in range(2))
    rows = q_ref.shape[0]
    slots = k_ref.shape[0]
    count = info_ref[0]
    part = info_ref[1]
    blocks, half, total_steps = _steps(info_ref, rows, wide)

    def flip(c, carry):
        at = pl.multiple_of(c * size, size)
        vt_ref[:, pl.ds(at, size)] = _transposed(v_ref[pl.ds(at, size), :], jnp.bfloat16)
        return carry

    lax.fori_loop(0, slots // size, flip, 0)

    def step(i, carry):
        second = i >= blocks
        block = jnp.where(second, half * part + i - blocks, i)
        at = pl.multiple_of(block * wide, wide)
        mine = _masked_rows(second, (lanes, wide), 0)
        queries = jnp.where(mine, jnp.transpose(q_ref[pl.ds(at, wide), :].astype(jnp.float32)), 0.0)
        queries = queries.astype(jnp.bfloat16)
        chunks = _chunk_count(count, block, wide, size, causal)

        def scores(c, top):
            spot = pl.multiple_of(c * size, size)
            s = jnp.dot(k_ref[pl.ds(spot, size), :], queries, preferred_element_type=jnp.float32)
            s = jnp.where(_score_mask(c, size, block, count, wide, causal), s, NEGATIVE)
            score_ref[pl.ds(spot, size), :] = s
            return jnp.maximum(top, jnp.max(s.reshape(size // 8, 8, wide), axis=0))

        top = lax.fori_loop(0, chunks, scores, jnp.full((8, wide), NEGATIVE, jnp.float32))
        top = jnp.max(top, axis=0, keepdims=True)

        def weigh(c, carry):
            total, numer = carry
            spot = pl.multiple_of(c * size, size)
            e = jnp.exp(score_ref[pl.ds(spot, size), :] - top)
            total = total + jnp.sum(e.reshape(size // 8, 8, wide), axis=0)
            numer = numer + jnp.dot(
                vt_ref[:, pl.ds(spot, size)], e.astype(jnp.bfloat16), preferred_element_type=jnp.float32
            )
            return total, numer

        total, numer = lax.fori_loop(
            0,
            chunks,
            weigh,
            (jnp.zeros((8, wide), jnp.float32), jnp.zeros((lanes, wide), jnp.float32)),
        )
        total = jnp.sum(total, axis=0, keepdims=True)
        mixed = jnp.where(mine, numer / total, 0.0)
        back = jnp.transpose(mixed)

        @pl.when(jnp.logical_not(second))
        def _():
            att_ref[pl.ds(at, wide), :] = back.astype(jnp.bfloat16)
            mix_ref[:, pl.ds(at, wide)] = mixed
            stat_ref[0:1, pl.ds(at, wide)] = top
            stat_ref[1:2, pl.ds(at, wide)] = total

        @pl.when(second)
        def _():
            kept = att_ref[pl.ds(at, wide), :].astype(jnp.float32)
            att_ref[pl.ds(at, wide), :] = (kept + back).astype(jnp.bfloat16)
            mix_ref[:, pl.ds(at, wide)] = mix_ref[:, pl.ds(at, wide)] + mixed
            stat_ref[2:3, pl.ds(at, wide)] = top
            stat_ref[3:4, pl.ds(at, wide)] = total

        return carry

    lax.fori_loop(0, total_steps, step, 0)


def attend_back_kernel(wide, size, causal, packed, info_ref, *refs):
    lanes = 2 * HEAD_DIM
    if packed:
        qkv_ref, dmix_ref, mix_ref, stat_ref, out_ref, kt_ref, dk_ref, dv_ref, dq_ref = refs
        q_ref, k_ref, v_ref = (qkv_ref.at[:, pl.ds(i * lanes, lanes)] for i in range(3))
    else:
        q_ref, kv_ref, dmix_ref, mix_ref, stat_ref, dqo_ref, out_ref, kt_ref, dk_ref, dv_ref, dq_ref = refs
        k_ref, v_ref = (kv_ref.at[:, pl.ds(i * lanes, lanes)] for i in range(2))
    rows = q_ref.shape[0]
    slots = k_ref.shape[0]
    count = info_ref[0]
    part = info_ref[1]
    blocks, half, total_steps = _steps(info_ref, rows, wide)

    def flip(c, carry):
        at = pl.multiple_of(c * size, size)
        kt_ref[:, pl.ds(at, size)] = _transposed(k_ref[pl.ds(at, size), :], jnp.bfloat16)
        dk_ref[pl.ds(at, size), :] = jnp.zeros((size, lanes), jnp.float32)
        dv_ref[pl.ds(at, size), :] = jnp.zeros((size, lanes), jnp.float32)
        return carry

    lax.fori_loop(0, slots // size, flip, 0)

    def step(i, carry):
        second = i >= blocks
        block = jnp.where(second, half * part + i - blocks, i)
        at = pl.multiple_of(block * wide, wide)
        mine = _masked_rows(second, (lanes, wide), 0)
        mine_lanes = _masked_rows(second, (wide, lanes), 1)
        q_plain = q_ref[pl.ds(at, wide), :].astype(jnp.float32)
        q_rows = jnp.where(mine_lanes, q_plain, 0.0).astype(jnp.bfloat16)
        q_cols = jnp.where(mine, jnp.transpose(q_plain), 0.0).astype(jnp.bfloat16)
        dmix = jnp.where(mine, jnp.transpose(dmix_ref[pl.ds(at, wide), :].astype(jnp.float32)), 0.0)
        stats = stat_ref[:, pl.ds(at, wide)]
        top = jnp.where(second, stats[2:3, :], stats[0:1, :])
        total = jnp.where(second, stats[3:4, :], stats[1:2, :])
        dn_wide = dmix / total
        dn_cols = dn_wide.astype(jnp.bfloat16)
        dn_rows = jnp.transpose(dn_wide).astype(jnp.bfloat16)
        mixed = mix_ref[:, pl.ds(at, wide)]
        dtotal = -jnp.sum(dmix * mixed, axis=0, keepdims=True) / total
        dtotal = dtotal.astype(jnp.bfloat16).astype(jnp.float32)
        chunks = _chunk_count(count, block, wide, size, causal)

        def one(c, dq):
            spot = pl.multiple_of(c * size, size)
            s = jnp.dot(k_ref[pl.ds(spot, size), :], q_cols, preferred_element_type=jnp.float32)
            s = jnp.where(_score_mask(c, size, block, count, wide, causal), s, NEGATIVE)
            e = jnp.exp(s - top)
            through = jnp.dot(v_ref[pl.ds(spot, size), :], dn_cols, preferred_element_type=jnp.float32)
            ds = (e * (through + dtotal)).astype(jnp.bfloat16)
            dv_ref[pl.ds(spot, size), :] = dv_ref[pl.ds(spot, size), :] + jnp.dot(
                e.astype(jnp.bfloat16), dn_rows, preferred_element_type=jnp.float32
            )
            dk_ref[pl.ds(spot, size), :] = dk_ref[pl.ds(spot, size), :] + jnp.dot(
                ds, q_rows, preferred_element_type=jnp.float32
            )
            return dq + jnp.dot(kt_ref[:, pl.ds(spot, size)], ds, preferred_element_type=jnp.float32)

        dq = lax.fori_loop(0, chunks, one, jnp.zeros((lanes, wide), jnp.float32))
        back = jnp.transpose(jnp.where(mine, dq, 0.0))

        @pl.when(jnp.logical_not(second))
        def _():
            dq_ref[pl.ds(at, wide), :] = back

        @pl.when(second)
        def _():
            dq_ref[pl.ds(at, wide), :] = dq_ref[pl.ds(at, wide), :] + back

        return carry

    lax.fori_loop(0, total_steps, step, 0)
    shift = lanes if packed else 0
    if packed:
        out_ref[:, 0:lanes] = dq_ref[...].astype(jnp.bfloat16)
    else:
        dqo_ref[...] = dq_ref[...].astype(jnp.bfloat16)

    def emit(c, carry):
        at = pl.multiple_of(c * size, size)
        out_ref[pl.ds(at, size), shift : shift + lanes] = dk_ref[pl.ds(at, size), :].astype(jnp.bfloat16)
        out_ref[pl.ds(at, size), shift + lanes : shift + 2 * lanes] = dv_ref[pl.ds(at, size), :].astype(
            jnp.bfloat16
        )
        return carry

    lax.fori_loop(0, slots // size, emit, 0)


def attention(info, parts, causal):
    lanes = 2 * HEAD_DIM
    rows = parts[0].shape[0]
    slots = parts[-1].shape[0]
    wide = min(256, rows // 2)
    size = min(256 if causal else 512, slots)
    work = rows * slots * lanes * (2 if causal else 4)
    return pl.pallas_call(
        functools.partial(attend_kernel, wide, size, causal, len(parts) == 1),
        name="attend_self" if causal else "attend_cross",
        out_shape=(
            jax.ShapeDtypeStruct((rows, lanes), jnp.bfloat16),
            jax.ShapeDtypeStruct((lanes, rows), jnp.float32),
            jax.ShapeDtypeStruct((8, rows), jnp.float32),
        ),
        in_specs=[pl.BlockSpec(memory_space=pltpu.SMEM)]
        + [pl.BlockSpec(memory_space=pltpu.VMEM)] * len(parts),
        out_specs=(pl.BlockSpec(memory_space=pltpu.VMEM),) * 3,
        scratch_shapes=[
            pltpu.VMEM((lanes, slots), jnp.bfloat16),
            pltpu.VMEM((slots, wide), jnp.float32),
        ],
        compiler_params=pltpu.CompilerParams(vmem_limit_bytes=32 * 1024 * 1024),
        cost_estimate=pl.CostEstimate(flops=work, bytes_accessed=slots * lanes * 8, transcendentals=rows * slots),
    )(info, *parts)


def attention_back(info, parts, dmix, mixed, stats, causal):
    lanes = 2 * HEAD_DIM
    rows = parts[0].shape[0]
    slots = parts[-1].shape[0]
    wide = min(256, rows // 2)
    size = min(256 if causal else 512, slots)
    work = rows * slots * lanes * (5 if causal else 10)
    packed = len(parts) == 1
    outs = (jax.ShapeDtypeStruct((slots, (3 if packed else 2) * lanes), jnp.bfloat16),)
    if not packed:
        outs = (jax.ShapeDtypeStruct((rows, lanes), jnp.bfloat16),) + outs
    return pl.pallas_call(
        functools.partial(attend_back_kernel, wide, size, causal, packed),
        name="attend_self_back" if causal else "attend_cross_back",
        out_shape=outs,
        in_specs=[pl.BlockSpec(memory_space=pltpu.SMEM)]
        + [pl.BlockSpec(memory_space=pltpu.VMEM)] * (len(parts) + 3),
        out_specs=(pl.BlockSpec(memory_space=pltpu.VMEM),) * len(outs),
        scratch_shapes=[
            pltpu.VMEM((lanes, slots), jnp.bfloat16),
            pltpu.VMEM((slots, lanes), jnp.float32),
            pltpu.VMEM((slots, lanes), jnp.float32),
            pltpu.VMEM((rows, lanes), jnp.float32),
        ],
        compiler_params=pltpu.CompilerParams(vmem_limit_bytes=40 * 1024 * 1024),
        cost_estimate=pl.CostEstimate(flops=work, bytes_accessed=slots * lanes * 8, transcendentals=rows * slots),
    )(info, *parts, dmix, mixed, stats)


def spread_heads(array):
    d = HEAD_DIM
    pick = lambda h: array[..., h * d : (h + 1) * d]
    return jnp.stack(
        [jnp.concatenate([pick(a), pick(b)], axis=-1) for a, b in ((0, 1), (2, 1), (3, 4), (5, 4))]
    )


def merge_heads(array):
    d = HEAD_DIM
    wide = array.astype(jnp.float32)
    first = [wide[j, ..., :d] for j in range(4)]
    shared = [wide[j, ..., d:] + wide[j + 1, ..., d:] for j in (0, 2)]
    return jnp.concatenate(
        [first[0], shared[0], first[1], first[2], shared[1], first[3]], axis=-1
    ).astype(jnp.bfloat16)


def by_document(array, x_rank, swap):
    own = lax.dynamic_index_in_dim(array, x_rank, 0, False)
    other = lax.ppermute(lax.dynamic_index_in_dim(array, 1 - x_rank, 0, False), "seq", swap)
    first = x_rank == 0
    return jnp.concatenate([jnp.where(first, own, other), jnp.where(first, other, own)], axis=0)


def by_position(array, x_rank, swap):
    pair = array.reshape((2, array.shape[0] // 2) + array.shape[1:])
    own = lax.dynamic_index_in_dim(pair, x_rank, 0, False)
    other = lax.ppermute(lax.dynamic_index_in_dim(pair, 1 - x_rank, 0, False), "seq", swap)
    first = x_rank == 0
    return jnp.stack([jnp.where(first, own, other), jnp.where(first, other, own)])


def send_z(array, z_rank, shifts):
    count = array.shape[0]
    return [
        lax.ppermute(lax.dynamic_index_in_dim(array, (z_rank + k) % count, 0, False), "seq", shifts[k])
        for k in range(1, count)
    ]


def place_z(array, arrived, z_rank):
    count = array.shape[0]
    out = array
    for k in range(1, count):
        out = lax.dynamic_update_index_in_dim(out, arrived[k - 1], (z_rank - k) % count, 0)
    return out


def exchange_z(array, z_rank, shifts):
    return place_z(array, send_z(array, z_rank, shifts), z_rank)


def add_z(array, z_rank, shifts):
    total = lax.dynamic_index_in_dim(array, z_rank, 0, False).astype(jnp.float32)
    for arrived in send_z(array, z_rank, shifts):
        total = total + arrived.astype(jnp.float32)
    return total


def add_x(array, x_rank, swap):
    keep = lax.dynamic_index_in_dim(array, x_rank, 1, False).astype(jnp.float32)
    send = lax.dynamic_index_in_dim(array, 1 - x_rank, 1, False)
    return (keep + lax.ppermute(send, "seq", swap).astype(jnp.float32)).astype(jnp.bfloat16)


def gather_doc(array, pairs_core, pairs_y):
    across = lax.ppermute(array, "doc", pairs_y)
    beside = lax.ppermute(array, "doc", pairs_core)
    far = lax.ppermute(across, "doc", pairs_core)
    return jnp.concatenate([array, beside], axis=0), jnp.concatenate([across, far], axis=0)


def add_core(array, pairs_core):
    n = array.shape[0] // 2
    return array[:n] + lax.ppermute(array[n:].astype(jnp.bfloat16), "doc", pairs_core).astype(jnp.float32)


def relative_doc(array, core_rank, y_rank):
    a, b, c, d = (array[..., i, :] for i in range(4))
    even = core_rank == 0
    a, b, c, d = (jnp.where(even, a, b), jnp.where(even, b, a), jnp.where(even, c, d), jnp.where(even, d, c))
    low = y_rank == 0
    return [jnp.where(low, a, c), jnp.where(low, b, d), jnp.where(low, c, a), jnp.where(low, d, b)]


def by_heads(
    dec_in,
    enc_in,
    tgt_len,
    enc_len,
    self_qkv,
    self_out,
    cross_q,
    cross_kv,
    cross_out,
    ff_in,
    ff_out,
    gains,
    cotangent,
):
    f32, bf16 = jnp.float32, jnp.bfloat16
    tie = lax.optimization_barrier
    docs_here, rows_doc, width = dec_in.shape
    slots_doc = enc_in.shape[1]
    doc_ranks, seq_ranks = lax.axis_size("doc"), lax.axis_size("seq")
    seq_rank, doc_rank = lax.axis_index("seq"), lax.axis_index("doc")
    z_rank, x_rank = seq_rank // 2, seq_rank % 2
    y_rank, core_rank = doc_rank // 2, doc_rank % 2
    swap = [(i, i ^ 1) for i in range(seq_ranks)]
    shifts = [[(i, (i + 2 * k) % seq_ranks) for i in range(seq_ranks)] for k in range(seq_ranks // 2)]
    pairs_core = [(i, i ^ 1) for i in range(doc_ranks)]
    pairs_y = [(i, i ^ 2) for i in range(doc_ranks)]
    inner = HEADS * HEAD_DIM
    lanes = 2 * HEAD_DIM
    share = inner // doc_ranks
    depth = width // seq_ranks
    rows = docs_here * rows_doc
    slots = docs_here * slots_doc

    small = jnp.concatenate(
        [self_qkv[0], self_qkv[1], self_qkv[2], cross_q, cross_kv[0], cross_kv[1], self_out.T, cross_out.T],
        axis=1,
    )
    every = lax.all_gather(small, ("doc", "seq"), axis=0, tiled=True)
    ff_mine = jnp.concatenate([ff_in[0], ff_in[1], ff_out.T], axis=1)
    ff_all = lax.all_gather(ff_mine, "seq", axis=0, tiled=True)
    hidden_here = ff_in.shape[2]

    gain_other = lax.ppermute(gains, "seq", swap)
    gain_pair = jnp.where(x_rank == 0, jnp.stack([gains, gain_other]), jnp.stack([gain_other, gains]))
    gain_all = jnp.broadcast_to(gain_pair, (seq_ranks // 2,) + gain_pair.shape)
    gain_all = exchange_z(gain_all, z_rank, shifts)
    gain_all = gain_all.transpose(2, 0, 1, 3).reshape(3, width).astype(f32)

    def project(rows_in, weight, parts):
        out = jnp.einsum("td,edk->etk", rows_in, weight, preferred_element_type=f32).astype(bf16)
        return [
            jnp.concatenate([out[e, :, i * share : (i + 1) * share] for e in range(doc_ranks)], axis=-1)
            for i in range(parts)
        ]

    def lift(inner_in, weight):
        split = inner_in.reshape(inner_in.shape[0], doc_ranks, share)
        return jnp.einsum("tek,edk->td", split, weight, preferred_element_type=f32)

    def outer(inner_in, rows_in):
        parts = relative_doc(inner_in.reshape(inner_in.shape[0], doc_ranks, share), core_rank, y_rank)
        every_part = jnp.concatenate(parts, axis=-1)
        return matmul_outer(every_part, rows_in).astype(bf16).reshape(doc_ranks, share, width)

    info_self = jnp.stack([lax.dynamic_index_in_dim(tgt_len, x_rank, 0, False), z_rank % 2])
    info_cross = jnp.stack([lax.dynamic_index_in_dim(enc_len, x_rank, 0, False), z_rank % 2])

    stream = by_document(dec_in, x_rank, swap).astype(f32)
    cot = by_document(cotangent, x_rank, swap)
    normed1, inverse1 = norm_parts(stream, gain_all[0])
    normed1 = normed1.astype(bf16)
    cot_near, cot_far = gather_doc(cot, pairs_core, pairs_y)
    n1_near, n1_far = gather_doc(normed1, pairs_core, pairs_y)
    every, normed1, cot_near, cot_far, n1_near, n1_far = tie(
        (every, normed1, cot_near, cot_far, n1_near, n1_far)
    )
    every = every.reshape(doc_ranks, width, 8 * share)
    w_qkv = every[:, :, : 3 * share]
    w_cq = every[:, :, 3 * share : 4 * share]
    w_ckv = every[:, :, 4 * share : 6 * share]
    w_so = every[:, :, 6 * share : 7 * share]
    w_co = every[:, :, 7 * share :]

    qkv = jnp.concatenate([spread_heads(p) for p in project(normed1, w_qkv, 3)], axis=-1)
    qkv_heads = exchange_z(qkv, z_rank, shifts).reshape(4 * rows, 3 * lanes)
    enc_rows = enc_in.reshape(slots, width)
    ckv = jnp.concatenate([spread_heads(p) for p in project(enc_rows, w_ckv, 2)], axis=-1)
    ckv = ckv.reshape(4, docs_here, slots_doc, 2 * lanes).transpose(1, 2, 0, 3)
    ckv = by_document(ckv, x_rank, swap).transpose(1, 0, 2)
    qkv_heads, ckv = tie((qkv_heads, ckv))
    ckv_arrived = send_z(ckv, z_rank, shifts)
    att1, mix1, stat1 = attention(info_self, (qkv_heads,), True)
    att1 = exchange_z(att1.reshape(4, rows, lanes), z_rank, shifts)
    att1, ckv_arrived[0] = tie((att1, ckv_arrived[0]))
    att1 = merge_heads(att1)
    stream1 = stream + lift(att1, w_so)
    normed2, inverse2 = norm_parts(stream1, gain_all[1])
    normed2 = normed2.astype(bf16)
    (cq,) = project(normed2, w_cq, 1)
    cq_heads = exchange_z(spread_heads(cq), z_rank, shifts).reshape(4 * rows, lanes)
    ckv_heads = place_z(ckv, ckv_arrived, z_rank).reshape(4 * slots, 2 * lanes)

    att2, mix2, stat2 = attention(info_cross, (cq_heads, ckv_heads), False)
    att2 = merge_heads(exchange_z(att2.reshape(4, rows, lanes), z_rank, shifts))
    stream2 = stream1 + lift(att2, w_co)
    normed3, inverse3 = norm_parts(stream2, gain_all[2])
    normed3 = normed3.astype(bf16)

    w_gate, w_up = ff_all[:, :hidden_here], ff_all[:, hidden_here : 2 * hidden_here]
    w_down = ff_all[:, 2 * hidden_here :]

    def inside(n3_rows, cot_rows):
        gate_pre = matmul_rows(n3_rows, w_gate)
        up_pre = matmul_rows(n3_rows, w_up)
        d_hidden = matmul_rows(cot_rows, w_down)
        hidden, gelu_pull = jax.vjp(
            lambda gate_val, up_val: jax.nn.gelu(gate_val, approximate=True) * up_val, gate_pre, up_pre
        )
        d_gate, d_up = gelu_pull(d_hidden)
        return hidden.astype(bf16), d_gate.astype(bf16), d_up.astype(bf16)

    def through(d_gate, d_up):
        return matmul_back(d_gate, w_gate) + matmul_back(d_up, w_up)

    n3_near, n3_far = gather_doc(normed3, pairs_core, pairs_y)
    hid_near, dg_near, du_near = inside(n3_near, cot_near)
    hid_near, n3_far = tie((hid_near, n3_far))
    hid_far, dg_far, du_far = inside(n3_far, cot_far)
    dn3_far = add_core(through(dg_far, du_far), pairs_core).astype(bf16)
    dn3_across = lax.ppermute(dn3_far, "doc", pairs_y)
    dn3_near = add_core(through(dg_near, du_near), pairs_core)
    n3_all = jnp.concatenate([n3_near, n3_far], axis=0)
    cot_all = jnp.concatenate([cot_near, cot_far], axis=0)
    d_gate = jnp.concatenate([dg_near, dg_far], axis=0)
    d_up = jnp.concatenate([du_near, du_far], axis=0)
    hidden = jnp.concatenate([hid_near, hid_far], axis=0)
    ff_grads = jnp.concatenate(
        [
            matmul_outer(n3_all, d_gate).astype(bf16),
            matmul_outer(n3_all, d_up).astype(bf16),
            matmul_outer(cot_all, hidden).astype(bf16),
        ],
        axis=1,
    )
    ff_sum = lax.psum_scatter(ff_grads, "seq", scatter_dimension=0, tiled=True)
    dn3_across, ff_grads = tie((dn3_across, ff_grads))
    d_normed3 = dn3_near + dn3_across.astype(f32)

    back_three, gain_grad3 = norm_back(stream2, inverse3, gain_all[2], d_normed3)
    d_stream2 = cot.astype(f32) + back_three
    d_branch2 = d_stream2.astype(bf16)
    (d_mix2,) = project(d_branch2, w_co, 1)
    d_mix2 = exchange_z(spread_heads(d_mix2), z_rank, shifts).reshape(4 * rows, lanes)
    d_mix2, hidden_late = tie((d_mix2, hidden))
    branch_far = add_core(matmul_back(hidden_late[2 * rows :], w_down), pairs_core).astype(bf16)
    branch_across = lax.ppermute(branch_far, "doc", pairs_y)
    branch = add_core(matmul_back(hidden_late[: 2 * rows], w_down), pairs_core)
    d_cq, d_ckv = attention_back(info_cross, (cq_heads, ckv_heads), d_mix2, mix2, stat2, False)
    d_ckv = d_ckv.reshape(4, slots, 2 * lanes)
    d_ckv_arrived = send_z(d_ckv, z_rank, shifts)
    d_cq = exchange_z(d_cq.reshape(4, rows, lanes), z_rank, shifts)
    d_cq, branch_across = tie((d_cq, branch_across))
    layer_out = by_position(stream2 + (branch + branch_across.astype(f32)), x_rank, swap)
    d_cq = merge_heads(d_cq)
    back_two, gain_grad2 = norm_back(stream1, inverse2, gain_all[1], lift(d_cq, w_cq))
    d_stream1 = d_stream2 + back_two
    d_branch1 = d_stream1.astype(bf16)
    (d_mix1,) = project(d_branch1, w_so, 1)
    d_mix1 = exchange_z(spread_heads(d_mix1), z_rank, shifts).reshape(4 * rows, lanes)
    d_mix1, layer_out, *d_ckv_arrived = tie((d_mix1, layer_out, *d_ckv_arrived))
    d_ckv = place_z(d_ckv, d_ckv_arrived, z_rank)
    d_stream1_out = by_position(d_stream1, x_rank, swap)
    (d_qkv,) = attention_back(info_self, (qkv_heads,), d_mix1, mix1, stat1, True)
    d_qkv = exchange_z(d_qkv.reshape(4, rows, 3 * lanes), z_rank, shifts)
    d_ckv = by_position(d_ckv.transpose(1, 0, 2), x_rank, swap)
    d_qkv, d_ckv, d_stream1_out = tie((d_qkv, d_ckv, d_stream1_out))
    d_q, d_k, d_v = (merge_heads(d_qkv[..., i * lanes : (i + 1) * lanes]) for i in range(3))

    by_doc = jnp.concatenate(
        [d.reshape(rows, doc_ranks, share) for d in (d_q, d_k, d_v)], axis=-1
    )
    own, beside, across, far = relative_doc(by_doc, core_rank, y_rank)
    arrived = lax.ppermute(jnp.stack([beside, far]), "doc", pairs_core)
    across = jnp.concatenate([across, arrived[1]], axis=0)
    d_near = jnp.concatenate([own, arrived[0]], axis=0)
    d_far = lax.ppermute(across, "doc", pairs_y)
    d_normed1 = (
        lift(d_q, w_qkv[:, :, :share])
        + lift(d_k, w_qkv[:, :, share : 2 * share])
        + lift(d_v, w_qkv[:, :, 2 * share :])
    )
    back_one, gain_grad1 = norm_back(stream, inverse1, gain_all[0], d_normed1)
    dec_grad = d_stream1_out + by_position(back_one.astype(bf16), x_rank, swap).astype(f32)

    d_ckv = d_ckv.reshape(slots, 4, 2 * lanes).transpose(1, 0, 2)
    d_ck, d_cv = (merge_heads(d_ckv[..., i * lanes : (i + 1) * lanes]) for i in range(2))
    enc_grad = lift(d_ck, w_ckv[:, :, :share]) + lift(d_cv, w_ckv[:, :, share:])
    enc_grad = enc_grad.reshape(docs_here, slots_doc, width)

    terms = jnp.concatenate(
        [
            outer(d_cq, normed2),
            outer(d_ck, enc_rows),
            outer(d_cv, enc_rows),
            outer(att1, d_branch1),
            outer(att2, d_branch2),
        ],
        axis=1,
    )
    arrived = lax.ppermute(jnp.stack([terms[1], terms[3]]), "doc", pairs_core).astype(f32)
    across = (terms[2].astype(f32) + arrived[1]).astype(bf16)
    terms = (terms[0].astype(f32) + arrived[0]) + lax.ppermute(across, "doc", pairs_y).astype(f32)
    terms = terms.astype(bf16).T.reshape(seq_ranks // 2, 2, depth, 5 * share)
    others = add_z(add_x(terms, x_rank, swap), z_rank, shifts)

    gain_terms = jnp.stack([gain_grad1, gain_grad2, gain_grad3])
    gain_terms = gain_terms + lax.ppermute(gain_terms, "doc", pairs_core)
    gain_terms = gain_terms + lax.ppermute(gain_terms, "doc", pairs_y)
    gain_terms = gain_terms.reshape(3, seq_ranks, depth).transpose(1, 0, 2)
    gain_terms = gain_terms.reshape(seq_ranks, 2, 3 * depth // 2).astype(bf16)
    gain_terms = jnp.pad(gain_terms, ((0, 0), (0, 6), (0, 3 * share - 3 * depth // 2)))
    grad_qkv = matmul_outer(n1_near, d_near) + matmul_outer(n1_far, d_far)
    grad_qkv = grad_qkv.astype(bf16).reshape(seq_ranks, depth, 3 * share)
    grad_qkv = jnp.concatenate([grad_qkv, gain_terms], axis=1)
    grad_qkv = grad_qkv.reshape(seq_ranks // 2, 2, depth + 8, 3 * share)
    summed = add_z(add_x(grad_qkv, x_rank, swap), z_rank, shifts)
    grad_gains = summed[depth : depth + 2, : 3 * depth // 2].reshape(3, depth)
    piece = lambda a, i: a[:depth, i * share : (i + 1) * share]
    ff_sum = ff_sum.astype(f32)
    return (
        layer_out,
        dec_grad,
        enc_grad,
        jnp.stack([piece(summed, 0), piece(summed, 1), piece(summed, 2)]),
        piece(others, 3).T,
        piece(others, 0),
        jnp.stack([piece(others, 1), piece(others, 2)]),
        piece(others, 4).T,
        jnp.stack([ff_sum[:, :hidden_here], ff_sum[:, hidden_here : 2 * hidden_here]]),
        ff_sum[:, 2 * hidden_here :].T,
        grad_gains,
    )


def fits_by_heads(doc_ranks, seq_ranks, docs):
    return doc_ranks == 4 and seq_ranks == 8 and docs == 8


def solution(mesh):
    def either(dec_in, *others):
        docs = dec_in.shape[0] * mesh.shape["doc"]
        if fits_by_heads(mesh.shape["doc"], mesh.shape["seq"], docs):
            return by_heads(dec_in, *others)
        return per_device(dec_in, *others)

    return jax.shard_map(
        either,
        mesh=mesh,
        in_specs=(
            P("doc", "seq", None),
            P("doc", "seq", None),
            P("doc"),
            P("doc"),
            P(None, "seq", "doc"),
            P("doc", "seq"),
            P("seq", "doc"),
            P(None, "seq", "doc"),
            P("doc", "seq"),
            P(None, "seq", "doc"),
            P("doc", "seq"),
            P(None, "seq"),
            P("doc", "seq", None),
        ),
        out_specs=(
            P("doc", "seq", None),
            P("doc", "seq", None),
            P("doc", "seq", None),
            P(None, "seq", "doc"),
            P("doc", "seq"),
            P("seq", "doc"),
            P(None, "seq", "doc"),
            P("doc", "seq"),
            P(None, "seq", "doc"),
            P("doc", "seq"),
            P(None, "seq"),
        ),
        check_vma=False,
    )
```

```python
import functools

import jax
import jax.numpy as jnp
from jax import lax
from jax.experimental import pallas as pl
from jax.experimental.pallas import tpu as pltpu
from jax.sharding import PartitionSpec as P

HEADS = 6
HEAD_DIM = 64


EPSILON = 1e-06
NEGATIVE = -1e30


def norm_parts(values, gain_row):
    inverse = lax.rsqrt(jnp.mean(values * values, axis=-1, keepdims=True) + EPSILON)
    return (values * inverse * gain_row, inverse)


def norm_back(values, inverse, gain_row, upstream):
    weighted = upstream * gain_row
    inner_sum = jnp.mean(weighted * values, axis=-1, keepdims=True)
    lowered = weighted * inverse - values * (inverse * inverse * inverse) * inner_sum
    return (lowered, jnp.sum(upstream * values * inverse, axis=0))


def matmul_rows(left_op, right_op):
    return jnp.dot(left_op, right_op, preferred_element_type=jnp.float32)


def matmul_back(left_op, right_op):
    return lax.dot_general(
        left_op, right_op, (((1,), (1,)), ((), ())), preferred_element_type=jnp.float32
    )


def matmul_outer(left_op, right_op):
    return lax.dot_general(
        left_op, right_op, (((0,), (0,)), ((), ())), preferred_element_type=jnp.float32
    )


def head_scores(queries, keys_in, allowed):
    scores = jnp.einsum("bqhd,bkhd->bqhk", queries, keys_in, preferred_element_type=jnp.float32)
    return jnp.where(allowed[:, :, None, :], scores, NEGATIVE)


def weigh_values(raised, values_in):
    return jnp.einsum(
        "bqhk,bkhd->bqhd",
        raised.astype(jnp.bfloat16),
        values_in,
        preferred_element_type=jnp.float32,
    )


def mixed_grads(dmixed, numerator, totals):
    d_numer = (dmixed / totals[..., None]).astype(jnp.bfloat16)
    d_total = (-jnp.sum(dmixed * numerator, axis=-1) / (totals * totals)).astype(jnp.bfloat16)
    return (d_numer, d_total)


def score_grads(raised, d_numer, d_total, values_in):
    through = jnp.einsum("bqhd,bkhd->bqhk", d_numer, values_in, preferred_element_type=jnp.float32)
    return (raised * (through + d_total.astype(jnp.float32)[..., None])).astype(jnp.bfloat16)


def pair_grads(d_scores, raised, queries, keys_in, d_numer):
    d_query = jnp.einsum("bqhk,bkhd->bqhd", d_scores, keys_in, preferred_element_type=jnp.float32)
    d_keys = jnp.einsum("bqhk,bqhd->bkhd", d_scores, queries, preferred_element_type=jnp.float32)
    d_values = jnp.einsum(
        "bqhk,bqhd->bkhd", raised.astype(jnp.bfloat16), d_numer, preferred_element_type=jnp.float32
    )
    return (d_query, d_keys, d_values)


def block_size(docs_here):
    if docs_here % 4 == 0:
        return 4
    if docs_here % 2 == 0:
        return 2
    return 1


def feed_forward(rows_in, cot_in, w_in, w_out):
    gate_pre = matmul_rows(rows_in, w_in[0])
    up_pre = matmul_rows(rows_in, w_in[1])
    hidden = (jax.nn.gelu(gate_pre, approximate=True) * up_pre).astype(jnp.bfloat16)
    branch = matmul_rows(hidden, w_out)
    grad_out = matmul_outer(hidden, cot_in)
    d_hidden = matmul_back(cot_in, w_out)
    unused, gelu_pull = jax.vjp(
        lambda gate_val, up_val: jax.nn.gelu(gate_val, approximate=True) * up_val, gate_pre, up_pre
    )
    d_gate, d_up = gelu_pull(d_hidden)
    d_gate_up = jnp.stack([d_gate, d_up]).astype(jnp.bfloat16)
    grad_in = jnp.einsum("td,ctf->cdf", rows_in, d_gate_up, preferred_element_type=jnp.float32)
    d_rows = jnp.einsum("ctf,cdf->td", d_gate_up, w_in, preferred_element_type=jnp.float32)
    return (branch, grad_in, grad_out, d_rows)


def per_device(
    dec_in,
    enc_in,
    tgt_len,
    enc_len,
    self_qkv,
    self_out,
    cross_q,
    cross_kv,
    cross_out,
    ff_in,
    ff_out,
    gains,
    cotangent,
):
    by_rows = (
        lax.all_gather(self_qkv, "seq", axis=1, tiled=True),
        lax.all_gather(self_out, "seq", axis=1, tiled=True),
        lax.all_gather(cross_q, "seq", axis=0, tiled=True),
        lax.all_gather(cross_kv, "seq", axis=1, tiled=True),
        lax.all_gather(cross_out, "seq", axis=1, tiled=True),
        lax.all_gather(ff_in, "seq", axis=1, tiled=True),
        lax.all_gather(ff_out, "seq", axis=1, tiled=True),
        lax.all_gather(gains, "seq", axis=1, tiled=True),
    )
    w_qkv, w_so, w_cq, w_ckv, w_co, w_in, w_out = (
        lax.all_gather(by_rows[0], "doc", axis=2, tiled=True),
        lax.all_gather(by_rows[1], "doc", axis=0, tiled=True),
        lax.all_gather(by_rows[2], "doc", axis=1, tiled=True),
        lax.all_gather(by_rows[3], "doc", axis=2, tiled=True),
        lax.all_gather(by_rows[4], "doc", axis=0, tiled=True),
        lax.all_gather(by_rows[5], "doc", axis=2, tiled=True),
        lax.all_gather(by_rows[6], "doc", axis=0, tiled=True),
    )
    gain_all = by_rows[7].astype(jnp.float32)
    docs_here, rows_doc, model_width = dec_in.shape
    slot_count = enc_in.shape[1]
    seq_ranks = lax.axis_size("seq")
    my_rank = lax.axis_index("seq")
    length = rows_doc * seq_ranks
    inner_width = HEADS * HEAD_DIM
    rows_all = docs_here * rows_doc
    stream = dec_in.reshape(rows_all, model_width).astype(jnp.float32)
    normed1, inverse1 = norm_parts(stream, gain_all[0])
    normed1 = normed1.astype(jnp.bfloat16)
    proj_qkv = jnp.einsum("td,cdk->ctk", normed1, w_qkv, preferred_element_type=jnp.float32).astype(
        jnp.bfloat16
    )
    self_query = proj_qkv[0].reshape(docs_here, rows_doc, HEADS, HEAD_DIM)
    keys_all, values_all = (
        lax.all_gather(
            proj_qkv[1].reshape(docs_here, rows_doc, inner_width), "seq", axis=1, tiled=True
        ),
        lax.all_gather(
            proj_qkv[2].reshape(docs_here, rows_doc, inner_width), "seq", axis=1, tiled=True
        ),
    )
    keys_all = keys_all.reshape(docs_here, length, HEADS, HEAD_DIM)
    values_all = values_all.reshape(docs_here, length, HEADS, HEAD_DIM)
    query_pos = my_rank * rows_doc + jnp.arange(rows_doc, dtype=jnp.int32)
    key_pos = jnp.arange(length, dtype=jnp.int32)
    self_allowed = (key_pos[None, None, :] <= query_pos[None, :, None]) & (
        key_pos[None, None, :] < tgt_len[:, None, None]
    )
    self_scores = head_scores(self_query, keys_all, self_allowed)
    self_top = jnp.max(self_scores, axis=-1)
    self_raised = jnp.exp(self_scores - self_top[..., None])
    self_total = jnp.sum(self_raised, axis=-1)
    self_numer = weigh_values(self_raised, values_all)
    self_mixed = (
        (self_numer / self_total[..., None]).astype(jnp.bfloat16).reshape(rows_all, inner_width)
    )
    stream1 = stream + matmul_rows(self_mixed, w_so)
    normed2, inverse2 = norm_parts(stream1, gain_all[1])
    normed2 = normed2.astype(jnp.bfloat16)
    cross_query = (
        matmul_rows(normed2, w_cq).astype(jnp.bfloat16).reshape(docs_here, rows_doc, inner_width)
    )
    enc_proj = jnp.einsum(
        "bsd,cdk->cbsk", enc_in, w_ckv, preferred_element_type=jnp.float32
    ).astype(jnp.bfloat16)
    queries_all = lax.all_gather(cross_query, "seq", axis=1, tiled=True)
    per_block = block_size(docs_here)
    block_count = docs_here // per_block

    def split_docs(array):
        return array.reshape((block_count, per_block) + array.shape[1:])

    block_queries = split_docs(queries_all.reshape(docs_here, length, HEADS, HEAD_DIM))
    block_keys = split_docs(enc_proj[0].reshape(docs_here, slot_count, HEADS, HEAD_DIM))
    block_values = split_docs(enc_proj[1].reshape(docs_here, slot_count, HEADS, HEAD_DIM))
    slot_pos = my_rank * slot_count + jnp.arange(slot_count, dtype=jnp.int32)
    slot_live = split_docs(slot_pos[None, :] < enc_len[:, None])

    def cross_scores(queries, keys_in, slot_alive):
        allowed = jnp.broadcast_to(
            slot_alive[:, None, :], (slot_alive.shape[0], queries.shape[1], slot_alive.shape[1])
        )
        return head_scores(queries, keys_in, allowed)

    def local_peak(bundle):
        return jnp.max(cross_scores(bundle[0], bundle[1], bundle[2]), axis=-1)

    local_top = lax.map(local_peak, (block_queries, block_keys, slot_live))
    cross_top = lax.pmax(local_top.reshape(docs_here, length, HEADS), "seq")
    block_top = split_docs(cross_top)

    def cross_partial(bundle):
        queries, keys_in, values_in, slot_alive, peak_row = bundle
        raised = jnp.exp(cross_scores(queries, keys_in, slot_alive) - peak_row[..., None])
        return (weigh_values(raised, values_in), jnp.sum(raised, axis=-1))

    part_numer, part_total = lax.map(
        cross_partial, (block_queries, block_keys, block_values, slot_live, block_top)
    )
    cross_numer, cross_total = (
        lax.psum_scatter(
            part_numer.reshape(docs_here, length, inner_width),
            "seq",
            scatter_dimension=1,
            tiled=True,
        ),
        lax.psum_scatter(
            part_total.reshape(docs_here, length, HEADS), "seq", scatter_dimension=1, tiled=True
        ),
    )
    cross_numer = cross_numer.reshape(docs_here, rows_doc, HEADS, HEAD_DIM)
    cross_mixed = (
        (cross_numer / cross_total[..., None]).astype(jnp.bfloat16).reshape(rows_all, inner_width)
    )
    stream2 = stream1 + matmul_rows(cross_mixed, w_co)
    normed3, inverse3 = norm_parts(stream2, gain_all[2])
    normed3 = normed3.astype(jnp.bfloat16)
    cot_rows = cotangent.reshape(rows_all, model_width)
    ff_branch, grad_in, grad_out, d_normed3 = feed_forward(normed3, cot_rows, w_in, w_out)
    layer_out = (stream2 + ff_branch).reshape(docs_here, rows_doc, model_width)
    back_three, gain_grad3 = norm_back(stream2, inverse3, gain_all[2], d_normed3)
    d_stream2 = cot_rows.astype(jnp.float32) + back_three
    d_branch2 = d_stream2.astype(jnp.bfloat16)
    grad_co = matmul_outer(cross_mixed, d_branch2)
    d_mixed2 = matmul_back(d_branch2, w_co).reshape(docs_here, rows_doc, HEADS, HEAD_DIM)
    d_numer2, d_total2 = mixed_grads(d_mixed2, cross_numer, cross_total)
    numer_back, total_back = (
        lax.all_gather(
            d_numer2.reshape(docs_here, rows_doc, inner_width), "seq", axis=1, tiled=True
        ),
        lax.all_gather(d_total2, "seq", axis=1, tiled=True),
    )

    def cross_back_block(bundle):
        queries, keys_in, values_in, slot_alive, peak_row, d_numer, d_total = bundle
        raised = jnp.exp(cross_scores(queries, keys_in, slot_alive) - peak_row[..., None])
        d_scores = score_grads(raised, d_numer, d_total, values_in)
        return pair_grads(d_scores, raised, queries, keys_in, d_numer)

    part_dq, part_dk, part_dv = lax.map(
        cross_back_block,
        (
            block_queries,
            block_keys,
            block_values,
            slot_live,
            block_top,
            split_docs(numer_back.reshape(docs_here, length, HEADS, HEAD_DIM)),
            split_docs(total_back),
        ),
    )
    d_cross_q = lax.psum_scatter(
        part_dq.reshape(docs_here, length, inner_width), "seq", scatter_dimension=1, tiled=True
    )
    d_cross_q = d_cross_q.astype(jnp.bfloat16).reshape(rows_all, inner_width)
    d_enc_proj = jnp.stack(
        [
            part_dk.reshape(docs_here, slot_count, inner_width),
            part_dv.reshape(docs_here, slot_count, inner_width),
        ]
    ).astype(jnp.bfloat16)
    grad_cq = matmul_outer(normed2, d_cross_q)
    grad_ckv = jnp.einsum("bsd,cbsk->cdk", enc_in, d_enc_proj, preferred_element_type=jnp.float32)
    enc_grad = jnp.einsum("cbsk,cdk->bsd", d_enc_proj, w_ckv, preferred_element_type=jnp.float32)
    back_two, gain_grad2 = norm_back(stream1, inverse2, gain_all[1], matmul_back(d_cross_q, w_cq))
    d_stream1 = d_stream2 + back_two
    d_branch1 = d_stream1.astype(jnp.bfloat16)
    grad_so = matmul_outer(self_mixed, d_branch1)
    d_mixed1 = matmul_back(d_branch1, w_so).reshape(docs_here, rows_doc, HEADS, HEAD_DIM)
    d_numer1, d_total1 = mixed_grads(d_mixed1, self_numer, self_total)
    again_raised = jnp.exp(head_scores(self_query, keys_all, self_allowed) - self_top[..., None])
    d_scores1 = score_grads(again_raised, d_numer1, d_total1, values_all)
    d_query1, part_dk1, part_dv1 = pair_grads(
        d_scores1, again_raised, self_query, keys_all, d_numer1
    )
    d_keys1, d_values1 = (
        lax.psum_scatter(
            part_dk1.reshape(docs_here, length, inner_width), "seq", scatter_dimension=1, tiled=True
        ),
        lax.psum_scatter(
            part_dv1.reshape(docs_here, length, inner_width), "seq", scatter_dimension=1, tiled=True
        ),
    )
    d_qkv = jnp.stack(
        [
            d_query1.reshape(rows_all, inner_width),
            d_keys1.reshape(rows_all, inner_width),
            d_values1.reshape(rows_all, inner_width),
        ]
    ).astype(jnp.bfloat16)
    grad_qkv = jnp.einsum("td,ctk->cdk", normed1, d_qkv, preferred_element_type=jnp.float32)
    d_normed1 = jnp.einsum("ctk,cdk->td", d_qkv, w_qkv, preferred_element_type=jnp.float32)
    back_one, gain_grad1 = norm_back(stream, inverse1, gain_all[0], d_normed1)
    dec_grad = (d_stream1 + back_one).reshape(docs_here, rows_doc, model_width)
    gain_sum = lax.psum(jnp.stack([gain_grad1, gain_grad2, gain_grad3]), ("doc", "seq"))
    share_len = model_width // seq_ranks
    grad_gains = lax.dynamic_slice_in_dim(gain_sum, my_rank * share_len, share_len, 1)
    halfway = (
        lax.psum_scatter(grad_qkv, "doc", scatter_dimension=2, tiled=True),
        lax.psum_scatter(grad_so, "doc", scatter_dimension=0, tiled=True),
        lax.psum_scatter(grad_cq, "doc", scatter_dimension=1, tiled=True),
        lax.psum_scatter(grad_ckv, "doc", scatter_dimension=2, tiled=True),
        lax.psum_scatter(grad_co, "doc", scatter_dimension=0, tiled=True),
        lax.psum_scatter(grad_in, "doc", scatter_dimension=2, tiled=True),
        lax.psum_scatter(grad_out, "doc", scatter_dimension=0, tiled=True),
    )
    reduced = (
        lax.psum_scatter(halfway[0], "seq", scatter_dimension=1, tiled=True),
        lax.psum_scatter(halfway[1], "seq", scatter_dimension=1, tiled=True),
        lax.psum_scatter(halfway[2], "seq", scatter_dimension=0, tiled=True),
        lax.psum_scatter(halfway[3], "seq", scatter_dimension=1, tiled=True),
        lax.psum_scatter(halfway[4], "seq", scatter_dimension=1, tiled=True),
        lax.psum_scatter(halfway[5], "seq", scatter_dimension=1, tiled=True),
        lax.psum_scatter(halfway[6], "seq", scatter_dimension=1, tiled=True),
    )
    return (
        layer_out,
        dec_grad,
        enc_grad,
        reduced[0],
        reduced[1],
        reduced[2],
        reduced[3],
        reduced[4],
        reduced[5],
        reduced[6],
        grad_gains,
    )


def _masked_rows(is_second, shape, axis):
    index = lax.broadcasted_iota(jnp.int32, shape, axis)
    return (index >= HEAD_DIM) == is_second


def _transposed(array, dtype):
    return jnp.transpose(array.astype(jnp.float32)).astype(dtype)


def _score_mask(chunk, size, block, count, width, causal):
    slot = chunk * size + lax.broadcasted_iota(jnp.int32, (size, width), 0)
    live = slot < count
    if causal:
        query = block * width + lax.broadcasted_iota(jnp.int32, (size, width), 1)
        live = live & (slot <= query)
    return live


def _steps(info_ref, rows, wide):
    blocks = rows // wide
    half = blocks // 2
    return blocks, half, blocks + half


def _chunk_count(count, block, wide, size, causal):
    chunks = (count + size - 1) // size
    if causal:
        chunks = jnp.minimum(chunks, ((block + 1) * wide + size - 1) // size)
    return chunks


def _full_count(count, block, wide, size, causal):
    chunks = count // size
    if causal:
        chunks = jnp.minimum(chunks, block * wide // size)
    return chunks


def attend_kernel(wide, size, causal, packed, info_ref, *refs):
    if packed:
        qkv_ref, att_ref, mix_ref, stat_ref, vt_ref, score_ref = refs
        lanes = 2 * HEAD_DIM
        q_ref, k_ref, v_ref = (qkv_ref.at[:, pl.ds(i * lanes, lanes)] for i in range(3))
    else:
        q_ref, kv_ref, att_ref, mix_ref, stat_ref, vt_ref, score_ref = refs
        lanes = 2 * HEAD_DIM
        k_ref, v_ref = (kv_ref.at[:, pl.ds(i * lanes, lanes)] for i in range(2))
    rows = q_ref.shape[0]
    slots = k_ref.shape[0]
    count = info_ref[0]
    part = info_ref[1]
    blocks, half, total_steps = _steps(info_ref, rows, wide)

    def flip(c, carry):
        at = pl.multiple_of(c * size, size)
        vt_ref[:, pl.ds(at, size)] = _transposed(v_ref[pl.ds(at, size), :], jnp.bfloat16)
        return carry

    lax.fori_loop(0, slots // size, flip, 0)

    def step(i, carry):
        second = i >= blocks
        block = jnp.where(second, half * part + i - blocks, i)
        at = pl.multiple_of(block * wide, wide)
        mine = _masked_rows(second, (lanes, wide), 0)
        queries = jnp.where(mine, jnp.transpose(q_ref[pl.ds(at, wide), :].astype(jnp.float32)), 0.0)
        queries = queries.astype(jnp.bfloat16)
        chunks = _chunk_count(count, block, wide, size, causal)

        full = _full_count(count, block, wide, size, causal)

        def scores(masked, c, top):
            spot = pl.multiple_of(c * size, size)
            s = jnp.dot(k_ref[pl.ds(spot, size), :], queries, preferred_element_type=jnp.float32)
            if masked:
                s = jnp.where(_score_mask(c, size, block, count, wide, causal), s, NEGATIVE)
            score_ref[pl.ds(spot, size), :] = s
            return jnp.maximum(top, jnp.max(s.reshape(size // 8, 8, wide), axis=0))

        top = jnp.full((8, wide), NEGATIVE, jnp.float32)
        top = lax.fori_loop(0, full, functools.partial(scores, False), top)
        top = lax.fori_loop(full, chunks, functools.partial(scores, True), top)
        top = jnp.max(top, axis=0, keepdims=True)

        def weigh(c, carry):
            total, numer = carry
            spot = pl.multiple_of(c * size, size)
            e = jnp.exp(score_ref[pl.ds(spot, size), :] - top)
            total = total + jnp.sum(e.reshape(size // 8, 8, wide), axis=0)
            numer = numer + jnp.dot(
                vt_ref[:, pl.ds(spot, size)], e.astype(jnp.bfloat16), preferred_element_type=jnp.float32
            )
            return total, numer

        total, numer = lax.fori_loop(
            0,
            chunks,
            weigh,
            (jnp.zeros((8, wide), jnp.float32), jnp.zeros((lanes, wide), jnp.float32)),
        )
        total = jnp.sum(total, axis=0, keepdims=True)
        mixed = jnp.where(mine, numer / total, 0.0)
        back = jnp.transpose(mixed)

        @pl.when(jnp.logical_not(second))
        def _():
            att_ref[pl.ds(at, wide), :] = back.astype(jnp.bfloat16)
            mix_ref[:, pl.ds(at, wide)] = mixed
            stat_ref[0:1, pl.ds(at, wide)] = top
            stat_ref[1:2, pl.ds(at, wide)] = total

        @pl.when(second)
        def _():
            kept = att_ref[pl.ds(at, wide), :].astype(jnp.float32)
            att_ref[pl.ds(at, wide), :] = (kept + back).astype(jnp.bfloat16)
            mix_ref[:, pl.ds(at, wide)] = mix_ref[:, pl.ds(at, wide)] + mixed
            stat_ref[2:3, pl.ds(at, wide)] = top
            stat_ref[3:4, pl.ds(at, wide)] = total

        return carry

    lax.fori_loop(0, total_steps, step, 0)


def attend_back_kernel(wide, size, causal, packed, info_ref, *refs):
    lanes = 2 * HEAD_DIM
    if packed:
        qkv_ref, dmix_ref, mix_ref, stat_ref, out_ref, kt_ref, dk_ref, dv_ref, dq_ref = refs
        q_ref, k_ref, v_ref = (qkv_ref.at[:, pl.ds(i * lanes, lanes)] for i in range(3))
    else:
        q_ref, kv_ref, dmix_ref, mix_ref, stat_ref, dqo_ref, out_ref, kt_ref, dk_ref, dv_ref, dq_ref = refs
        k_ref, v_ref = (kv_ref.at[:, pl.ds(i * lanes, lanes)] for i in range(2))
    rows = q_ref.shape[0]
    slots = k_ref.shape[0]
    count = info_ref[0]
    part = info_ref[1]
    blocks, half, total_steps = _steps(info_ref, rows, wide)

    def flip(c, carry):
        at = pl.multiple_of(c * size, size)
        kt_ref[:, pl.ds(at, size)] = _transposed(k_ref[pl.ds(at, size), :], jnp.bfloat16)
        dk_ref[pl.ds(at, size), :] = jnp.zeros((size, lanes), jnp.float32)
        dv_ref[pl.ds(at, size), :] = jnp.zeros((size, lanes), jnp.float32)
        return carry

    lax.fori_loop(0, slots // size, flip, 0)

    def step(i, carry):
        second = i >= blocks
        block = jnp.where(second, half * part + i - blocks, i)
        at = pl.multiple_of(block * wide, wide)
        mine = _masked_rows(second, (lanes, wide), 0)
        mine_lanes = _masked_rows(second, (wide, lanes), 1)
        q_plain = q_ref[pl.ds(at, wide), :].astype(jnp.float32)
        q_rows = jnp.where(mine_lanes, q_plain, 0.0).astype(jnp.bfloat16)
        q_cols = jnp.where(mine, jnp.transpose(q_plain), 0.0).astype(jnp.bfloat16)
        dmix = jnp.where(mine, jnp.transpose(dmix_ref[pl.ds(at, wide), :].astype(jnp.float32)), 0.0)
        stats = stat_ref[:, pl.ds(at, wide)]
        top = jnp.where(second, stats[2:3, :], stats[0:1, :])
        total = jnp.where(second, stats[3:4, :], stats[1:2, :])
        dn_wide = dmix / total
        dn_cols = dn_wide.astype(jnp.bfloat16)
        dn_rows = jnp.transpose(dn_wide).astype(jnp.bfloat16)
        mixed = mix_ref[:, pl.ds(at, wide)]
        dtotal = -jnp.sum(dmix * mixed, axis=0, keepdims=True) / total
        dtotal = dtotal.astype(jnp.bfloat16).astype(jnp.float32)
        chunks = _chunk_count(count, block, wide, size, causal)

        full = _full_count(count, block, wide, size, causal)

        def one(masked, c, dq):
            spot = pl.multiple_of(c * size, size)
            s = jnp.dot(k_ref[pl.ds(spot, size), :], q_cols, preferred_element_type=jnp.float32)
            if masked:
                s = jnp.where(_score_mask(c, size, block, count, wide, causal), s, NEGATIVE)
            e = jnp.exp(s - top)
            through = jnp.dot(v_ref[pl.ds(spot, size), :], dn_cols, preferred_element_type=jnp.float32)
            ds = (e * (through + dtotal)).astype(jnp.bfloat16)
            dv_ref[pl.ds(spot, size), :] = dv_ref[pl.ds(spot, size), :] + jnp.dot(
                e.astype(jnp.bfloat16), dn_rows, preferred_element_type=jnp.float32
            )
            dk_ref[pl.ds(spot, size), :] = dk_ref[pl.ds(spot, size), :] + jnp.dot(
                ds, q_rows, preferred_element_type=jnp.float32
            )
            return dq + jnp.dot(kt_ref[:, pl.ds(spot, size)], ds, preferred_element_type=jnp.float32)

        dq = jnp.zeros((lanes, wide), jnp.float32)
        dq = lax.fori_loop(0, full, functools.partial(one, False), dq)
        dq = lax.fori_loop(full, chunks, functools.partial(one, True), dq)
        back = jnp.transpose(jnp.where(mine, dq, 0.0))

        @pl.when(jnp.logical_not(second))
        def _():
            dq_ref[pl.ds(at, wide), :] = back

        @pl.when(second)
        def _():
            dq_ref[pl.ds(at, wide), :] = dq_ref[pl.ds(at, wide), :] + back

        return carry

    lax.fori_loop(0, total_steps, step, 0)
    shift = lanes if packed else 0
    if packed:
        out_ref[:, 0:lanes] = dq_ref[...].astype(jnp.bfloat16)
    else:
        dqo_ref[...] = dq_ref[...].astype(jnp.bfloat16)

    def emit(c, carry):
        at = pl.multiple_of(c * size, size)
        out_ref[pl.ds(at, size), shift : shift + lanes] = dk_ref[pl.ds(at, size), :].astype(jnp.bfloat16)
        out_ref[pl.ds(at, size), shift + lanes : shift + 2 * lanes] = dv_ref[pl.ds(at, size), :].astype(
            jnp.bfloat16
        )
        return carry

    lax.fori_loop(0, slots // size, emit, 0)


def attention(info, parts, causal):
    lanes = 2 * HEAD_DIM
    rows = parts[0].shape[0]
    slots = parts[-1].shape[0]
    wide = min(256, rows // 2)
    size = min(256 if causal else 512, slots)
    work = rows * slots * lanes * (2 if causal else 4)
    return pl.pallas_call(
        functools.partial(attend_kernel, wide, size, causal, len(parts) == 1),
        name="attend_self" if causal else "attend_cross",
        out_shape=(
            jax.ShapeDtypeStruct((rows, lanes), jnp.bfloat16),
            jax.ShapeDtypeStruct((lanes, rows), jnp.float32),
            jax.ShapeDtypeStruct((8, rows), jnp.float32),
        ),
        in_specs=[pl.BlockSpec(memory_space=pltpu.SMEM)]
        + [pl.BlockSpec(memory_space=pltpu.VMEM)] * len(parts),
        out_specs=(pl.BlockSpec(memory_space=pltpu.VMEM),) * 3,
        scratch_shapes=[
            pltpu.VMEM((lanes, slots), jnp.bfloat16),
            pltpu.VMEM((slots, wide), jnp.float32),
        ],
        compiler_params=pltpu.CompilerParams(vmem_limit_bytes=32 * 1024 * 1024),
        cost_estimate=pl.CostEstimate(flops=work, bytes_accessed=slots * lanes * 8, transcendentals=rows * slots),
    )(info, *parts)


def attention_back(info, parts, dmix, mixed, stats, causal):
    lanes = 2 * HEAD_DIM
    rows = parts[0].shape[0]
    slots = parts[-1].shape[0]
    wide = min(256, rows // 2)
    size = min(256 if causal else 512, slots)
    work = rows * slots * lanes * (5 if causal else 10)
    packed = len(parts) == 1
    outs = (jax.ShapeDtypeStruct((slots, (3 if packed else 2) * lanes), jnp.bfloat16),)
    if not packed:
        outs = (jax.ShapeDtypeStruct((rows, lanes), jnp.bfloat16),) + outs
    return pl.pallas_call(
        functools.partial(attend_back_kernel, wide, size, causal, packed),
        name="attend_self_back" if causal else "attend_cross_back",
        out_shape=outs,
        in_specs=[pl.BlockSpec(memory_space=pltpu.SMEM)]
        + [pl.BlockSpec(memory_space=pltpu.VMEM)] * (len(parts) + 3),
        out_specs=(pl.BlockSpec(memory_space=pltpu.VMEM),) * len(outs),
        scratch_shapes=[
            pltpu.VMEM((lanes, slots), jnp.bfloat16),
            pltpu.VMEM((slots, lanes), jnp.float32),
            pltpu.VMEM((slots, lanes), jnp.float32),
            pltpu.VMEM((rows, lanes), jnp.float32),
        ],
        compiler_params=pltpu.CompilerParams(vmem_limit_bytes=40 * 1024 * 1024),
        cost_estimate=pl.CostEstimate(flops=work, bytes_accessed=slots * lanes * 8, transcendentals=rows * slots),
    )(info, *parts, dmix, mixed, stats)


def take(array, index, axis=0):
    return lax.dynamic_index_in_dim(array, index, axis, False)


def put(array, piece, index):
    return lax.dynamic_update_index_in_dim(array, piece, index, 0)


def twins(first, own, other):
    return jnp.where(first, jnp.stack([own, other]), jnp.stack([other, own]))


def by_heads(
    dec_in,
    enc_in,
    tgt_len,
    enc_len,
    self_qkv,
    self_out,
    cross_q,
    cross_kv,
    cross_out,
    ff_in,
    ff_out,
    gains,
    cotangent,
):
    f32, bf16 = jnp.float32, jnp.bfloat16
    tie = lax.optimization_barrier
    docs_here, rows_doc, width = dec_in.shape
    slots_doc = enc_in.shape[1]
    doc_ranks, seq_ranks = lax.axis_size("doc"), lax.axis_size("seq")
    seq_rank, doc_rank = lax.axis_index("seq"), lax.axis_index("doc")
    z_rank, x_rank = seq_rank // 2, seq_rank % 2
    units = seq_ranks // 2
    column_pairs = [(i, i ^ 1) for i in range(seq_ranks)]
    shifts = [[(i, (i + 2 * k) % seq_ranks) for i in range(seq_ranks)] for k in range(units)]
    lanes = 2 * HEAD_DIM
    share = HEADS * HEAD_DIM // doc_ranks
    rest = share - HEAD_DIM
    depth = width // seq_ranks
    rows = docs_here * rows_doc
    slots = docs_here * slots_doc
    hidden_here = ff_in.shape[2]
    even = doc_rank % 2 == 0
    first = x_rank == 0

    def swap_x(array):
        return lax.ppermute(array, "seq", column_pairs)

    def swap_y(array):
        return lax.ppermute(array, "doc", [(i, i ^ 2) for i in range(doc_ranks)])

    def swap_core(array):
        return lax.ppermute(array, "doc", [(i, i ^ 1) for i in range(doc_ranks)])

    def shift_z(array, k):
        return lax.ppermute(array, "seq", shifts[k % units])

    def by_document(array):
        pair = twins(first, take(array, x_rank), swap_x(take(array, 1 - x_rank)))
        return pair.reshape((-1,) + pair.shape[2:])

    def by_position(array):
        pair = array.reshape((2, array.shape[0] // 2) + array.shape[1:])
        return twins(first, take(pair, x_rank), swap_x(take(pair, 1 - x_rank)))

    def gather_z(array):
        out = jnp.broadcast_to(array, (units,) + array.shape)
        for k in range(1, units):
            out = put(out, shift_z(array, k), (z_rank - k) % units)
        return out

    def send_units(array):
        return [take(array, z_rank)] + [
            shift_z(take(array, (z_rank + k) % units), k) for k in range(1, units)
        ]

    def to_unit(array):
        out = array
        for k, arrived in enumerate(send_units(array)):
            out = put(out, arrived, (z_rank - k) % units)
        return out.reshape((-1,) + out.shape[2:])

    def to_rows(array):
        array = array.reshape((units, -1) + array.shape[1:])
        out = array
        for k in range(units):
            piece = take(array, (z_rank + k) % units)
            piece = shift_z(piece, k) if k else piece
            out = put(out, piece, (z_rank - k) % units)
        return out

    def return_units(pieces):
        out = jnp.zeros((units,) + pieces[0].shape, pieces[0].dtype)
        for k, piece in enumerate(pieces):
            arrived = shift_z(piece, units - k) if k else piece
            out = put(out, arrived, (z_rank + k) % units)
        return out

    def gather_doc(array):
        across, beside = swap_y(array), swap_core(array)
        return jnp.concatenate([array, beside], axis=0), jnp.concatenate([across, swap_core(across)], axis=0)

    def add_core(array):
        n = array.shape[0] // 2
        return array[:n] + swap_core(array[n:].astype(bf16)).astype(f32)

    def add_x(array):
        arrived = swap_x(take(array, 1 - x_rank, 1))
        return (take(array, x_rank, 1).astype(f32) + arrived.astype(f32)).astype(bf16)

    def add_z(array):
        total = take(array, z_rank).astype(f32)
        for k in range(1, units):
            total = total + shift_z(take(array, (z_rank + k) % units), k).astype(f32)
        return total

    def whole_first(block):
        return jnp.where(even, block, jnp.concatenate([block[:, rest:], block[:, :rest]], axis=1))

    def whole_back(block):
        return jnp.where(even, block, jnp.concatenate([block[:, HEAD_DIM:], block[:, :HEAD_DIM]], axis=1))

    def spread(out, parts):
        pieces = []
        for j in range(doc_ranks):
            line = []
            for i in range(parts):
                line.append(out[j, :, i * share : (i + 1) * share])
                line.append(out[j ^ 1, :, i * share + HEAD_DIM : (i + 1) * share])
            pieces.append(jnp.concatenate(line, axis=1))
        return jnp.stack(pieces)

    def merge(array, parts):
        wide_in = array.astype(f32)
        pieces = []
        for j in range(doc_ranks):
            line = []
            for i in range(parts):
                at = i * lanes
                line.append(wide_in[j, :, at : at + HEAD_DIM])
                line.append(
                    wide_in[j, :, at + HEAD_DIM : at + share] + wide_in[j ^ 1, :, at + share : at + lanes]
                )
            pieces.append(jnp.concatenate(line, axis=1))
        return jnp.stack(pieces).astype(bf16)

    def spread_weight(block, parts):
        return spread(block, parts)

    def project_wide(rows_in, weight):
        return jnp.einsum("td,jdk->jtk", rows_in, weight, preferred_element_type=f32).astype(bf16)

    def project(rows_in, weight, parts):
        return spread(project_wide(rows_in, weight), parts)

    def lift(inner_in, weight):
        return jnp.einsum("jtk,jdk->td", inner_in, weight, preferred_element_type=f32)

    def fold(terms, parts):
        terms = terms.reshape(doc_ranks, parts, lanes, width)
        other = jnp.stack([terms[j ^ 1, :, share:] for j in range(doc_ranks)]).astype(f32)
        split = (terms[:, :, HEAD_DIM:share].astype(f32) + other).astype(bf16)
        return jnp.concatenate([terms[:, :, :HEAD_DIM], split], axis=2).reshape(doc_ranks, parts * share, width)

    def outer(inner_in, rows_in):
        return jnp.einsum("jtk,td->jkd", inner_in, rows_in, preferred_element_type=f32).astype(bf16)

    part = z_rank % 2
    info_self = jnp.stack([take(tgt_len, x_rank), part])
    info_cross = jnp.stack([take(enc_len, x_rank), part])

    small = jnp.concatenate(
        [
            whole_first(b)
            for b in (
                self_qkv[0],
                self_qkv[1],
                self_qkv[2],
                cross_q,
                cross_kv[0],
                cross_kv[1],
                self_out.T,
                cross_out.T,
            )
        ],
        axis=1,
    )
    every = lax.all_gather(small, ("doc", "seq"), axis=0, tiled=True)
    ff_mine = jnp.concatenate([ff_in[0], ff_in[1], ff_out.T], axis=1)
    ff_all = lax.all_gather(ff_mine, "seq", axis=0, tiled=True)
    gain_pair = twins(first, gains, swap_x(gains))
    gain_all = gather_z(gain_pair).transpose(2, 0, 1, 3).reshape(3, width).astype(f32)
    stream = by_document(dec_in).astype(f32)
    normed1, inverse1 = norm_parts(stream, gain_all[0])
    normed1 = normed1.astype(bf16)
    every, normed1, cotangent = tie((every, normed1, cotangent))
    every = every.reshape(doc_ranks, width, 8 * share)
    w_qkv = every[:, :, : 3 * share]
    w_cq = every[:, :, 3 * share : 4 * share]
    w_ckv = every[:, :, 4 * share : 6 * share]
    w_so = every[:, :, 6 * share : 7 * share]
    w_co = every[:, :, 7 * share :]

    qkv_rows = project(normed1, w_qkv, 3)
    qkv_heads = to_unit(qkv_rows)
    enc_rows = enc_in.reshape(slots, width)
    w_kv = spread_weight(w_ckv, 2)
    ckv = project_wide(enc_rows, w_kv).reshape(units, docs_here, slots_doc, 2 * lanes)
    ckv_other = swap_x(take(ckv, 1 - x_rank, 1))
    ckv_own = to_unit(take(ckv, x_rank, 1))
    qkv_heads, ckv, cotangent = tie((qkv_heads, ckv, cotangent))
    att1, mix1, stat1 = attention(info_self, (qkv_heads,), True)
    att1 = to_rows(att1)
    att1, ckv_other = tie((att1, ckv_other))
    ckv_other = to_unit(ckv_other)
    att1 = merge(att1, 1)
    cot = by_document(cotangent)
    cot_near, cot_far = gather_doc(cot)
    stream1 = stream + lift(att1, w_so)
    normed2, inverse2 = norm_parts(stream1, gain_all[1])
    normed2 = normed2.astype(bf16)
    cq_heads = to_unit(project(normed2, w_cq, 1))
    cq_heads, normed1 = tie((cq_heads, normed1))
    n1_near, n1_far = gather_doc(normed1)
    halves = (ckv_own.reshape(units, slots_doc, 2 * lanes), ckv_other.reshape(units, slots_doc, 2 * lanes))
    ckv_heads = jnp.where(first, jnp.stack(halves, axis=1), jnp.stack(halves[::-1], axis=1))
    ckv_heads = ckv_heads.reshape(units * slots, 2 * lanes)
    att2, mix2, stat2 = attention(info_cross, (cq_heads, ckv_heads), False)
    att2 = merge(to_rows(att2), 1)
    att2, n1_near, n1_far, cot_near, cot_far = tie((att2, n1_near, n1_far, cot_near, cot_far))
    stream2 = stream1 + lift(att2, w_co)
    normed3, inverse3 = norm_parts(stream2, gain_all[2])
    normed3 = normed3.astype(bf16)

    w_gate, w_up = ff_all[:, :hidden_here], ff_all[:, hidden_here : 2 * hidden_here]
    w_down = ff_all[:, 2 * hidden_here :]

    def inside(n3_rows, cot_rows):
        gate_pre = matmul_rows(n3_rows, w_gate)
        up_pre = matmul_rows(n3_rows, w_up)
        d_hidden = matmul_rows(cot_rows, w_down)
        hidden, gelu_pull = jax.vjp(
            lambda gate_val, up_val: jax.nn.gelu(gate_val, approximate=True) * up_val, gate_pre, up_pre
        )
        d_gate, d_up = gelu_pull(d_hidden)
        return hidden.astype(bf16), d_gate.astype(bf16), d_up.astype(bf16)

    def through(d_gate, d_up):
        return matmul_back(d_gate, w_gate) + matmul_back(d_up, w_up)

    n3_near, n3_far = gather_doc(normed3)
    hid_near, dg_near, du_near = inside(n3_near, cot_near)
    hid_near, n3_far = tie((hid_near, n3_far))
    hid_far, dg_far, du_far = inside(n3_far, cot_far)
    dn3_across = swap_y(add_core(through(dg_far, du_far)).astype(bf16))
    dn3_near = add_core(through(dg_near, du_near))
    n3_all = jnp.concatenate([n3_near, n3_far], axis=0)
    cot_all = jnp.concatenate([cot_near, cot_far], axis=0)
    d_gate = jnp.concatenate([dg_near, dg_far], axis=0)
    d_up = jnp.concatenate([du_near, du_far], axis=0)
    hidden = jnp.concatenate([hid_near, hid_far], axis=0)
    ff_grads = jnp.concatenate(
        [
            matmul_outer(n3_all, d_gate).astype(bf16),
            matmul_outer(n3_all, d_up).astype(bf16),
            matmul_outer(cot_all, hidden).astype(bf16),
        ],
        axis=1,
    )
    ff_sum = lax.psum_scatter(ff_grads, "seq", scatter_dimension=0, tiled=True)
    dn3_across, ff_grads = tie((dn3_across, ff_grads))
    d_normed3 = dn3_near + dn3_across.astype(f32)

    back_three, gain_grad3 = norm_back(stream2, inverse3, gain_all[2], d_normed3)
    d_stream2 = cot.astype(f32) + back_three
    d_branch2 = d_stream2.astype(bf16)
    d_mix2 = to_unit(project(d_branch2, w_co, 1))
    d_mix2, hidden_late = tie((d_mix2, hidden))
    branch_across = swap_y(add_core(matmul_back(hidden_late[2 * rows :], w_down)).astype(bf16))
    branch = add_core(matmul_back(hidden_late[: 2 * rows], w_down))
    d_cq, d_ckv = attention_back(info_cross, (cq_heads, ckv_heads), d_mix2, mix2, stat2, False)
    d_ckv = d_ckv.reshape(units, 2, slots_doc, 2 * lanes)
    d_cq = to_rows(d_cq)
    d_cq, d_ckv, branch_across = tie((d_cq, d_ckv, branch_across))
    d_ckv_other = to_rows(take(d_ckv, 1 - x_rank, 1).reshape(-1, 2 * lanes))
    d_cq = merge(d_cq, 1)
    back_two, gain_grad2 = norm_back(stream1, inverse2, gain_all[1], lift(d_cq, w_cq))
    d_stream1 = d_stream2 + back_two
    d_branch1 = d_stream1.astype(bf16)
    d_branch1, d_ckv = tie((d_branch1, d_ckv))
    d_mix1 = to_unit(project(d_branch1, w_so, 1))
    d_ckv_own = to_rows(take(d_ckv, x_rank, 1).reshape(-1, 2 * lanes))
    d_mix1, d_ckv_other = tie((d_mix1, d_ckv_other))
    d_ckv_other = swap_x(d_ckv_other)
    (d_qkv,) = attention_back(info_self, (qkv_heads,), d_mix1, mix1, stat1, True)
    d_qkv, d_ckv_own, d_ckv_other, d_stream1, branch = tie((d_qkv, d_ckv_own, d_ckv_other, d_stream1, branch))
    d_qkv = to_rows(d_qkv)
    d_ckv = jnp.where(first, jnp.stack([d_ckv_own, d_ckv_other], axis=1), jnp.stack([d_ckv_other, d_ckv_own], axis=1))
    d_ckv = d_ckv.reshape(units, slots, 2 * lanes)
    enc_grad = lift(d_ckv, w_kv).reshape(docs_here, slots_doc, width)
    layer_out = by_position(stream2 + (branch + branch_across.astype(f32)))
    d_qkv, enc_grad, layer_out = tie((d_qkv, enc_grad, layer_out))
    d_qkv = merge(d_qkv, 3)

    def beside(array, k):
        return take(array, doc_rank ^ k)

    arrived = swap_core(jnp.stack([beside(d_qkv, 1), beside(d_qkv, 3)]))
    d_near = jnp.concatenate([beside(d_qkv, 0), arrived[0]], axis=0)
    d_far = swap_y(jnp.concatenate([beside(d_qkv, 2), arrived[1]], axis=0))
    back_one, gain_grad1 = norm_back(stream, inverse1, gain_all[0], lift(d_qkv, w_qkv))
    dec_grad = by_position(d_stream1 + back_one)

    terms = jnp.concatenate(
        [
            outer(d_cq, normed2),
            fold(outer(d_ckv, enc_rows), 2),
            outer(att1, d_branch1),
            outer(att2, d_branch2),
        ],
        axis=1,
    )
    arrived = swap_core(jnp.stack([beside(terms, 1), beside(terms, 3)])).astype(f32)
    across = swap_y((beside(terms, 2).astype(f32) + arrived[1]).astype(bf16))
    terms = (beside(terms, 0).astype(f32) + arrived[0]) + across.astype(f32)
    terms = terms.astype(bf16).T.reshape(units, 2, depth, 5 * share)
    others = add_z(add_x(terms))

    gain_terms = jnp.stack([gain_grad1, gain_grad2, gain_grad3])
    gain_terms = gain_terms + swap_core(gain_terms)
    gain_terms = gain_terms + swap_y(gain_terms)
    gain_terms = gain_terms.reshape(3, seq_ranks, depth).transpose(1, 0, 2)
    gain_terms = gain_terms.reshape(seq_ranks, 2, 3 * depth // 2).astype(bf16)
    gain_terms = jnp.pad(gain_terms, ((0, 0), (0, 6), (0, 3 * share - 3 * depth // 2)))
    grad_qkv = matmul_outer(n1_near, d_near) + matmul_outer(n1_far, d_far)
    grad_qkv = grad_qkv.astype(bf16).reshape(seq_ranks, depth, 3 * share)
    grad_qkv = jnp.concatenate([grad_qkv, gain_terms], axis=1)
    grad_qkv = grad_qkv.reshape(units, 2, depth + 8, 3 * share)
    summed = add_z(add_x(grad_qkv))
    grad_gains = summed[depth : depth + 2, : 3 * depth // 2].reshape(3, depth)
    piece = lambda a, i: whole_back(a[:depth, i * share : (i + 1) * share])
    ff_sum = ff_sum.astype(f32)
    return (
        layer_out,
        dec_grad,
        enc_grad,
        jnp.stack([piece(summed, 0), piece(summed, 1), piece(summed, 2)]),
        piece(others, 3).T,
        piece(others, 0),
        jnp.stack([piece(others, 1), piece(others, 2)]),
        piece(others, 4).T,
        jnp.stack([ff_sum[:, :hidden_here], ff_sum[:, hidden_here : 2 * hidden_here]]),
        ff_sum[:, 2 * hidden_here :].T,
        grad_gains,
    )


def fits_by_heads(doc_ranks, seq_ranks, docs):
    return doc_ranks == 4 and seq_ranks == 8 and docs == 8


def solution(mesh):
    def either(dec_in, *others):
        docs = dec_in.shape[0] * mesh.shape["doc"]
        if fits_by_heads(mesh.shape["doc"], mesh.shape["seq"], docs):
            return by_heads(dec_in, *others)
        return per_device(dec_in, *others)

    return jax.shard_map(
        either,
        mesh=mesh,
        in_specs=(
            P("doc", "seq", None),
            P("doc", "seq", None),
            P("doc"),
            P("doc"),
            P(None, "seq", "doc"),
            P("doc", "seq"),
            P("seq", "doc"),
            P(None, "seq", "doc"),
            P("doc", "seq"),
            P(None, "seq", "doc"),
            P("doc", "seq"),
            P(None, "seq"),
            P("doc", "seq", None),
        ),
        out_specs=(
            P("doc", "seq", None),
            P("doc", "seq", None),
            P("doc", "seq", None),
            P(None, "seq", "doc"),
            P("doc", "seq"),
            P("seq", "doc"),
            P(None, "seq", "doc"),
            P("doc", "seq"),
            P(None, "seq", "doc"),
            P("doc", "seq"),
            P(None, "seq"),
        ),
        check_vma=False,
    )
```

```python
import functools

import jax
import jax.numpy as jnp
from jax import lax
from jax.experimental import pallas as pl
from jax.experimental.pallas import tpu as pltpu
from jax.sharding import PartitionSpec as P

HEADS = 6
HEAD_DIM = 64


EPSILON = 1e-06
NEGATIVE = -1e30


def norm_parts(values, gain_row):
    inverse = lax.rsqrt(jnp.mean(values * values, axis=-1, keepdims=True) + EPSILON)
    return (values * inverse * gain_row, inverse)


def norm_back(values, inverse, gain_row, upstream):
    weighted = upstream * gain_row
    inner_sum = jnp.mean(weighted * values, axis=-1, keepdims=True)
    lowered = weighted * inverse - values * (inverse * inverse * inverse) * inner_sum
    return (lowered, jnp.sum(upstream * values * inverse, axis=0))


def matmul_rows(left_op, right_op):
    return jnp.dot(left_op, right_op, preferred_element_type=jnp.float32)


def matmul_back(left_op, right_op):
    return lax.dot_general(
        left_op, right_op, (((1,), (1,)), ((), ())), preferred_element_type=jnp.float32
    )


def matmul_outer(left_op, right_op):
    return lax.dot_general(
        left_op, right_op, (((0,), (0,)), ((), ())), preferred_element_type=jnp.float32
    )


def head_scores(queries, keys_in, allowed):
    scores = jnp.einsum("bqhd,bkhd->bqhk", queries, keys_in, preferred_element_type=jnp.float32)
    return jnp.where(allowed[:, :, None, :], scores, NEGATIVE)


def weigh_values(raised, values_in):
    return jnp.einsum(
        "bqhk,bkhd->bqhd",
        raised.astype(jnp.bfloat16),
        values_in,
        preferred_element_type=jnp.float32,
    )


def mixed_grads(dmixed, numerator, totals):
    d_numer = (dmixed / totals[..., None]).astype(jnp.bfloat16)
    d_total = (-jnp.sum(dmixed * numerator, axis=-1) / (totals * totals)).astype(jnp.bfloat16)
    return (d_numer, d_total)


def score_grads(raised, d_numer, d_total, values_in):
    through = jnp.einsum("bqhd,bkhd->bqhk", d_numer, values_in, preferred_element_type=jnp.float32)
    return (raised * (through + d_total.astype(jnp.float32)[..., None])).astype(jnp.bfloat16)


def pair_grads(d_scores, raised, queries, keys_in, d_numer):
    d_query = jnp.einsum("bqhk,bkhd->bqhd", d_scores, keys_in, preferred_element_type=jnp.float32)
    d_keys = jnp.einsum("bqhk,bqhd->bkhd", d_scores, queries, preferred_element_type=jnp.float32)
    d_values = jnp.einsum(
        "bqhk,bqhd->bkhd", raised.astype(jnp.bfloat16), d_numer, preferred_element_type=jnp.float32
    )
    return (d_query, d_keys, d_values)


def block_size(docs_here):
    if docs_here % 4 == 0:
        return 4
    if docs_here % 2 == 0:
        return 2
    return 1


def feed_forward(rows_in, cot_in, w_in, w_out):
    gate_pre = matmul_rows(rows_in, w_in[0])
    up_pre = matmul_rows(rows_in, w_in[1])
    hidden = (jax.nn.gelu(gate_pre, approximate=True) * up_pre).astype(jnp.bfloat16)
    branch = matmul_rows(hidden, w_out)
    grad_out = matmul_outer(hidden, cot_in)
    d_hidden = matmul_back(cot_in, w_out)
    unused, gelu_pull = jax.vjp(
        lambda gate_val, up_val: jax.nn.gelu(gate_val, approximate=True) * up_val, gate_pre, up_pre
    )
    d_gate, d_up = gelu_pull(d_hidden)
    d_gate_up = jnp.stack([d_gate, d_up]).astype(jnp.bfloat16)
    grad_in = jnp.einsum("td,ctf->cdf", rows_in, d_gate_up, preferred_element_type=jnp.float32)
    d_rows = jnp.einsum("ctf,cdf->td", d_gate_up, w_in, preferred_element_type=jnp.float32)
    return (branch, grad_in, grad_out, d_rows)


def per_device(
    dec_in,
    enc_in,
    tgt_len,
    enc_len,
    self_qkv,
    self_out,
    cross_q,
    cross_kv,
    cross_out,
    ff_in,
    ff_out,
    gains,
    cotangent,
):
    by_rows = (
        lax.all_gather(self_qkv, "seq", axis=1, tiled=True),
        lax.all_gather(self_out, "seq", axis=1, tiled=True),
        lax.all_gather(cross_q, "seq", axis=0, tiled=True),
        lax.all_gather(cross_kv, "seq", axis=1, tiled=True),
        lax.all_gather(cross_out, "seq", axis=1, tiled=True),
        lax.all_gather(ff_in, "seq", axis=1, tiled=True),
        lax.all_gather(ff_out, "seq", axis=1, tiled=True),
        lax.all_gather(gains, "seq", axis=1, tiled=True),
    )
    w_qkv, w_so, w_cq, w_ckv, w_co, w_in, w_out = (
        lax.all_gather(by_rows[0], "doc", axis=2, tiled=True),
        lax.all_gather(by_rows[1], "doc", axis=0, tiled=True),
        lax.all_gather(by_rows[2], "doc", axis=1, tiled=True),
        lax.all_gather(by_rows[3], "doc", axis=2, tiled=True),
        lax.all_gather(by_rows[4], "doc", axis=0, tiled=True),
        lax.all_gather(by_rows[5], "doc", axis=2, tiled=True),
        lax.all_gather(by_rows[6], "doc", axis=0, tiled=True),
    )
    gain_all = by_rows[7].astype(jnp.float32)
    docs_here, rows_doc, model_width = dec_in.shape
    slot_count = enc_in.shape[1]
    seq_ranks = lax.axis_size("seq")
    my_rank = lax.axis_index("seq")
    length = rows_doc * seq_ranks
    inner_width = HEADS * HEAD_DIM
    rows_all = docs_here * rows_doc
    stream = dec_in.reshape(rows_all, model_width).astype(jnp.float32)
    normed1, inverse1 = norm_parts(stream, gain_all[0])
    normed1 = normed1.astype(jnp.bfloat16)
    proj_qkv = jnp.einsum("td,cdk->ctk", normed1, w_qkv, preferred_element_type=jnp.float32).astype(
        jnp.bfloat16
    )
    self_query = proj_qkv[0].reshape(docs_here, rows_doc, HEADS, HEAD_DIM)
    keys_all, values_all = (
        lax.all_gather(
            proj_qkv[1].reshape(docs_here, rows_doc, inner_width), "seq", axis=1, tiled=True
        ),
        lax.all_gather(
            proj_qkv[2].reshape(docs_here, rows_doc, inner_width), "seq", axis=1, tiled=True
        ),
    )
    keys_all = keys_all.reshape(docs_here, length, HEADS, HEAD_DIM)
    values_all = values_all.reshape(docs_here, length, HEADS, HEAD_DIM)
    query_pos = my_rank * rows_doc + jnp.arange(rows_doc, dtype=jnp.int32)
    key_pos = jnp.arange(length, dtype=jnp.int32)
    self_allowed = (key_pos[None, None, :] <= query_pos[None, :, None]) & (
        key_pos[None, None, :] < tgt_len[:, None, None]
    )
    self_scores = head_scores(self_query, keys_all, self_allowed)
    self_top = jnp.max(self_scores, axis=-1)
    self_raised = jnp.exp(self_scores - self_top[..., None])
    self_total = jnp.sum(self_raised, axis=-1)
    self_numer = weigh_values(self_raised, values_all)
    self_mixed = (
        (self_numer / self_total[..., None]).astype(jnp.bfloat16).reshape(rows_all, inner_width)
    )
    stream1 = stream + matmul_rows(self_mixed, w_so)
    normed2, inverse2 = norm_parts(stream1, gain_all[1])
    normed2 = normed2.astype(jnp.bfloat16)
    cross_query = (
        matmul_rows(normed2, w_cq).astype(jnp.bfloat16).reshape(docs_here, rows_doc, inner_width)
    )
    enc_proj = jnp.einsum(
        "bsd,cdk->cbsk", enc_in, w_ckv, preferred_element_type=jnp.float32
    ).astype(jnp.bfloat16)
    queries_all = lax.all_gather(cross_query, "seq", axis=1, tiled=True)
    per_block = block_size(docs_here)
    block_count = docs_here // per_block

    def split_docs(array):
        return array.reshape((block_count, per_block) + array.shape[1:])

    block_queries = split_docs(queries_all.reshape(docs_here, length, HEADS, HEAD_DIM))
    block_keys = split_docs(enc_proj[0].reshape(docs_here, slot_count, HEADS, HEAD_DIM))
    block_values = split_docs(enc_proj[1].reshape(docs_here, slot_count, HEADS, HEAD_DIM))
    slot_pos = my_rank * slot_count + jnp.arange(slot_count, dtype=jnp.int32)
    slot_live = split_docs(slot_pos[None, :] < enc_len[:, None])

    def cross_scores(queries, keys_in, slot_alive):
        allowed = jnp.broadcast_to(
            slot_alive[:, None, :], (slot_alive.shape[0], queries.shape[1], slot_alive.shape[1])
        )
        return head_scores(queries, keys_in, allowed)

    def local_peak(bundle):
        return jnp.max(cross_scores(bundle[0], bundle[1], bundle[2]), axis=-1)

    local_top = lax.map(local_peak, (block_queries, block_keys, slot_live))
    cross_top = lax.pmax(local_top.reshape(docs_here, length, HEADS), "seq")
    block_top = split_docs(cross_top)

    def cross_partial(bundle):
        queries, keys_in, values_in, slot_alive, peak_row = bundle
        raised = jnp.exp(cross_scores(queries, keys_in, slot_alive) - peak_row[..., None])
        return (weigh_values(raised, values_in), jnp.sum(raised, axis=-1))

    part_numer, part_total = lax.map(
        cross_partial, (block_queries, block_keys, block_values, slot_live, block_top)
    )
    cross_numer, cross_total = (
        lax.psum_scatter(
            part_numer.reshape(docs_here, length, inner_width),
            "seq",
            scatter_dimension=1,
            tiled=True,
        ),
        lax.psum_scatter(
            part_total.reshape(docs_here, length, HEADS), "seq", scatter_dimension=1, tiled=True
        ),
    )
    cross_numer = cross_numer.reshape(docs_here, rows_doc, HEADS, HEAD_DIM)
    cross_mixed = (
        (cross_numer / cross_total[..., None]).astype(jnp.bfloat16).reshape(rows_all, inner_width)
    )
    stream2 = stream1 + matmul_rows(cross_mixed, w_co)
    normed3, inverse3 = norm_parts(stream2, gain_all[2])
    normed3 = normed3.astype(jnp.bfloat16)
    cot_rows = cotangent.reshape(rows_all, model_width)
    ff_branch, grad_in, grad_out, d_normed3 = feed_forward(normed3, cot_rows, w_in, w_out)
    layer_out = (stream2 + ff_branch).reshape(docs_here, rows_doc, model_width)
    back_three, gain_grad3 = norm_back(stream2, inverse3, gain_all[2], d_normed3)
    d_stream2 = cot_rows.astype(jnp.float32) + back_three
    d_branch2 = d_stream2.astype(jnp.bfloat16)
    grad_co = matmul_outer(cross_mixed, d_branch2)
    d_mixed2 = matmul_back(d_branch2, w_co).reshape(docs_here, rows_doc, HEADS, HEAD_DIM)
    d_numer2, d_total2 = mixed_grads(d_mixed2, cross_numer, cross_total)
    numer_back, total_back = (
        lax.all_gather(
            d_numer2.reshape(docs_here, rows_doc, inner_width), "seq", axis=1, tiled=True
        ),
        lax.all_gather(d_total2, "seq", axis=1, tiled=True),
    )

    def cross_back_block(bundle):
        queries, keys_in, values_in, slot_alive, peak_row, d_numer, d_total = bundle
        raised = jnp.exp(cross_scores(queries, keys_in, slot_alive) - peak_row[..., None])
        d_scores = score_grads(raised, d_numer, d_total, values_in)
        return pair_grads(d_scores, raised, queries, keys_in, d_numer)

    part_dq, part_dk, part_dv = lax.map(
        cross_back_block,
        (
            block_queries,
            block_keys,
            block_values,
            slot_live,
            block_top,
            split_docs(numer_back.reshape(docs_here, length, HEADS, HEAD_DIM)),
            split_docs(total_back),
        ),
    )
    d_cross_q = lax.psum_scatter(
        part_dq.reshape(docs_here, length, inner_width), "seq", scatter_dimension=1, tiled=True
    )
    d_cross_q = d_cross_q.astype(jnp.bfloat16).reshape(rows_all, inner_width)
    d_enc_proj = jnp.stack(
        [
            part_dk.reshape(docs_here, slot_count, inner_width),
            part_dv.reshape(docs_here, slot_count, inner_width),
        ]
    ).astype(jnp.bfloat16)
    grad_cq = matmul_outer(normed2, d_cross_q)
    grad_ckv = jnp.einsum("bsd,cbsk->cdk", enc_in, d_enc_proj, preferred_element_type=jnp.float32)
    enc_grad = jnp.einsum("cbsk,cdk->bsd", d_enc_proj, w_ckv, preferred_element_type=jnp.float32)
    back_two, gain_grad2 = norm_back(stream1, inverse2, gain_all[1], matmul_back(d_cross_q, w_cq))
    d_stream1 = d_stream2 + back_two
    d_branch1 = d_stream1.astype(jnp.bfloat16)
    grad_so = matmul_outer(self_mixed, d_branch1)
    d_mixed1 = matmul_back(d_branch1, w_so).reshape(docs_here, rows_doc, HEADS, HEAD_DIM)
    d_numer1, d_total1 = mixed_grads(d_mixed1, self_numer, self_total)
    again_raised = jnp.exp(head_scores(self_query, keys_all, self_allowed) - self_top[..., None])
    d_scores1 = score_grads(again_raised, d_numer1, d_total1, values_all)
    d_query1, part_dk1, part_dv1 = pair_grads(
        d_scores1, again_raised, self_query, keys_all, d_numer1
    )
    d_keys1, d_values1 = (
        lax.psum_scatter(
            part_dk1.reshape(docs_here, length, inner_width), "seq", scatter_dimension=1, tiled=True
        ),
        lax.psum_scatter(
            part_dv1.reshape(docs_here, length, inner_width), "seq", scatter_dimension=1, tiled=True
        ),
    )
    d_qkv = jnp.stack(
        [
            d_query1.reshape(rows_all, inner_width),
            d_keys1.reshape(rows_all, inner_width),
            d_values1.reshape(rows_all, inner_width),
        ]
    ).astype(jnp.bfloat16)
    grad_qkv = jnp.einsum("td,ctk->cdk", normed1, d_qkv, preferred_element_type=jnp.float32)
    d_normed1 = jnp.einsum("ctk,cdk->td", d_qkv, w_qkv, preferred_element_type=jnp.float32)
    back_one, gain_grad1 = norm_back(stream, inverse1, gain_all[0], d_normed1)
    dec_grad = (d_stream1 + back_one).reshape(docs_here, rows_doc, model_width)
    gain_sum = lax.psum(jnp.stack([gain_grad1, gain_grad2, gain_grad3]), ("doc", "seq"))
    share_len = model_width // seq_ranks
    grad_gains = lax.dynamic_slice_in_dim(gain_sum, my_rank * share_len, share_len, 1)
    halfway = (
        lax.psum_scatter(grad_qkv, "doc", scatter_dimension=2, tiled=True),
        lax.psum_scatter(grad_so, "doc", scatter_dimension=0, tiled=True),
        lax.psum_scatter(grad_cq, "doc", scatter_dimension=1, tiled=True),
        lax.psum_scatter(grad_ckv, "doc", scatter_dimension=2, tiled=True),
        lax.psum_scatter(grad_co, "doc", scatter_dimension=0, tiled=True),
        lax.psum_scatter(grad_in, "doc", scatter_dimension=2, tiled=True),
        lax.psum_scatter(grad_out, "doc", scatter_dimension=0, tiled=True),
    )
    reduced = (
        lax.psum_scatter(halfway[0], "seq", scatter_dimension=1, tiled=True),
        lax.psum_scatter(halfway[1], "seq", scatter_dimension=1, tiled=True),
        lax.psum_scatter(halfway[2], "seq", scatter_dimension=0, tiled=True),
        lax.psum_scatter(halfway[3], "seq", scatter_dimension=1, tiled=True),
        lax.psum_scatter(halfway[4], "seq", scatter_dimension=1, tiled=True),
        lax.psum_scatter(halfway[5], "seq", scatter_dimension=1, tiled=True),
        lax.psum_scatter(halfway[6], "seq", scatter_dimension=1, tiled=True),
    )
    return (
        layer_out,
        dec_grad,
        enc_grad,
        reduced[0],
        reduced[1],
        reduced[2],
        reduced[3],
        reduced[4],
        reduced[5],
        reduced[6],
        grad_gains,
    )


def _masked_rows(is_second, shape, axis):
    index = lax.broadcasted_iota(jnp.int32, shape, axis)
    return (index >= HEAD_DIM) == is_second


def _transposed(array, dtype):
    return jnp.transpose(array.astype(jnp.float32)).astype(dtype)


def _score_mask(chunk, size, block, count, width, causal):
    slot = chunk * size + lax.broadcasted_iota(jnp.int32, (size, width), 0)
    live = slot < count
    if causal:
        query = block * width + lax.broadcasted_iota(jnp.int32, (size, width), 1)
        live = live & (slot <= query)
    return live


def _steps(info_ref, rows, wide):
    blocks = rows // wide
    half = blocks // 2
    return blocks, half, blocks + half


def _chunk_count(count, block, wide, size, causal):
    chunks = (count + size - 1) // size
    if causal:
        chunks = jnp.minimum(chunks, ((block + 1) * wide + size - 1) // size)
    return chunks


def _full_count(count, block, wide, size, causal):
    chunks = count // size
    if causal:
        chunks = jnp.minimum(chunks, block * wide // size)
    return chunks


def attend_kernel(wide, size, causal, packed, info_ref, *refs):
    if packed:
        qkv_ref, att_ref, mix_ref, stat_ref, vt_ref, score_ref = refs
        lanes = 2 * HEAD_DIM
        q_ref, k_ref, v_ref = (qkv_ref.at[:, pl.ds(i * lanes, lanes)] for i in range(3))
    else:
        q_ref, kv_ref, att_ref, mix_ref, stat_ref, vt_ref, score_ref = refs
        lanes = 2 * HEAD_DIM
        k_ref, v_ref = (kv_ref.at[:, pl.ds(i * lanes, lanes)] for i in range(2))
    rows = q_ref.shape[0]
    slots = k_ref.shape[0]
    count = info_ref[0]
    part = info_ref[1]
    blocks, half, total_steps = _steps(info_ref, rows, wide)

    def flip(c, carry):
        at = pl.multiple_of(c * size, size)
        vt_ref[:, pl.ds(at, size)] = _transposed(v_ref[pl.ds(at, size), :], jnp.bfloat16)
        return carry

    lax.fori_loop(0, slots // size, flip, 0)

    def step(i, carry):
        second = i >= blocks
        block = jnp.where(second, half * part + i - blocks, i)
        at = pl.multiple_of(block * wide, wide)
        mine = _masked_rows(second, (lanes, wide), 0)
        queries = jnp.where(mine, jnp.transpose(q_ref[pl.ds(at, wide), :].astype(jnp.float32)), 0.0)
        queries = queries.astype(jnp.bfloat16)
        chunks = _chunk_count(count, block, wide, size, causal)

        full = _full_count(count, block, wide, size, causal)

        def scores(masked, c, top):
            spot = pl.multiple_of(c * size, size)
            s = jnp.dot(k_ref[pl.ds(spot, size), :], queries, preferred_element_type=jnp.float32)
            if masked:
                s = jnp.where(_score_mask(c, size, block, count, wide, causal), s, NEGATIVE)
            score_ref[pl.ds(spot, size), :] = s
            return jnp.maximum(top, jnp.max(s.reshape(size // 8, 8, wide), axis=0))

        top = jnp.full((8, wide), NEGATIVE, jnp.float32)
        top = lax.fori_loop(0, full, functools.partial(scores, False), top)
        top = lax.fori_loop(full, chunks, functools.partial(scores, True), top)
        top = jnp.max(top, axis=0, keepdims=True)

        def weigh(c, carry):
            total, numer = carry
            spot = pl.multiple_of(c * size, size)
            e = jnp.exp(score_ref[pl.ds(spot, size), :] - top)
            total = total + jnp.sum(e.reshape(size // 8, 8, wide), axis=0)
            numer = numer + jnp.dot(
                vt_ref[:, pl.ds(spot, size)], e.astype(jnp.bfloat16), preferred_element_type=jnp.float32
            )
            return total, numer

        total, numer = lax.fori_loop(
            0,
            chunks,
            weigh,
            (jnp.zeros((8, wide), jnp.float32), jnp.zeros((lanes, wide), jnp.float32)),
        )
        total = jnp.sum(total, axis=0, keepdims=True)
        mixed = jnp.where(mine, numer / total, 0.0)
        back = jnp.transpose(mixed)

        @pl.when(jnp.logical_not(second))
        def _():
            att_ref[pl.ds(at, wide), :] = back.astype(jnp.bfloat16)
            mix_ref[:, pl.ds(at, wide)] = mixed
            stat_ref[0:1, pl.ds(at, wide)] = top
            stat_ref[1:2, pl.ds(at, wide)] = total

        @pl.when(second)
        def _():
            kept = att_ref[pl.ds(at, wide), :].astype(jnp.float32)
            att_ref[pl.ds(at, wide), :] = (kept + back).astype(jnp.bfloat16)
            mix_ref[:, pl.ds(at, wide)] = mix_ref[:, pl.ds(at, wide)] + mixed
            stat_ref[2:3, pl.ds(at, wide)] = top
            stat_ref[3:4, pl.ds(at, wide)] = total

        return carry

    lax.fori_loop(0, total_steps, step, 0)


def attend_back_kernel(wide, size, causal, packed, info_ref, *refs):
    lanes = 2 * HEAD_DIM
    if packed:
        qkv_ref, dmix_ref, mix_ref, stat_ref, out_ref, kt_ref, dk_ref, dv_ref, dq_ref = refs
        q_ref, k_ref, v_ref = (qkv_ref.at[:, pl.ds(i * lanes, lanes)] for i in range(3))
    else:
        q_ref, kv_ref, dmix_ref, mix_ref, stat_ref, dqo_ref, out_ref, kt_ref, dk_ref, dv_ref, dq_ref = refs
        k_ref, v_ref = (kv_ref.at[:, pl.ds(i * lanes, lanes)] for i in range(2))
    rows = q_ref.shape[0]
    slots = k_ref.shape[0]
    count = info_ref[0]
    part = info_ref[1]
    blocks, half, total_steps = _steps(info_ref, rows, wide)

    def flip(c, carry):
        at = pl.multiple_of(c * size, size)
        kt_ref[:, pl.ds(at, size)] = _transposed(k_ref[pl.ds(at, size), :], jnp.bfloat16)
        dk_ref[pl.ds(at, size), :] = jnp.zeros((size, lanes), jnp.float32)
        dv_ref[pl.ds(at, size), :] = jnp.zeros((size, lanes), jnp.float32)
        return carry

    lax.fori_loop(0, slots // size, flip, 0)

    def step(i, carry):
        second = i >= blocks
        block = jnp.where(second, half * part + i - blocks, i)
        at = pl.multiple_of(block * wide, wide)
        mine = _masked_rows(second, (lanes, wide), 0)
        mine_lanes = _masked_rows(second, (wide, lanes), 1)
        q_plain = q_ref[pl.ds(at, wide), :].astype(jnp.float32)
        q_rows = jnp.where(mine_lanes, q_plain, 0.0).astype(jnp.bfloat16)
        q_cols = jnp.where(mine, jnp.transpose(q_plain), 0.0).astype(jnp.bfloat16)
        dmix = jnp.where(mine, jnp.transpose(dmix_ref[pl.ds(at, wide), :].astype(jnp.float32)), 0.0)
        stats = stat_ref[:, pl.ds(at, wide)]
        top = jnp.where(second, stats[2:3, :], stats[0:1, :])
        total = jnp.where(second, stats[3:4, :], stats[1:2, :])
        dn_wide = dmix / total
        dn_cols = dn_wide.astype(jnp.bfloat16)
        dn_rows = jnp.transpose(dn_wide).astype(jnp.bfloat16)
        mixed = mix_ref[:, pl.ds(at, wide)]
        dtotal = -jnp.sum(dmix * mixed, axis=0, keepdims=True) / total
        dtotal = dtotal.astype(jnp.bfloat16).astype(jnp.float32)
        chunks = _chunk_count(count, block, wide, size, causal)

        full = _full_count(count, block, wide, size, causal)

        def one(masked, c, dq):
            spot = pl.multiple_of(c * size, size)
            s = jnp.dot(k_ref[pl.ds(spot, size), :], q_cols, preferred_element_type=jnp.float32)
            if masked:
                s = jnp.where(_score_mask(c, size, block, count, wide, causal), s, NEGATIVE)
            e = jnp.exp(s - top)
            through = jnp.dot(v_ref[pl.ds(spot, size), :], dn_cols, preferred_element_type=jnp.float32)
            ds = (e * (through + dtotal)).astype(jnp.bfloat16)
            dv_ref[pl.ds(spot, size), :] = dv_ref[pl.ds(spot, size), :] + jnp.dot(
                e.astype(jnp.bfloat16), dn_rows, preferred_element_type=jnp.float32
            )
            dk_ref[pl.ds(spot, size), :] = dk_ref[pl.ds(spot, size), :] + jnp.dot(
                ds, q_rows, preferred_element_type=jnp.float32
            )
            return dq + jnp.dot(kt_ref[:, pl.ds(spot, size)], ds, preferred_element_type=jnp.float32)

        dq = jnp.zeros((lanes, wide), jnp.float32)
        dq = lax.fori_loop(0, full, functools.partial(one, False), dq)
        dq = lax.fori_loop(full, chunks, functools.partial(one, True), dq)
        back = jnp.transpose(jnp.where(mine, dq, 0.0))

        @pl.when(jnp.logical_not(second))
        def _():
            dq_ref[pl.ds(at, wide), :] = back

        @pl.when(second)
        def _():
            dq_ref[pl.ds(at, wide), :] = dq_ref[pl.ds(at, wide), :] + back

        return carry

    lax.fori_loop(0, total_steps, step, 0)
    shift = lanes if packed else 0
    if packed:
        out_ref[:, 0:lanes] = dq_ref[...].astype(jnp.bfloat16)
    else:
        dqo_ref[...] = dq_ref[...].astype(jnp.bfloat16)

    def emit(c, carry):
        at = pl.multiple_of(c * size, size)
        out_ref[pl.ds(at, size), shift : shift + lanes] = dk_ref[pl.ds(at, size), :].astype(jnp.bfloat16)
        out_ref[pl.ds(at, size), shift + lanes : shift + 2 * lanes] = dv_ref[pl.ds(at, size), :].astype(
            jnp.bfloat16
        )
        return carry

    lax.fori_loop(0, slots // size, emit, 0)


def attention(info, parts, causal):
    lanes = 2 * HEAD_DIM
    rows = parts[0].shape[0]
    slots = parts[-1].shape[0]
    wide = min(256, rows // 2)
    size = min(256 if causal else 512, slots)
    work = rows * slots * lanes * (2 if causal else 4)
    return pl.pallas_call(
        functools.partial(attend_kernel, wide, size, causal, len(parts) == 1),
        name="attend_self" if causal else "attend_cross",
        out_shape=(
            jax.ShapeDtypeStruct((rows, lanes), jnp.bfloat16),
            jax.ShapeDtypeStruct((lanes, rows), jnp.float32),
            jax.ShapeDtypeStruct((8, rows), jnp.float32),
        ),
        in_specs=[pl.BlockSpec(memory_space=pltpu.SMEM)]
        + [pl.BlockSpec(memory_space=pltpu.VMEM)] * len(parts),
        out_specs=(pl.BlockSpec(memory_space=pltpu.VMEM),) * 3,
        scratch_shapes=[
            pltpu.VMEM((lanes, slots), jnp.bfloat16),
            pltpu.VMEM((slots, wide), jnp.float32),
        ],
        compiler_params=pltpu.CompilerParams(vmem_limit_bytes=32 * 1024 * 1024),
        cost_estimate=pl.CostEstimate(flops=work, bytes_accessed=slots * lanes * 8, transcendentals=rows * slots),
    )(info, *parts)


def attention_back(info, parts, dmix, mixed, stats, causal):
    lanes = 2 * HEAD_DIM
    rows = parts[0].shape[0]
    slots = parts[-1].shape[0]
    wide = min(256, rows // 2)
    size = min(256 if causal else 512, slots)
    work = rows * slots * lanes * (5 if causal else 10)
    packed = len(parts) == 1
    outs = (jax.ShapeDtypeStruct((slots, (3 if packed else 2) * lanes), jnp.bfloat16),)
    if not packed:
        outs = (jax.ShapeDtypeStruct((rows, lanes), jnp.bfloat16),) + outs
    return pl.pallas_call(
        functools.partial(attend_back_kernel, wide, size, causal, packed),
        name="attend_self_back" if causal else "attend_cross_back",
        out_shape=outs,
        in_specs=[pl.BlockSpec(memory_space=pltpu.SMEM)]
        + [pl.BlockSpec(memory_space=pltpu.VMEM)] * (len(parts) + 3),
        out_specs=(pl.BlockSpec(memory_space=pltpu.VMEM),) * len(outs),
        scratch_shapes=[
            pltpu.VMEM((lanes, slots), jnp.bfloat16),
            pltpu.VMEM((slots, lanes), jnp.float32),
            pltpu.VMEM((slots, lanes), jnp.float32),
            pltpu.VMEM((rows, lanes), jnp.float32),
        ],
        compiler_params=pltpu.CompilerParams(vmem_limit_bytes=40 * 1024 * 1024),
        cost_estimate=pl.CostEstimate(flops=work, bytes_accessed=slots * lanes * 8, transcendentals=rows * slots),
    )(info, *parts, dmix, mixed, stats)


def project_units_kernel(where_ref, rows_ref, weight_ref, out_ref):
    out_ref[0, 0] = jnp.dot(
        rows_ref[0], weight_ref[0], preferred_element_type=jnp.float32
    ).astype(jnp.bfloat16)


def project_units(rows, weight, x_rank, z_rank):
    docs, count, width = rows.shape
    units, _, lanes = weight.shape
    where = jnp.stack([x_rank, z_rank]).astype(jnp.int32)
    return pl.pallas_call(
        project_units_kernel,
        name="project_units",
        out_shape=jax.ShapeDtypeStruct((docs, units, count, lanes), jnp.bfloat16),
        grid_spec=pltpu.PrefetchScalarGridSpec(
            num_scalar_prefetch=1,
            grid=(docs, units),
            in_specs=[
                pl.BlockSpec((1, count, width), lambda h, k, at: ((at[0] + h) % docs, 0, 0)),
                pl.BlockSpec((1, width, lanes), lambda h, k, at: ((at[1] + k) % units, 0, 0)),
            ],
            out_specs=pl.BlockSpec((1, 1, count, lanes), lambda h, k, at: (h, k, 0, 0)),
        ),
        compiler_params=pltpu.CompilerParams(vmem_limit_bytes=24 * 1024 * 1024),
        cost_estimate=pl.CostEstimate(
            flops=2 * docs * count * width * units * lanes,
            bytes_accessed=2 * (docs * count * width + units * width * lanes + docs * units * count * lanes),
            transcendentals=0,
        ),
    )(where, rows, weight)


def take(array, index, axis=0):
    return lax.dynamic_index_in_dim(array, index, axis, False)


def put(array, piece, index):
    return lax.dynamic_update_index_in_dim(array, piece, index, 0)


def twins(first, own, other):
    return jnp.where(first, jnp.stack([own, other]), jnp.stack([other, own]))


def by_heads(
    dec_in,
    enc_in,
    tgt_len,
    enc_len,
    self_qkv,
    self_out,
    cross_q,
    cross_kv,
    cross_out,
    ff_in,
    ff_out,
    gains,
    cotangent,
):
    f32, bf16 = jnp.float32, jnp.bfloat16
    tie = lax.optimization_barrier
    docs_here, rows_doc, width = dec_in.shape
    slots_doc = enc_in.shape[1]
    doc_ranks, seq_ranks = lax.axis_size("doc"), lax.axis_size("seq")
    seq_rank, doc_rank = lax.axis_index("seq"), lax.axis_index("doc")
    z_rank, x_rank = seq_rank // 2, seq_rank % 2
    units = seq_ranks // 2
    column_pairs = [(i, i ^ 1) for i in range(seq_ranks)]
    shifts = [[(i, (i + 2 * k) % seq_ranks) for i in range(seq_ranks)] for k in range(units)]
    lanes = 2 * HEAD_DIM
    share = HEADS * HEAD_DIM // doc_ranks
    rest = share - HEAD_DIM
    depth = width // seq_ranks
    rows = docs_here * rows_doc
    slots = docs_here * slots_doc
    hidden_here = ff_in.shape[2]
    even = doc_rank % 2 == 0
    first = x_rank == 0

    def swap_x(array):
        return lax.ppermute(array, "seq", column_pairs)

    def swap_y(array):
        return lax.ppermute(array, "doc", [(i, i ^ 2) for i in range(doc_ranks)])

    def swap_core(array):
        return lax.ppermute(array, "doc", [(i, i ^ 1) for i in range(doc_ranks)])

    def shift_z(array, k):
        return lax.ppermute(array, "seq", shifts[k % units])

    def by_document(array):
        pair = twins(first, take(array, x_rank), swap_x(take(array, 1 - x_rank)))
        return pair.reshape((-1,) + pair.shape[2:])

    def by_position(array):
        pair = array.reshape((2, array.shape[0] // 2) + array.shape[1:])
        return twins(first, take(pair, x_rank), swap_x(take(pair, 1 - x_rank)))

    def gather_z(array):
        out = jnp.broadcast_to(array, (units,) + array.shape)
        for k in range(1, units):
            out = put(out, shift_z(array, k), (z_rank - k) % units)
        return out

    def send_units(array):
        return [take(array, z_rank)] + [
            shift_z(take(array, (z_rank + k) % units), k) for k in range(1, units)
        ]

    def to_unit(array):
        out = array
        for k, arrived in enumerate(send_units(array)):
            out = put(out, arrived, (z_rank - k) % units)
        return out.reshape((-1,) + out.shape[2:])

    def collect(pieces):
        out = jnp.broadcast_to(pieces[0], (units,) + pieces[0].shape)
        for k in range(1, units):
            out = put(out, shift_z(pieces[k], k), (z_rank - k) % units)
        return out

    def to_rows(array):
        array = array.reshape((units, -1) + array.shape[1:])
        out = array
        for k in range(units):
            piece = take(array, (z_rank + k) % units)
            piece = shift_z(piece, k) if k else piece
            out = put(out, piece, (z_rank - k) % units)
        return out

    def return_units(pieces):
        out = jnp.zeros((units,) + pieces[0].shape, pieces[0].dtype)
        for k, piece in enumerate(pieces):
            arrived = shift_z(piece, units - k) if k else piece
            out = put(out, arrived, (z_rank + k) % units)
        return out

    def gather_doc(array):
        across, beside = swap_y(array), swap_core(array)
        return jnp.concatenate([array, beside], axis=0), jnp.concatenate([across, swap_core(across)], axis=0)

    def add_core(array):
        n = array.shape[0] // 2
        return array[:n] + swap_core(array[n:].astype(bf16)).astype(f32)

    def add_x(array):
        arrived = swap_x(take(array, 1 - x_rank, 1))
        return (take(array, x_rank, 1).astype(f32) + arrived.astype(f32)).astype(bf16)

    def add_z(array):
        total = take(array, z_rank).astype(f32)
        for k in range(1, units):
            total = total + shift_z(take(array, (z_rank + k) % units), k).astype(f32)
        return total

    def whole_first(block):
        return jnp.where(even, block, jnp.concatenate([block[:, rest:], block[:, :rest]], axis=1))

    def whole_back(block):
        return jnp.where(even, block, jnp.concatenate([block[:, HEAD_DIM:], block[:, :HEAD_DIM]], axis=1))

    def spread(out, parts):
        pieces = []
        for j in range(doc_ranks):
            line = []
            for i in range(parts):
                line.append(out[j, :, i * share : (i + 1) * share])
                line.append(out[j ^ 1, :, i * share + HEAD_DIM : (i + 1) * share])
            pieces.append(jnp.concatenate(line, axis=1))
        return jnp.stack(pieces)

    def merge(array, parts):
        wide_in = array.astype(f32)
        pieces = []
        for j in range(doc_ranks):
            line = []
            for i in range(parts):
                at = i * lanes
                line.append(wide_in[j, :, at : at + HEAD_DIM])
                line.append(
                    wide_in[j, :, at + HEAD_DIM : at + share] + wide_in[j ^ 1, :, at + share : at + lanes]
                )
            pieces.append(jnp.concatenate(line, axis=1))
        return jnp.stack(pieces).astype(bf16)

    def spread_weight(block, parts):
        return spread(block, parts)

    def project_wide(rows_in, weight):
        return jnp.einsum("td,jdk->jtk", rows_in, weight, preferred_element_type=f32).astype(bf16)

    def project(rows_in, weight, parts):
        return spread(project_wide(rows_in, weight), parts)

    def lift(inner_in, weight):
        return jnp.einsum("jtk,jdk->td", inner_in, weight, preferred_element_type=f32)

    def fold(terms, parts):
        terms = terms.reshape(doc_ranks, parts, lanes, width)
        other = jnp.stack([terms[j ^ 1, :, share:] for j in range(doc_ranks)]).astype(f32)
        split = (terms[:, :, HEAD_DIM:share].astype(f32) + other).astype(bf16)
        return jnp.concatenate([terms[:, :, :HEAD_DIM], split], axis=2).reshape(doc_ranks, parts * share, width)

    def outer(inner_in, rows_in):
        return jnp.einsum("jtk,td->jkd", inner_in, rows_in, preferred_element_type=f32).astype(bf16)

    part = z_rank % 2
    info_self = jnp.stack([take(tgt_len, x_rank), part])
    info_cross = jnp.stack([take(enc_len, x_rank), part])

    small = jnp.concatenate(
        [
            whole_first(b)
            for b in (
                self_qkv[0],
                self_qkv[1],
                self_qkv[2],
                cross_q,
                cross_kv[0],
                cross_kv[1],
                self_out.T,
                cross_out.T,
            )
        ],
        axis=1,
    )
    every = lax.all_gather(small, ("doc", "seq"), axis=0, tiled=True)
    ff_mine = jnp.concatenate([ff_in[0], ff_in[1], ff_out.T], axis=1)
    ff_all = lax.all_gather(ff_mine, "seq", axis=0, tiled=True)
    gain_pair = twins(first, gains, swap_x(gains))
    gain_all = gather_z(gain_pair).transpose(2, 0, 1, 3).reshape(3, width).astype(f32)
    stream = by_document(dec_in).astype(f32)
    normed1, inverse1 = norm_parts(stream, gain_all[0])
    normed1 = normed1.astype(bf16)
    cot = by_document(cotangent)
    cot_near, cot_far = gather_doc(cot)
    n1_near, n1_far = gather_doc(normed1)
    every, normed1, cot_near, cot_far, n1_near, n1_far = tie(
        (every, normed1, cot_near, cot_far, n1_near, n1_far)
    )
    every = every.reshape(doc_ranks, width, 8 * share)
    w_qkv = every[:, :, : 3 * share]
    w_cq = every[:, :, 3 * share : 4 * share]
    w_ckv = every[:, :, 4 * share : 6 * share]
    w_so = every[:, :, 6 * share : 7 * share]
    w_co = every[:, :, 7 * share :]

    qkv_rows = project(normed1, w_qkv, 3)
    qkv_rows, w_ckv = tie((qkv_rows, w_ckv))
    qkv_heads = to_unit(qkv_rows)
    enc_rows = enc_in.reshape(slots, width)
    w_kv = spread_weight(w_ckv, 2)
    ckv = project_units(enc_in, w_kv, x_rank, z_rank)
    ckv_other = swap_x(ckv[1])
    ckv_own = collect([ckv[0, k] for k in range(units)])
    qkv_heads, ckv = tie((qkv_heads, ckv))
    att1, mix1, stat1 = attention(info_self, (qkv_heads,), True)
    att1, ckv_own = tie((att1, ckv_own))
    att1 = to_rows(att1)
    att1, ckv_other = tie((att1, ckv_other))
    ckv_other = collect([ckv_other[k] for k in range(units)])
    att1 = merge(att1, 1)
    stream1 = stream + lift(att1, w_so)
    normed2, inverse2 = norm_parts(stream1, gain_all[1])
    normed2 = normed2.astype(bf16)
    cq_heads = to_unit(project(normed2, w_cq, 1))
    halves = (ckv_own, ckv_other)
    ckv_heads = jnp.where(first, jnp.stack(halves, axis=1), jnp.stack(halves[::-1], axis=1))
    ckv_heads = ckv_heads.reshape(units * slots, 2 * lanes)
    att2, mix2, stat2 = attention(info_cross, (cq_heads, ckv_heads), False)
    att2 = merge(to_rows(att2), 1)
    stream2 = stream1 + lift(att2, w_co)
    normed3, inverse3 = norm_parts(stream2, gain_all[2])
    normed3 = normed3.astype(bf16)

    w_gate, w_up = ff_all[:, :hidden_here], ff_all[:, hidden_here : 2 * hidden_here]
    w_down = ff_all[:, 2 * hidden_here :]

    def inside(n3_rows, cot_rows):
        gate_pre = matmul_rows(n3_rows, w_gate)
        up_pre = matmul_rows(n3_rows, w_up)
        d_hidden = matmul_rows(cot_rows, w_down)
        hidden, gelu_pull = jax.vjp(
            lambda gate_val, up_val: jax.nn.gelu(gate_val, approximate=True) * up_val, gate_pre, up_pre
        )
        d_gate, d_up = gelu_pull(d_hidden)
        return hidden.astype(bf16), d_gate.astype(bf16), d_up.astype(bf16)

    def through(d_gate, d_up):
        return matmul_back(d_gate, w_gate) + matmul_back(d_up, w_up)

    n3_near, n3_far = gather_doc(normed3)
    hid_near, dg_near, du_near = inside(n3_near, cot_near)
    hid_near, n3_far = tie((hid_near, n3_far))
    hid_far, dg_far, du_far = inside(n3_far, cot_far)
    dn3_across = swap_y(add_core(through(dg_far, du_far)).astype(bf16))
    dn3_near = add_core(through(dg_near, du_near))
    n3_all = jnp.concatenate([n3_near, n3_far], axis=0)
    cot_all = jnp.concatenate([cot_near, cot_far], axis=0)
    d_gate = jnp.concatenate([dg_near, dg_far], axis=0)
    d_up = jnp.concatenate([du_near, du_far], axis=0)
    hidden = jnp.concatenate([hid_near, hid_far], axis=0)
    ff_grads = jnp.concatenate(
        [
            matmul_outer(n3_all, d_gate).astype(bf16),
            matmul_outer(n3_all, d_up).astype(bf16),
            matmul_outer(cot_all, hidden).astype(bf16),
        ],
        axis=1,
    )
    ff_sum = lax.psum_scatter(ff_grads, "seq", scatter_dimension=0, tiled=True)
    dn3_across, ff_grads = tie((dn3_across, ff_grads))
    d_normed3 = dn3_near + dn3_across.astype(f32)

    back_three, gain_grad3 = norm_back(stream2, inverse3, gain_all[2], d_normed3)
    d_stream2 = cot.astype(f32) + back_three
    d_branch2 = d_stream2.astype(bf16)
    d_mix2 = to_unit(project(d_branch2, w_co, 1))
    d_mix2, hidden_late = tie((d_mix2, hidden))
    branch_across = swap_y(add_core(matmul_back(hidden_late[2 * rows :], w_down)).astype(bf16))
    branch = add_core(matmul_back(hidden_late[: 2 * rows], w_down))
    d_cq, d_ckv = attention_back(info_cross, (cq_heads, ckv_heads), d_mix2, mix2, stat2, False)
    d_ckv = d_ckv.reshape(units, 2, slots_doc, 2 * lanes)
    d_cq = to_rows(d_cq)
    d_cq, d_ckv, branch_across = tie((d_cq, d_ckv, branch_across))
    d_ckv_other = to_rows(take(d_ckv, 1 - x_rank, 1).reshape(-1, 2 * lanes))
    d_cq = merge(d_cq, 1)
    back_two, gain_grad2 = norm_back(stream1, inverse2, gain_all[1], lift(d_cq, w_cq))
    d_stream1 = d_stream2 + back_two
    d_branch1 = d_stream1.astype(bf16)
    d_branch1, d_ckv = tie((d_branch1, d_ckv))
    d_mix1 = to_unit(project(d_branch1, w_so, 1))
    d_ckv_own = to_rows(take(d_ckv, x_rank, 1).reshape(-1, 2 * lanes))
    d_mix1, d_ckv_other = tie((d_mix1, d_ckv_other))
    d_ckv_other = swap_x(d_ckv_other)
    (d_qkv,) = attention_back(info_self, (qkv_heads,), d_mix1, mix1, stat1, True)
    d_qkv, d_ckv_own, d_ckv_other, d_stream1, branch = tie((d_qkv, d_ckv_own, d_ckv_other, d_stream1, branch))
    d_qkv = to_rows(d_qkv)
    d_ckv = jnp.where(first, jnp.stack([d_ckv_own, d_ckv_other], axis=1), jnp.stack([d_ckv_other, d_ckv_own], axis=1))
    d_ckv = d_ckv.reshape(units, slots, 2 * lanes)
    enc_grad = lift(d_ckv, w_kv).reshape(docs_here, slots_doc, width)
    layer_out = by_position(stream2 + (branch + branch_across.astype(f32)))
    d_qkv, enc_grad, layer_out = tie((d_qkv, enc_grad, layer_out))
    d_qkv = merge(d_qkv, 3)

    def beside(array, k):
        return take(array, doc_rank ^ k)

    arrived = swap_core(jnp.stack([beside(d_qkv, 1), beside(d_qkv, 3)]))
    d_near = jnp.concatenate([beside(d_qkv, 0), arrived[0]], axis=0)
    d_far = swap_y(jnp.concatenate([beside(d_qkv, 2), arrived[1]], axis=0))
    back_one, gain_grad1 = norm_back(stream, inverse1, gain_all[0], lift(d_qkv, w_qkv))
    dec_grad = by_position(d_stream1 + back_one)

    terms = jnp.concatenate(
        [
            outer(d_cq, normed2),
            fold(outer(d_ckv, enc_rows), 2),
            outer(att1, d_branch1),
            outer(att2, d_branch2),
        ],
        axis=1,
    )
    arrived = swap_core(jnp.stack([beside(terms, 1), beside(terms, 3)])).astype(f32)
    across = swap_y((beside(terms, 2).astype(f32) + arrived[1]).astype(bf16))
    terms = (beside(terms, 0).astype(f32) + arrived[0]) + across.astype(f32)
    terms = terms.astype(bf16).T.reshape(units, 2, depth, 5 * share)
    others = add_z(add_x(terms))

    gain_terms = jnp.stack([gain_grad1, gain_grad2, gain_grad3])
    gain_terms = gain_terms + swap_core(gain_terms)
    gain_terms = gain_terms + swap_y(gain_terms)
    gain_terms = gain_terms.reshape(3, seq_ranks, depth).transpose(1, 0, 2)
    gain_terms = gain_terms.reshape(seq_ranks, 2, 3 * depth // 2).astype(bf16)
    gain_terms = jnp.pad(gain_terms, ((0, 0), (0, 6), (0, 3 * share - 3 * depth // 2)))
    grad_qkv = matmul_outer(n1_near, d_near) + matmul_outer(n1_far, d_far)
    grad_qkv = grad_qkv.astype(bf16).reshape(seq_ranks, depth, 3 * share)
    grad_qkv = jnp.concatenate([grad_qkv, gain_terms], axis=1)
    grad_qkv = grad_qkv.reshape(units, 2, depth + 8, 3 * share)
    summed = add_z(add_x(grad_qkv))
    grad_gains = summed[depth : depth + 2, : 3 * depth // 2].reshape(3, depth)
    piece = lambda a, i: whole_back(a[:depth, i * share : (i + 1) * share])
    ff_sum = ff_sum.astype(f32)
    return (
        layer_out,
        dec_grad,
        enc_grad,
        jnp.stack([piece(summed, 0), piece(summed, 1), piece(summed, 2)]),
        piece(others, 3).T,
        piece(others, 0),
        jnp.stack([piece(others, 1), piece(others, 2)]),
        piece(others, 4).T,
        jnp.stack([ff_sum[:, :hidden_here], ff_sum[:, hidden_here : 2 * hidden_here]]),
        ff_sum[:, 2 * hidden_here :].T,
        grad_gains,
    )


def fits_by_heads(doc_ranks, seq_ranks, docs):
    return doc_ranks == 4 and seq_ranks == 8 and docs == 8


def solution(mesh):
    def either(dec_in, *others):
        docs = dec_in.shape[0] * mesh.shape["doc"]
        if fits_by_heads(mesh.shape["doc"], mesh.shape["seq"], docs):
            return by_heads(dec_in, *others)
        return per_device(dec_in, *others)

    return jax.shard_map(
        either,
        mesh=mesh,
        in_specs=(
            P("doc", "seq", None),
            P("doc", "seq", None),
            P("doc"),
            P("doc"),
            P(None, "seq", "doc"),
            P("doc", "seq"),
            P("seq", "doc"),
            P(None, "seq", "doc"),
            P("doc", "seq"),
            P(None, "seq", "doc"),
            P("doc", "seq"),
            P(None, "seq"),
            P("doc", "seq", None),
        ),
        out_specs=(
            P("doc", "seq", None),
            P("doc", "seq", None),
            P("doc", "seq", None),
            P(None, "seq", "doc"),
            P("doc", "seq"),
            P("seq", "doc"),
            P(None, "seq", "doc"),
            P("doc", "seq"),
            P(None, "seq", "doc"),
            P("doc", "seq"),
            P(None, "seq"),
        ),
        check_vma=False,
    )
```
